32 devices in a mesh: fsdp: 4 (over y, core), ctx: 2 (over x), tp: 4 (over z).
Axes of the slice: x: 2, y: 2, z: 4, core: 2. Of those that a mesh axis runs over, the one named last changes fastest.
Arguments:
- tokens: bfloat16 [2, 4, 1024, 768], P(None, 'fsdp', 'ctx'), may hold values from -6 to 6
- segments: int32 [2, 4, 1024], P(None, 'fsdp'), may hold values from 0 to 3, never falling along the last dimension, each value on 1 to 640 neighbouring positions
- cotangent: bfloat16 [2, 4, 1024, 768], P(None, 'fsdp', 'ctx'), may hold values from -6 to 6
- query_weight: bfloat16 [768, 768], P(('fsdp', 'ctx'), 'tp'), may hold values from -0.21875 to 0.21875
- key_weight: bfloat16 [768, 768], P(('fsdp', 'ctx'), 'tp'), may hold values from -0.21875 to 0.21875
- value_weight: bfloat16 [768, 768], P(('fsdp', 'ctx'), 'tp'), may hold values from -0.21875 to 0.21875
- out_weight: bfloat16 [768, 768], P(('fsdp', 'ctx'), 'tp'), may hold values from -0.875 to 0.875
- gate_weight: bfloat16 [768, 2048], P(('fsdp', 'ctx'), 'tp'), may hold values from -0.21875 to 0.21875
- up_weight: bfloat16 [768, 2048], P(('fsdp', 'ctx'), 'tp'), may hold values from -0.21875 to 0.21875
- down_weight: bfloat16 [768, 2048], P(('fsdp', 'ctx'), 'tp'), may hold values from -0.125 to 0.125
- attn_gain: bfloat16 [768], P(('fsdp', 'ctx')), may hold values from 0.5 to 1.5
- ffn_gain: bfloat16 [768], P(('fsdp', 'ctx')), may hold values from 0.5 to 1.5
Outputs:
- output: bfloat16 [2, 4, 1024, 768], P(None, 'fsdp', 'ctx')
- input_grad: float32 [2, 4, 1024, 768], P(None, 'fsdp', 'ctx')
- query_grad: float32 [768, 768], P(('fsdp', 'ctx'), 'tp')
- key_grad: float32 [768, 768], P(('fsdp', 'ctx'), 'tp')
- value_grad: float32 [768, 768], P(('fsdp', 'ctx'), 'tp')
- out_grad: float32 [768, 768], P(('fsdp', 'ctx'), 'tp')
- gate_grad: float32 [768, 2048], P(('fsdp', 'ctx'), 'tp')
- up_grad: float32 [768, 2048], P(('fsdp', 'ctx'), 'tp')
- down_grad: float32 [768, 2048], P(('fsdp', 'ctx'), 'tp')
- attn_gain_grad: float32 [768], P(('fsdp', 'ctx'))
- ffn_gain_grad: float32 [768], P(('fsdp', 'ctx'))
The draws below stay inside these ranges and needn't reach their ends.
Inputs may be any that keep to these rules, and one draw needn't show every extreme that they name: `segments`: within each sequence the numbers never fall; each covers 1 to 640 positions, one exactly that many.
All inputs are finite; a program needn't handle non-finite values.
Results may differ from the reference program's by a relative error of at most 0.014.
Values may be sent and summed in bfloat16 or wider, within the bound.
A program may use at most 320 MiB of HBM per device.

```python
import math
import jax
import jax.numpy as jnp
import numpy as np
from jax import lax

D = 768
HEADS = 12
HEAD_DIM = 64
FF = 2048
MICRO = 2
SEQ_LEN = 1024
BATCH = 4


def block_levels(key, dims, split, least, high):
    def one(position, blocks):
        steps = jax.random.uniform(jax.random.fold_in(jax.random.fold_in(key, 6), position), (blocks,), jnp.float32, least / len(split), high / len(split))
        return jnp.repeat(jnp.exp(steps), dims[position] // blocks).reshape((-1,) + (1,) * (len(dims) - position - 1))

    level = one(*split[0])
    for cut in split[1:]:
        level = level * one(*cut)
    return level


def profile(count, total, reach, slope):
    loads = [(1 << 20) // math.isqrt(grade ** slope) + 1 for grade in range(2, count + 1)]
    spare, counts = total - reach - (count - 1), [1] * (count - 1)
    while spare > 0:
        free = [i for i in range(count - 1) if counts[i] < reach]
        whole, remaining = sum([loads[i] for i in free]), spare
        for i in free:
            extra = min(reach - counts[i], max(1, remaining * loads[i] // whole), spare)
            counts[i] = counts[i] + extra
            spare = spare - extra
    return np.array([reach] + counts)


def uneven(key, number_of, total, most, slope):
    if number_of == 2:
        one = jax.random.randint(key, (), max(1, total - most), min(most, total - 1) + 1)
        return jnp.stack([one, total - one])
    sizes = jnp.asarray(profile(number_of, total, most, slope), jnp.int32)
    pairs = (number_of - 1) // 2
    donor, taker = sizes[1:1 + 2 * pairs:2], sizes[2:2 + 2 * pairs:2]
    slack = jnp.minimum(donor - 1, most - taker)
    moved = jax.random.randint(jax.random.fold_in(key, 1), (pairs,), 0, 1 << 20) % (slack + 1)
    sizes = sizes.at[1:1 + 2 * pairs:2].set(donor - moved).at[2:2 + 2 * pairs:2].set(taker + moved)
    return sizes[jax.random.permutation(jax.random.fold_in(key, 2), number_of)]


def noise(own_key, shape, spread, reach, shards=(), kind=jnp.bfloat16):
    gain = block_levels(own_key, shape, shards, -0.22, 0.18) if shards else 1.0
    values = jax.random.normal(own_key, shape, jnp.float32) * spread * gain
    return jnp.minimum(jnp.maximum(values, -reach), reach).astype(kind)


def setup_inputs(seed: int = 0) -> dict:
    splits = jax.random.split(jax.random.key(seed), 13)
    return {
        "tokens": noise(splits[0], (MICRO, BATCH, SEQ_LEN, D), 1.0, 6.0, ((1, 4), (2, 2))),
        "segments": jax.vmap(lambda own: jnp.searchsorted(jnp.cumsum(uneven(own, 4, SEQ_LEN, 5 * SEQ_LEN // 8, 0)), jnp.arange(SEQ_LEN), side="right"))(jax.random.split(splits[1], MICRO * BATCH)).reshape((MICRO, BATCH, SEQ_LEN)).astype(jnp.int32),
        "cotangent": noise(splits[2], (MICRO, BATCH, SEQ_LEN, D), 1.0, 6.0, ((1, 4), (2, 2))),
        "query_weight": noise(splits[3], (D, D), D ** -0.5, 0.21875, ((0, 8), (1, 4))),
        "key_weight": noise(splits[4], (D, D), D ** -0.5, 0.21875, ((0, 8), (1, 4))),
        "value_weight": noise(splits[5], (D, D), D ** -0.5, 0.21875, ((0, 8), (1, 4))),
        "out_weight": noise(splits[6], (D, D), (D // 16) ** -0.5, 0.875, ((0, 8), (1, 4))),
        "gate_weight": noise(splits[7], (D, FF), D ** -0.5, 0.21875, ((0, 8), (1, 4))),
        "up_weight": noise(splits[8], (D, FF), D ** -0.5, 0.21875, ((0, 8), (1, 4))),
        "down_weight": noise(splits[9], (D, FF), FF ** -0.5, 0.125, ((0, 8), (1, 4))),
        "attn_gain": jnp.clip(1.0 + 0.1 * jax.random.normal(splits[10], (D,), jnp.float32), 0.5, 1.5).astype(jnp.bfloat16),
        "ffn_gain": jnp.clip(1.0 + 0.1 * jax.random.normal(splits[11], (D,), jnp.float32), 0.5, 1.5).astype(jnp.bfloat16),
    }


@jax.custom_vjp
def low(v):
    return lax.optimization_barrier(v.astype(jnp.bfloat16)).astype(jnp.float32)

@jax.custom_vjp
def low_back(v):
    return v

def low_keep(v):
    return (low(v), None)

def low_pass(kept, grad):
    return (grad,)

def back_keep(v):
    return (v, None)

def back_low(kept, grad):
    return (low(grad),)
low.defvjp(low_keep, low_pass)
low_back.defvjp(back_keep, back_low)
EPS = 1e-06
HIGH = lax.Precision.HIGHEST

def normalize(values, gain_vec):
    return values * lax.rsqrt(lax.optimization_barrier(jnp.mean(values * values, -1, keepdims=True)) + EPS) * gain_vec

def matmul(left_op, right_op):
    return jnp.dot(left_op, right_op, precision=HIGH)

def layer(inputs, seg_ids, params):
    w_query, w_key, w_value, w_out, w_gate, w_up, w_down, gain_attn, gain_ffn = params
    length = inputs.shape[0]
    normed_one = low(normalize(inputs, gain_attn))
    queries = low_back(low(matmul(normed_one, w_query))).reshape(length, HEADS, HEAD_DIM)
    key_heads = low_back(low(matmul(normed_one, w_key))).reshape(length, HEADS, HEAD_DIM)
    value_heads = low_back(low(matmul(normed_one, w_value))).reshape(length, HEADS, HEAD_DIM)
    scores = jnp.einsum('qhd,khd->hqk', queries, key_heads, precision=HIGH) * HEAD_DIM ** (-0.5)
    same_doc = seg_ids[:, None] == seg_ids[None, :]
    scores = low_back(jnp.where(same_doc[None], scores, -1e+30))
    weights = low(jax.nn.softmax(scores, axis=-1))
    attn_mixed = jnp.einsum('hqk,khd->qhd', weights, value_heads, precision=HIGH).reshape(length, D)
    attn_mixed = low_back(low(attn_mixed))
    attn_sum = low_back(matmul(attn_mixed, w_out.T))
    residual = inputs + attn_sum
    normed_two = low(normalize(residual, gain_ffn))
    gate_act = low_back(matmul(normed_two, w_gate))
    up_act = low_back(matmul(normed_two, w_up))
    hidden = low(jax.nn.gelu(gate_act, approximate=True) * up_act)
    ffn_sum = low_back(matmul(hidden, w_down.T))
    return residual + ffn_sum

def reference(tokens, segments, cotangent, query_weight, key_weight, value_weight, out_weight, gate_weight, up_weight, down_weight, attn_gain, ffn_gain):
    params = tuple((weight.astype(jnp.float32) for weight in (query_weight, key_weight, value_weight, out_weight, gate_weight, up_weight, down_weight, attn_gain, ffn_gain)))
    inputs = tokens.astype(jnp.float32).reshape(MICRO * BATCH, SEQ_LEN, D)
    seg_flat = segments.reshape(MICRO * BATCH, SEQ_LEN)

    def forward(inputs_all, params_all):

        def one_seq(pair):
            return layer(pair[0], pair[1], params_all)
        return lax.map(jax.checkpoint(one_seq), (inputs_all, seg_flat))
    result, pullback = jax.vjp(forward, inputs, params)
    input_grad, param_grads = pullback(cotangent.astype(jnp.float32).reshape(MICRO * BATCH, SEQ_LEN, D))
    return (result.reshape(tokens.shape).astype(jnp.bfloat16), input_grad.reshape(tokens.shape), param_grads[0], param_grads[1], param_grads[2], param_grads[3], param_grads[4], param_grads[5], param_grads[6], param_grads[7], param_grads[8])
```

```python
import functools

import jax
import jax.numpy as jnp
from jax import lax
from jax.experimental import pallas as pl
from jax.experimental.pallas import tpu as pltpu
from jax.sharding import PartitionSpec as P

HEAD_DIM = 64


EPS = 1e-06


def gather_weights(
    query_weight,
    key_weight,
    value_weight,
    out_weight,
    gate_weight,
    up_weight,
    down_weight,
    attn_gain,
    ffn_gain,
):
    return (
        lax.all_gather(query_weight, ("fsdp", "ctx"), axis=0, tiled=True),
        lax.all_gather(key_weight, ("fsdp", "ctx"), axis=0, tiled=True),
        lax.all_gather(value_weight, ("fsdp", "ctx"), axis=0, tiled=True),
        lax.all_gather(out_weight, ("fsdp", "ctx"), axis=0, tiled=True),
        lax.all_gather(gate_weight, ("fsdp", "ctx"), axis=0, tiled=True),
        lax.all_gather(up_weight, ("fsdp", "ctx"), axis=0, tiled=True),
        lax.all_gather(down_weight, ("fsdp", "ctx"), axis=0, tiled=True),
        lax.all_gather(attn_gain, ("fsdp", "ctx"), axis=0, tiled=True),
        lax.all_gather(ffn_gain, ("fsdp", "ctx"), axis=0, tiled=True),
    )


def tensor_sum(partial_value):
    return lax.psum(partial_value, "tp")


def normalize(values, gain_vec):
    return values * lax.rsqrt(jnp.mean(values * values, -1, keepdims=True) + EPS) * gain_vec


def gelu_mix(gate_act, up_act):
    return jax.nn.gelu(gate_act, approximate=True) * up_act


def contract_last(left_op, right_op):
    return lax.dot_general(
        left_op, right_op, (((1,), (1,)), ((), ())), preferred_element_type=jnp.float32
    )


def contract_first(left_op, right_op):
    return lax.dot_general(
        left_op, right_op, (((0,), (0,)), ((), ())), preferred_element_type=jnp.float32
    )


def masked_scores(queries, key_whole, query_seg, seg_all, head_count):
    local_rows = queries.shape[0]
    query_heads = queries.reshape(local_rows, head_count, HEAD_DIM)
    key_heads = key_whole.reshape(key_whole.shape[0], head_count, HEAD_DIM)
    products = jnp.einsum(
        "qhd,khd->hqk", query_heads, key_heads, preferred_element_type=jnp.float32
    ) * HEAD_DIM ** (-0.5)
    same_doc = query_seg[:, None] == seg_all[None, :]
    return jnp.where(same_doc[None], products, -1e30)


def forward_pass(inputs, seg_all, gathered, ctx_pos):
    w_query, w_key, w_value, w_out, w_gate, w_up, w_down, gain_attn, gain_ffn = gathered
    head_count = w_query.shape[1] // HEAD_DIM
    local_rows = inputs.shape[0]
    query_seg = lax.dynamic_slice_in_dim(seg_all, ctx_pos * local_rows, local_rows)
    inputs_f = inputs.astype(jnp.float32)
    normed_one = normalize(inputs_f, gain_attn.astype(jnp.float32)).astype(jnp.bfloat16)
    queries = jnp.dot(normed_one, w_query, preferred_element_type=jnp.float32).astype(jnp.bfloat16)
    key_local = jnp.dot(normed_one, w_key, preferred_element_type=jnp.float32).astype(jnp.bfloat16)
    value_local = jnp.dot(normed_one, w_value, preferred_element_type=jnp.float32).astype(
        jnp.bfloat16
    )
    key_whole, value_whole = (
        lax.all_gather(key_local, "ctx", axis=0, tiled=True),
        lax.all_gather(value_local, "ctx", axis=0, tiled=True),
    )
    scores = masked_scores(queries, key_whole, query_seg, seg_all, head_count)
    row_max = jnp.max(scores, -1, keepdims=True)
    row_total = jnp.sum(jnp.exp(scores - row_max), -1, keepdims=True)
    log_total = row_max + jnp.log(row_total)
    probs_low = jnp.exp(scores - log_total).astype(jnp.bfloat16)
    value_heads = value_whole.reshape(value_whole.shape[0], head_count, HEAD_DIM)
    attn_mixed = jnp.einsum(
        "hqk,khd->qhd", probs_low, value_heads, preferred_element_type=jnp.float32
    )
    attn_mixed = attn_mixed.reshape(local_rows, head_count * HEAD_DIM).astype(jnp.bfloat16)
    attn_partial = contract_last(attn_mixed, w_out)
    residual = inputs_f + tensor_sum(attn_partial)
    normed_two = normalize(residual, gain_ffn.astype(jnp.float32)).astype(jnp.bfloat16)
    gate_act = jnp.dot(normed_two, w_gate, preferred_element_type=jnp.float32)
    up_act = jnp.dot(normed_two, w_up, preferred_element_type=jnp.float32)
    hidden = gelu_mix(gate_act, up_act).astype(jnp.bfloat16)
    ffn_partial = contract_last(hidden, w_down)
    result = (residual + tensor_sum(ffn_partial)).astype(jnp.bfloat16)
    stored = (
        inputs_f,
        normed_one,
        queries,
        key_whole,
        value_whole,
        log_total,
        attn_mixed,
        residual,
        normed_two,
        gate_act,
        up_act,
        hidden,
        query_seg,
    )
    return (result, stored)


def backward_pass(cot_rows, stored, gathered, seg_all, ctx_pos):
    w_query, w_key, w_value, w_out, w_gate, w_up, w_down, gain_attn, gain_ffn = gathered
    (
        inputs_f,
        normed_one,
        queries,
        key_whole,
        value_whole,
        log_total,
        attn_mixed,
        residual,
        normed_two,
        gate_act,
        up_act,
        hidden,
        query_seg,
    ) = stored
    head_count = w_query.shape[1] // HEAD_DIM
    local_rows = queries.shape[0]
    seq_rows = key_whole.shape[0]
    scale = HEAD_DIM ** (-0.5)
    dout = cot_rows.astype(jnp.float32)
    dout_low = dout.astype(jnp.bfloat16)
    grad_down = contract_first(dout_low, hidden)
    dhidden = jnp.dot(dout_low, w_down, preferred_element_type=jnp.float32)
    mixed_unused, mix_back = jax.vjp(gelu_mix, gate_act, up_act)
    dgate, dup = mix_back(dhidden)
    dgate_low = dgate.astype(jnp.bfloat16)
    dup_low = dup.astype(jnp.bfloat16)
    grad_gate = contract_first(normed_two, dgate_low)
    grad_up = contract_first(normed_two, dup_low)
    dn2_partial = contract_last(dgate_low, w_gate) + contract_last(dup_low, w_up)
    norm_unused, norm_back = jax.vjp(normalize, residual, gain_ffn.astype(jnp.float32))
    dresid_norm, grad_gain_ffn = norm_back(tensor_sum(dn2_partial))
    dresidual = dout + dresid_norm
    dres_low = dresidual.astype(jnp.bfloat16)
    grad_out = contract_first(dres_low, attn_mixed)
    dmixed = jnp.dot(dres_low, w_out, preferred_element_type=jnp.float32).astype(jnp.bfloat16)
    dmixed_heads = dmixed.reshape(local_rows, head_count, HEAD_DIM)
    scores = masked_scores(queries, key_whole, query_seg, seg_all, head_count)
    prob_full = jnp.exp(scores - log_total)
    key_heads = key_whole.reshape(seq_rows, head_count, HEAD_DIM)
    value_heads = value_whole.reshape(seq_rows, head_count, HEAD_DIM)
    dprobs = jnp.einsum(
        "qhd,khd->hqk", dmixed_heads, value_heads, preferred_element_type=jnp.float32
    )
    row_delta = jnp.sum(prob_full * dprobs, -1, keepdims=True)
    dscores = (prob_full * (dprobs - row_delta)).astype(jnp.bfloat16)
    dquery = (
        jnp.einsum("hqk,khd->qhd", dscores, key_heads, preferred_element_type=jnp.float32) * scale
    )
    query_all, dmixed_all = (
        lax.all_gather(queries, "ctx", axis=0, tiled=True),
        lax.all_gather(dmixed, "ctx", axis=0, tiled=True),
    )
    log_all, delta_all = (
        lax.all_gather(log_total, "ctx", axis=1, tiled=True),
        lax.all_gather(row_delta, "ctx", axis=1, tiled=True),
    )
    start = ctx_pos * local_rows
    key_own = lax.dynamic_slice_in_dim(key_whole, start, local_rows)
    value_own = lax.dynamic_slice_in_dim(value_whole, start, local_rows).reshape(
        local_rows, head_count, HEAD_DIM
    )
    scores_own = masked_scores(query_all, key_own, seg_all, query_seg, head_count)
    prob_own = jnp.exp(scores_own - log_all)
    dmixed_all_heads = dmixed_all.reshape(seq_rows, head_count, HEAD_DIM)
    query_all_heads = query_all.reshape(seq_rows, head_count, HEAD_DIM)
    dprobs_own = jnp.einsum(
        "qhd,khd->hqk", dmixed_all_heads, value_own, preferred_element_type=jnp.float32
    )
    dscores_own = (prob_own * (dprobs_own - delta_all)).astype(jnp.bfloat16)
    dkey_local = (
        jnp.einsum("hqk,qhd->khd", dscores_own, query_all_heads, preferred_element_type=jnp.float32)
        * scale
    ).reshape(local_rows, head_count * HEAD_DIM)
    dvalue_local = jnp.einsum(
        "hqk,qhd->khd",
        prob_own.astype(jnp.bfloat16),
        dmixed_all_heads,
        preferred_element_type=jnp.float32,
    ).reshape(local_rows, head_count * HEAD_DIM)
    dquery_low = dquery.reshape(local_rows, head_count * HEAD_DIM).astype(jnp.bfloat16)
    dkey_low = dkey_local.astype(jnp.bfloat16)
    dvalue_low = dvalue_local.astype(jnp.bfloat16)
    grad_query = contract_first(normed_one, dquery_low)
    grad_key = contract_first(normed_one, dkey_low)
    grad_value = contract_first(normed_one, dvalue_low)
    dn1_partial = (
        contract_last(dquery_low, w_query)
        + contract_last(dkey_low, w_key)
        + contract_last(dvalue_low, w_value)
    )
    norm_unused_two, norm_back_two = jax.vjp(normalize, inputs_f, gain_attn.astype(jnp.float32))
    dinput_norm, grad_gain_attn = norm_back_two(tensor_sum(dn1_partial))
    input_grad = dresidual + dinput_norm
    grad_terms = (
        grad_query,
        grad_key,
        grad_value,
        grad_out,
        grad_gate,
        grad_up,
        grad_down,
        grad_gain_attn,
        grad_gain_ffn,
    )
    return (input_grad, grad_terms)


def shards(
    tokens,
    segments,
    cotangent,
    query_weight,
    key_weight,
    value_weight,
    out_weight,
    gate_weight,
    up_weight,
    down_weight,
    attn_gain,
    ffn_gain,
):
    ctx_pos = lax.axis_index("ctx")
    results = []
    input_grads = []
    total_grads = None
    for micro_step in range(tokens.shape[0]):
        seg_all = segments[micro_step, 0]
        gathered = gather_weights(
            query_weight,
            key_weight,
            value_weight,
            out_weight,
            gate_weight,
            up_weight,
            down_weight,
            attn_gain,
            ffn_gain,
        )
        result, stored = forward_pass(tokens[micro_step, 0], seg_all, gathered, ctx_pos)
        gathered = gather_weights(
            query_weight,
            key_weight,
            value_weight,
            out_weight,
            gate_weight,
            up_weight,
            down_weight,
            attn_gain,
            ffn_gain,
        )
        input_grad, grad_terms = backward_pass(
            cotangent[micro_step, 0], stored, gathered, seg_all, ctx_pos
        )
        results.append(result)
        input_grads.append(input_grad)
        total_grads = (
            grad_terms if total_grads is None else jax.tree.map(jnp.add, total_grads, grad_terms)
        )
    gain_attn_total = total_grads[7]
    gain_ffn_total = total_grads[8]
    owned = (
        lax.psum_scatter(total_grads[0], ("fsdp", "ctx"), scatter_dimension=0, tiled=True),
        lax.psum_scatter(total_grads[1], ("fsdp", "ctx"), scatter_dimension=0, tiled=True),
        lax.psum_scatter(total_grads[2], ("fsdp", "ctx"), scatter_dimension=0, tiled=True),
        lax.psum_scatter(total_grads[3], ("fsdp", "ctx"), scatter_dimension=0, tiled=True),
        lax.psum_scatter(total_grads[4], ("fsdp", "ctx"), scatter_dimension=0, tiled=True),
        lax.psum_scatter(total_grads[5], ("fsdp", "ctx"), scatter_dimension=0, tiled=True),
        lax.psum_scatter(total_grads[6], ("fsdp", "ctx"), scatter_dimension=0, tiled=True),
        lax.psum_scatter(gain_attn_total, ("fsdp", "ctx"), scatter_dimension=0, tiled=True),
        lax.psum_scatter(gain_ffn_total, ("fsdp", "ctx"), scatter_dimension=0, tiled=True),
    )
    output = jnp.stack(results)[:, None]
    input_grad_all = jnp.stack(input_grads)[:, None]
    return (
        output,
        input_grad_all,
        owned[0],
        owned[1],
        owned[2],
        owned[3],
        owned[4],
        owned[5],
        owned[6],
        owned[7],
        owned[8],
    )


NEG = -1e30
MESH = pl.DeviceIdType.MESH
BF = jnp.bfloat16
F32 = jnp.float32
GELU_K = 0.7978845608028654
GELU_A = 0.044715


def dot_nn(a, b):
    return lax.dot_general(a, b, (((1,), (0,)), ((), ())), preferred_element_type=F32)


def dot_nt(a, b):
    return lax.dot_general(a, b, (((1,), (1,)), ((), ())), preferred_element_type=F32)


def dot_tn(a, b):
    return lax.dot_general(a, b, (((0,), (0,)), ((), ())), preferred_element_type=F32)


def at(i, n):
    return pl.ds(pl.multiple_of(i, n), n)


def layer_kernel(dims, names, *refs):
    r = dict(zip(names, refs))
    R, D, H, FF, C, NF, NT, MICRO = dims
    L = C * R
    NH = H // HEAD_DIM
    HP = 256
    KV = 2 * H
    Y = NF // 2
    SR = D // (NF * C)
    RT = 256
    CH = 128
    NCH = R // CH
    f = lax.axis_index("fsdp")
    c = lax.axis_index("ctx")
    t = lax.axis_index("tp")
    core = lax.rem(f, 2)
    y = f // 2
    shard = f * C + c
    partner = {"fsdp": f + 1 - 2 * core}
    ssem, rsem = r["ssem"], r["rsem"]
    counter = [0]
    pending = []

    def slot():
        counter[0] += 1
        return counter[0] - 1

    def copy_to(src, dst, idx, dev):
        return pltpu.make_async_remote_copy(
            src_ref=src, dst_ref=dst, send_sem=ssem.at[idx], recv_sem=rsem.at[idx],
            device_id=dev, device_id_type=MESH)

    offsets = [(dy, dc) for dy in range(Y) for dc in range(C) if (dy, dc) != (0, 0)]

    def square(off):
        dy, dc = off
        return (2 * lax.rem(y + dy, Y) + core, lax.rem(c + dc, C))

    def square_from(off):
        dy, dc = off
        return (2 * lax.rem(y + Y - dy, Y) + core, lax.rem(c + C - dc, C))

    def dev_sq(off):
        pf, pc = square(off)
        return {"fsdp": pf, "ctx": pc}

    def z_to(k):
        return {"tp": lax.rem(t + k, NT)}

    group = [(df, dc) for df in range(NF) for dc in range(C) if (df, dc) != (0, 0)]

    def dev_group(off):
        return {"fsdp": lax.rem(f + off[0], NF), "ctx": lax.rem(c + off[1], C)}

    outer = (t == 0) | (t == NT - 1)
    inner = (t != 0) & (t != NT - 1)
    side = jnp.where(t == 0, 1, jnp.where(t == NT - 1, NT - 2, jnp.where(t == 1, 0, NT - 1)))
    mid = NT - 1 - t

    bar = pltpu.get_barrier_semaphore()
    for off in group:
        pl.semaphore_signal(bar, inc=1, device_id=dev_group(off), device_id_type=MESH)
    for k in range(1, NT):
        pl.semaphore_signal(bar, inc=1, device_id=z_to(k), device_id_type=MESH)
    pl.semaphore_wait(bar, len(group) + NT - 1)

    sends = []

    def send(src, dst, idx, dev):
        cp = copy_to(src, dst, idx, dev)
        cp.start()
        sends.append(cp)
        return cp

    gm = r["gmine"]
    cols = lax.broadcasted_iota(jnp.int32, (SR, D), 1)
    rows = lax.broadcasted_iota(jnp.int32, (SR, D), 0)
    place = (cols == rows + shard * SR).astype(BF)
    gm[...] = jnp.zeros_like(gm)
    gm[0:1, :] = dot_nn(r["gain_a"][...], place)
    gm[1:2, :] = dot_nn(r["gain_f"][...], place)
    gall = r["gall"]
    gain_cp = []
    for n, off in enumerate(group):
        gain_cp.append(send(gm, gall.at[n], slot(), dev_group(off)))

    def rows_of(off):
        pf, pc = square_from(off)
        return at((pf * C + pc) * SR, SR)

    own_rows = at(shard * SR, SR)

    class Spread:
        def __init__(self, buf, view):
            self.buf, self.view = buf, view
            self.ix = [slot() for _ in offsets]
            self.px = slot()
            self.rx = [slot() for _ in offsets]

        def start(self):
            v = self.view
            for i, off in zip(self.ix, offsets):
                send(v(self.buf, own_rows), v(self.buf, own_rows), i, dev_sq(off))
            send(v(self.buf, own_rows), v(self.buf, own_rows), self.px, partner)

        def relay(self):
            v = self.view
            for i, x, off in zip(self.ix, self.rx, offsets):
                w = v(self.buf, rows_of(off))
                copy_to(w, w, i, dev_sq(off)).wait_recv()
                send(w, w, x, partner)

        def finish(self):
            v = self.view
            w = v(self.buf, own_rows)
            copy_to(w, w, self.px, partner).wait_recv()
            for x in self.rx:
                copy_to(w, w, x, partner).wait_recv()

    flat = lambda buf, rows: buf.at[rows]
    deep = lambda buf, rows: buf.at[:, rows]
    wqkv, wo, wg, wu, wd = r["wqkv"], r["wo"], r["wg"], r["wu"], r["wd"]
    wqkv[own_rows, :] = r["wqkv_in"][...]
    qkv_sp = Spread(wqkv, flat)
    qkv_sp.start()
    wo[t, own_rows, :] = r["wo_in"][...]
    wo_ix = [slot() for _ in range(1, NT)]
    for k, i in zip(range(1, NT), wo_ix):
        w = wo.at[t, own_rows]
        send(w, w, i, z_to(k))
    wg[own_rows, :] = r["wg_in"][...]
    wu[own_rows, :] = r["wu_in"][...]
    wd[own_rows, :] = r["wd_in"][...]
    wo_sp, wg_sp, wu_sp, wd_sp = Spread(wo, deep), Spread(wg, flat), Spread(wu, flat), Spread(wd, flat)

    segr, segc = r["segr"], r["segc"]
    for m in range(MICRO):
        for b in range(L // 128):
            row = segr[m:m + 1, 128 * b:128 * b + 128].astype(F32)
            segc[m, 128 * b:128 * b + 128, :] = jnp.broadcast_to(row, (128, 128)).T.astype(jnp.int32)

    for i, (n, off) in enumerate(enumerate(group)):
        gain_cp[n].wait_recv()
    gsum = gm[...]
    for n in range(len(group)):
        gsum = gsum + gall[n]
    gains = r["gains"]
    gains[...] = gsum

    tok, cot, n1 = r["tok"], r["cot"], r["n1"]

    def norm_one(m):
        @pl.loop(0, R // CH)
        def _(i):
            xf = tok[m, at(i * CH, CH), :].astype(F32)
            rs = lax.rsqrt(jnp.mean(xf * xf, -1, keepdims=True) + EPS)
            n1[at(m * R + i * CH, CH), :] = (xf * rs * gains[0:1, :]).astype(BF)

    for m in range(MICRO):
        norm_one(m)

    q, kv, kvT = r["q"], r["kv"], r["kvT"]
    scale = HEAD_DIM ** -0.5
    qkv_sp.relay()
    for sp in (wg_sp, wu_sp, wd_sp):
        sp.start()
    qkv_sp.finish()
    kv_ix = [slot() for _ in range(MICRO)]
    other = {"ctx": lax.rem(c + 1, C)}

    def project(m):
        @pl.loop(0, R // RT)
        def _(i):
            acc = dot_nn(n1[at(m * R + i * RT, RT), :], wqkv[...])
            q[m, at(i * RT, RT), :] = (acc[:, 0:HP] * scale).astype(BF)
            kv[m, at(c * R + i * RT, RT), :] = acc[:, HP:HP + KV].astype(BF)
        w = kv.at[m, at(c * R, R)]
        send(w, w, kv_ix[m], other)

    for m in range(MICRO):
        project(m)
    for k, i in zip(range(1, NT), wo_ix):
        w = wo.at[t, own_rows]
        copy_to(w, w, i, z_to(k)).wait_recv()
    wo_sp.start()

    oT, onat, oown, lse = r["oT"], r["onat"], r["oown"], r["lse"]
    lanes = lax.broadcasted_iota(jnp.int32, (RT, HP), 1)

    def head_mask(v, h, shift):
        lo = shift + h * HEAD_DIM
        return jnp.where((lanes >= lo) & (lanes < lo + HEAD_DIM), v, jnp.zeros_like(v))

    def flip(m, start):
        @pl.loop(0, R // RT)
        def _(i):
            kvT[m, :, at(start + i * RT, RT)] = kv[m, at(start + i * RT, RT), :].T

    VOFF = HP - H
    for m in range(MICRO):
        oT[m, :, 0:VOFF, :] = jnp.zeros((NT, VOFF, R), BF)

    def attend(m):
        @pl.loop(0, R // RT)
        def _(i):
            kk = kv[m, :, 0:HP]
            sc = segc[m]
            sc = jnp.concatenate([sc] * (RT // 128), axis=1)
            sr = segr[m:m + 1, at(c * R + i * RT, RT)]
            qq = q[m, at(i * RT, RT), :]
            for h in range(NH):
                s = dot_nt(kk, head_mask(qq, h, 0))
                s = jnp.where(sc == sr, s, NEG)
                mx = jnp.max(s, axis=0, keepdims=True)
                e = jnp.exp(s - mx)
                tot = jnp.sum(e, axis=0, keepdims=True)
                p = (e * (1.0 / tot)).astype(BF)
                vT = kvT[m, H + h * HEAD_DIM:H + (h + 1) * HEAD_DIM, :]
                lo = VOFF + h * HEAD_DIM
                oT[m, t, lo:lo + HEAD_DIM, at(i * RT, RT)] = dot_nn(vT, p).astype(BF)
                lse[m, h, :, at(i * RT, RT)] = mx + jnp.log(tot)

    ago_ix = [[slot() for _ in range(1, NT)] for _ in range(MICRO)]

    def share_o(m):
        w = oT.at[m, t, pl.ds(VOFF, H)]
        for k in range(1, NT):
            send(w, w, ago_ix[m][k - 1], z_to(k))

    def wait_o(m):
        w = oT.at[m, t, pl.ds(VOFF, H)]
        for k in range(1, NT):
            copy_to(w, w, ago_ix[m][k - 1], z_to(k)).wait_recv()

    for m in range(MICRO):
        flip(m, c * R)
    for m in range(MICRO):
        w = kv.at[m, at(c * R, R)]
        copy_to(w, w, kv_ix[m], other).wait_recv()
        flip(m, lax.rem(c + 1, C) * R)
        attend(m)
        share_o(m)
        if m == 0:
            for sp in (wg_sp, wu_sp, wd_sp, wo_sp):
                sp.relay()
    for sp in (wo_sp, wg_sp, wu_sp, wd_sp):
        sp.finish()

    snd, rc1, rc2 = r["snd"], r["rc1"], r["rc2"]

    class Sum:
        def __init__(self, a, b, d):
            self.a, self.b, self.d = a, b, d
            self.ix = [[slot() for _ in range(3)] for _ in range(NCH)]

        def part(self, ref, j):
            a = self.a if ref is snd else self.b if ref is rc1 else self.d
            return ref.at[a, pl.ds(j * CH, CH)]

        def begin(self, j):
            @pl.when(outer)
            def _():
                copy_to(self.part(snd, j), self.part(rc1, j), self.ix[j][0], {"tp": side}).start()

        def step_a(self, j):
            @pl.when(inner)
            def _():
                copy_to(self.part(snd, j), self.part(rc1, j), self.ix[j][0], {"tp": side}).wait_recv()
                s = pl.ds(j * CH, CH)
                snd[self.a, s, :] = (snd[self.a, s, :].astype(F32) + rc1[self.b, s, :].astype(F32)).astype(BF)
                copy_to(self.part(snd, j), self.part(rc2, j), self.ix[j][1], {"tp": mid}).start()

        def step_b(self, j):
            @pl.when(inner)
            def _():
                copy_to(self.part(snd, j), self.part(rc2, j), self.ix[j][1], {"tp": mid}).wait_recv()
                s = pl.ds(j * CH, CH)
                rc2[self.d, s, :] = (snd[self.a, s, :].astype(F32) + rc2[self.d, s, :].astype(F32)).astype(BF)
                copy_to(self.part(rc2, j), self.part(rc2, j), self.ix[j][2], {"tp": side}).start()

        def queue(self):
            pending.append(lambda: self.step_a(0))
            for j in range(1, NCH):
                def both(j=j):
                    self.step_a(j)
                    self.step_b(j - 1)
                pending.append(both)
            pending.append(lambda: self.step_b(NCH - 1))

        def wait(self):
            @pl.when(outer)
            def _():
                for j in range(NCH):
                    copy_to(self.part(rc2, j), self.part(rc2, j), self.ix[j][2], {"tp": side}).wait_recv()

        def close(self):
            @pl.when(outer)
            def _():
                for j in range(NCH):
                    copy_to(self.part(snd, j), self.part(rc1, j), self.ix[j][0], {"tp": side}).wait_send()

            @pl.when(inner)
            def _():
                for j in range(NCH):
                    copy_to(self.part(snd, j), self.part(rc2, j), self.ix[j][1], {"tp": mid}).wait_send()
                    copy_to(self.part(rc2, j), self.part(rc2, j), self.ix[j][2], {"tp": side}).wait_send()

    def service(n):
        for _ in range(min(n, len(pending))):
            pending.pop(0)()

    dn2_sum = [Sum(m, m, m) for m in range(MICRO)]
    ffn_sum = [Sum(MICRO + m, m, MICRO + m) for m in range(MICRO)]
    dn1_sum = [Sum(m, MICRO + m, 2 * MICRO + m) for m in range(MICRO)]

    y1, n2, big = r["y1"], r["n2"], r["big"]
    hid, dg, du = big.at[0], big.at[1], big.at[2]

    def flip_o(m):
        @pl.loop(0, NT * (R // RT))
        def _(n):
            k = n // (R // RT)
            i = lax.rem(n, R // RT)
            onat[k, at(i * RT, RT), :] = oT[m, k, :, at(i * RT, RT)].T

    def ffn_rows(m, i):
        rr = pl.ds(i * RT, RT)
        gr = pl.ds(m * R + i * RT, RT)
        acc = tok[m, rr, :].astype(F32)
        att = dot_nt(onat[0, rr, :], wo[0])
        for k in range(1, NT):
            att = att + dot_nt(onat[k, rr, :], wo[k])
        acc = acc + att
        y1[m, rr, :] = acc
        rs = lax.rsqrt(jnp.mean(acc * acc, -1, keepdims=True) + EPS)
        n2v = (acc * rs * gains[1:2, :]).astype(BF)
        n2[gr, :] = n2v
        g = dot_nn(n2v, wg[...])
        u = dot_nn(n2v, wu[...])
        th = jnp.tanh(GELU_K * (g + GELU_A * g * g * g))
        half = 0.5 * (1.0 + th)
        gl = g * half
        hv = (gl * u).astype(BF)
        hid[gr, :] = hv
        dh = dot_nn(cot[gr, :], wd[...])
        dgl = half + 0.5 * g * (1.0 - th * th) * (GELU_K * (1.0 + 3.0 * GELU_A * g * g))
        dgv = (dh * u * dgl).astype(BF)
        duv = (dh * gl).astype(BF)
        dg[gr, :] = dgv
        du[gr, :] = duv
        snd[m, rr, :] = (dot_nt(dgv, wg[...]) + dot_nt(duv, wu[...])).astype(BF)
        for j in range(RT // CH):
            dn2_sum[m].begin(i * (RT // CH) + j)
        snd[MICRO + m, rr, :] = dot_nt(hv, wd[...]).astype(BF)

    for m in range(MICRO):
        wait_o(m)
        flip_o(m)
        oown[m] = onat[t]
        for i in range(R // RT):
            ffn_rows(m, i)
        dn2_sum[m].queue()
    service(3)

    gq, gg, gu, gd = r["gq"], r["gg"], r["gu"], r["gd"]
    go = gd.at[:, pl.ds(0, HP)]

    def grad(dst, left, right):
        @pl.loop(0, D // RT)
        def _(i):
            dst[at(i * RT, RT), :] = dot_tn(left[:, at(i * RT, RT)], right[...])

    class Reduce:
        def __init__(self, g, recv, stage, parts, out):
            self.g, self.recv, self.stage, self.parts, self.out = g, recv, stage, parts, out
            self.px = [slot() for _ in range(Y)]
            self.ix = [slot() for _ in offsets]

        def pair(self):
            for n in range(Y):
                self.pair_copy(n).start()

        def pair_copy(self, n):
            src = self.g.at[at((2 * n + 1 - core) * C * SR, C * SR)]
            return copy_to(src, self.recv.at[pl.ds(n * C * SR, C * SR)], self.px[n], partner)

        def square(self):
            for n in range(Y):
                rows = at((2 * n + core) * C * SR, C * SR)
                self.pair_copy(n).wait()
                tot = self.g[rows, :] + self.recv[n * C * SR:(n + 1) * C * SR, :]
                self.recv[n * C * SR:(n + 1) * C * SR, :] = tot
                self.stage[n * C * SR:(n + 1) * C * SR, :] = tot.astype(BF)
            for n, off in enumerate(offsets):
                pf, pc = square(off)
                src = self.stage.at[at(((pf // 2) * C + pc) * SR, SR)]
                send(src, self.parts.at[n], self.ix[n], dev_sq(off))

        def finish(self):
            tot = self.recv[at((y * C + c) * SR, SR), :]
            for n, off in enumerate(offsets):
                copy_to(self.parts.at[n], self.parts.at[n], self.ix[n], dev_sq(off)).wait_recv()
            for n in range(len(offsets)):
                tot = tot + self.parts[n].astype(F32)
            self.out[...] = tot

    acc = {"q": gq, "o": go, "g": gg, "u": gu, "d": gd}
    reds = {k: Reduce(acc[k], r["rv_" + k], r["st_" + k], r["pt_" + k], r["out_" + k]) for k in ("d", "g", "u", "q", "o")}
    grad(gd, cot, hid)
    reds["d"].pair()
    service(1)
    grad(gg, n2, dg)
    reds["g"].pair()
    service(1)
    grad(gu, n2, du)
    reds["u"].pair()
    service(1)

    ig, gacc = r["ig"], r["gacc"]
    gacc[...] = jnp.zeros_like(gacc)
    qm_all, dom_all = r["qm_all"], r["dom_all"]
    delta, dqT, dkv, dkv_in = r["delta"], r["dqT"], r["dkv"], r["dkv_in"]
    dqkv = n2.at[:, pl.ds(0, HP + KV)]

    def back_norm(m):
        dn2_sum[m].wait()

        @pl.loop(0, R // RT)
        def _(i):
            rr = at(i * RT, RT)
            yv = y1[m, rr, :]
            d2 = rc2[m, rr, :].astype(F32)
            tv = lax.rsqrt(jnp.mean(yv * yv, -1, keepdims=True) + EPS)
            e2 = gains[1:2, :] * d2
            dot = jnp.mean(yv * e2, -1, keepdims=True)
            dy = cot[at(m * R + i * RT, RT), :].astype(F32) + tv * e2 - yv * (tv * tv * tv * dot)
            ig[m, rr, :] = dy
            gacc[1:2, :] += jnp.sum(d2 * (yv * tv), axis=0, keepdims=True)
            ar = dy.astype(BF)
            dov = dot_nn(ar, wo[t]).astype(BF)
            doT = dov.T
            for h in range(NH):
                lo = VOFF + h * HEAD_DIM
                prod = doT[lo:lo + HEAD_DIM, :].astype(F32) * oT[m, t, lo:lo + HEAD_DIM, rr].astype(F32)
                delta[h, :, rr] = jnp.sum(prod, axis=0, keepdims=True)
                dom_all[at(h * R + i * RT, RT), :] = head_mask(dov, h, VOFF)
                qm_all[at(h * R + i * RT, RT), :] = head_mask(q[m, rr, :], h, 0)

    def back_half(m, key0, first):
        @pl.loop(0, R // RT)
        def _(i):
            sc = segc[m, at(key0, R), :]
            sc = jnp.concatenate([sc] * (RT // 128), axis=1)
            sr = segr[m:m + 1, at(c * R + i * RT, RT)]
            for h in range(NH):
                qs = at(h * R + i * RT, RT)
                s = dot_nt(kv[m, at(key0, R), 0:HP], qm_all[qs, :])
                s = jnp.where(sc == sr, s, NEG)
                p = jnp.exp(s - lse[m, h, :, at(i * RT, RT)])
                dp = dot_nt(kv[m, at(key0, R), KV - HP:KV], dom_all[qs, :])
                cs = at(i * RT, RT)
                big[h, pl.ds(R, R), cs] = p.astype(BF)
                big[h, pl.ds(0, R), cs] = (p * (dp - delta[h, :, at(i * RT, RT)])).astype(BF)

        @pl.loop(0, R // RT)
        def _(i):
            rr = at(i * RT, RT)
            r2 = pl.ds(pl.multiple_of(R + i * RT, RT), RT)
            dk = dot_nn(big[0, rr, :], qm_all[pl.ds(0, R), :])
            dv = dot_nn(big[0, r2, :], dom_all[pl.ds(0, R), :])
            for h in range(1, NH):
                dk = dk + dot_nn(big[h, rr, :], qm_all[pl.ds(h * R, R), :])
                dv = dv + dot_nn(big[h, r2, :], dom_all[pl.ds(h * R, R), :])
            dkv[rr, 0:128] = dk[:, 0:128]
            dkv[rr, 128:256] = dk[:, 128:256] + dv[:, 0:128]
            dkv[rr, 256:384] = dv[:, 128:256]
        for h in range(NH):
            hs = pl.ds(h * HEAD_DIM, HEAD_DIM)
            part = dot_nn(kvT[m, hs, at(key0, R)], big[h, pl.ds(0, R), :])
            if first:
                dqT[hs, :] = part
            else:
                dqT[hs, :] = dqT[hs, :] + part

    dkv_ix = [slot() for _ in range(MICRO)]
    dkv_out = r["dkv_out"]

    def back_attn(m):
        back_half(m, lax.rem(c + 1, C) * R, True)
        dkv_out[m] = dkv[...].astype(BF)
        send(dkv_out.at[m], dkv_in.at[m], dkv_ix[m], other)
        service(2)
        back_half(m, c * R, False)
        dqkv[pl.ds(m * R, R), 0:HP] = jnp.zeros((R, HP), BF)
        dqkv[pl.ds(m * R, R), 0:H] = (dqT[...] * scale).T.astype(BF)

    def join(m):
        copy_to(dkv_out.at[m], dkv_in.at[m], dkv_ix[m], other).wait_recv()
        dn2_sum[m].close()

        for i in range(R // RT):
            rr = pl.ds(i * RT, RT)
            gr = pl.ds(m * R + i * RT, RT)
            dqkv[gr, HP:HP + KV] = (dkv[rr, :] + dkv_in[m, rr, :].astype(F32)).astype(BF)
            snd[m, rr, :] = dot_nt(dqkv[gr, :], wqkv[...]).astype(BF)
            for j in range(RT // CH):
                dn1_sum[m].begin(i * (RT // CH) + j)
        dn1_sum[m].queue()

    def ffn_begin(m):
        for j in range(NCH):
            ffn_sum[m].begin(j)
        ffn_sum[m].queue()

    service(len(pending))
    for k in ("d", "g", "u"):
        reds[k].square()
    for m in range(MICRO):
        back_norm(m)
        ffn_begin(m)
        back_attn(m)
        service(len(pending))
        join(m)
    grad(gq, n1, dqkv)
    reds["q"].pair()
    service(2)

    @pl.loop(0, D // RT)
    def _(i):
        cs = at(i * RT, RT)
        acc = dot_tn(ig[0, :, cs].astype(BF), oown[0])
        for m in range(1, MICRO):
            acc = acc + dot_tn(ig[m, :, cs].astype(BF), oown[m])
        go[cs, :] = acc
    reds["o"].pair()
    service(1)
    reds["q"].square()
    reds["o"].square()
    service(len(pending))

    out = r["out"]
    for m in range(MICRO):
        ffn_sum[m].wait()

        @pl.loop(0, R // CH)
        def _(i):
            rr = at(i * CH, CH)
            out[m, rr, :] = (y1[m, rr, :] + rc2[MICRO + m, rr, :].astype(F32)).astype(BF)

    for k in ("d", "g", "u"):
        reds[k].finish()

    for m in range(MICRO):
        dn1_sum[m].wait()

        @pl.loop(0, R // CH)
        def _(i):
            rr = at(i * CH, CH)
            xv = tok[m, rr, :].astype(F32)
            d1 = rc2[2 * MICRO + m, rr, :].astype(F32)
            tv = lax.rsqrt(jnp.mean(xv * xv, -1, keepdims=True) + EPS)
            e1 = gains[0:1, :] * d1
            dot = jnp.mean(xv * e1, -1, keepdims=True)
            ig[m, rr, :] = ig[m, rr, :] + tv * e1 - xv * (tv * tv * tv * dot)
            gacc[0:1, :] += jnp.sum(d1 * (xv * tv), axis=0, keepdims=True)

    gin = r["gin"]
    cps = []
    for n, off in enumerate(group):
        cps.append(send(gacc, gin.at[n], slot(), dev_group(off)))
    for k in ("q", "o"):
        reds[k].finish()
    for cp in cps:
        cp.wait_recv()
    tot = gacc[...]
    for n in range(len(group)):
        tot = tot + gin[n]
    r["out_gain"][...] = lax.dot_general(
        tot, place.astype(F32), (((1,), (1,)), ((), ())), precision=lax.Precision.HIGHEST,
        preferred_element_type=F32)

    for cp in sends:
        cp.wait_send()
    for s in ffn_sum + dn1_sum:
        s.close()
    assert counter[0] <= ssem.shape[0]


def fused_shards(dims, tokens, segments, cotangent, query_weight, key_weight, value_weight, out_weight,
                 gate_weight, up_weight, down_weight, attn_gain, ffn_gain):
    R, D, H, FF, C, NF, NT, MICRO = dims
    L = C * R
    SR = D // (NF * C)
    NH = H // HEAD_DIM
    HP, KV, Y = 256, 2 * H, NF // 2
    HALF = Y * C * SR
    NO = Y * C - 1
    NG = NF * C - 1
    W = HP + KV
    pad = jnp.zeros((SR, HP - H), BF)
    wqkv_in = jnp.concatenate([query_weight, pad, key_weight, value_weight], axis=1)
    wo_in = jnp.concatenate([pad, out_weight], axis=1)
    ins = [
        ("tok", tokens[:, 0]),
        ("segr", segments[:, 0]),
        ("cot", cotangent.reshape(MICRO * R, D)),
        ("wqkv_in", wqkv_in),
        ("wo_in", wo_in),
        ("wg_in", gate_weight),
        ("wu_in", up_weight),
        ("wd_in", down_weight),
        ("gain_a", attn_gain[None]),
        ("gain_f", ffn_gain[None]),
    ]
    outs = [
        ("out", (MICRO, R, D), BF),
        ("ig", (MICRO, R, D), F32),
        ("out_q", (SR, W), F32),
        ("out_o", (SR, HP), F32),
        ("out_g", (SR, FF), F32),
        ("out_u", (SR, FF), F32),
        ("out_d", (SR, FF), F32),
        ("out_gain", (8, SR), F32),
    ]
    v = pltpu.VMEM
    scratch = [
        ("gmine", v((8, D), F32)), ("gall", v((NG, 8, D), F32)), ("gains", v((8, D), F32)),
        ("gacc", v((8, D), F32)), ("gin", v((NG, 8, D), F32)),
        ("wqkv", v((D, W), BF)), ("wo", v((NT, D, HP), BF)),
        ("wg", v((D, FF), BF)), ("wu", v((D, FF), BF)), ("wd", v((D, FF), BF)),
        ("segc", v((MICRO, L, 128), jnp.int32)),
        ("n1", v((MICRO * R, D), BF)), ("q", v((MICRO, R, HP), BF)),
        ("kv", v((MICRO, L, KV), BF)), ("kvT", v((MICRO, KV, L), BF)),
        ("oT", v((MICRO, NT, HP, R), BF)), ("onat", v((NT, R, HP), BF)), ("oown", v((MICRO, R, HP), BF)),
        ("lse", v((MICRO, NH, 1, R), F32)),
        ("snd", v((2 * MICRO, R, D), BF)), ("rc1", v((2 * MICRO, R, D), BF)), ("rc2", v((3 * MICRO, R, D), BF)),
        ("y1", v((MICRO, R, D), F32)), ("n2", v((MICRO * R, D), BF)),
        ("big", v((3, MICRO * R, FF), BF)),
        ("qm_all", v((NH * R, HP), BF)), ("dom_all", v((NH * R, HP), BF)),
        ("delta", v((NH, 1, R), F32)), ("dqT", v((H, R), F32)),
        ("dkv", v((R, KV), F32)),
        ("dkv_in", v((MICRO, R, KV), BF)), ("dkv_out", v((MICRO, R, KV), BF)),
    ]
    for k, cols in (("q", W), ("o", HP), ("g", FF), ("u", FF), ("d", FF)):
        if k != "o":
            scratch += [("g" + k, v((D, cols), F32))]
        scratch += [("rv_" + k, v((HALF, cols), F32)),
                    ("st_" + k, v((HALF, cols), BF)), ("pt_" + k, v((NO, SR, cols), BF))]
    nsem = 256
    scratch += [("ssem", pltpu.SemaphoreType.DMA((nsem,))), ("rsem", pltpu.SemaphoreType.DMA((nsem,)))]
    names = [n for n, _ in ins] + [n for n, _, _ in outs] + [n for n, _ in scratch]
    vm = pl.BlockSpec(memory_space=pltpu.VMEM)
    res = pl.pallas_call(
        functools.partial(layer_kernel, dims, names),
        out_shape=[jax.ShapeDtypeStruct(s, d) for _, s, d in outs],
        in_specs=[vm] * len(ins),
        out_specs=[vm] * len(outs),
        scratch_shapes=[s for _, s in scratch],
        compiler_params=pltpu.CompilerParams(
            collective_id=0, has_side_effects=True, vmem_limit_bytes=67043328),
    )(*[a for _, a in ins])
    out, ig, g_q, g_o, g_g, g_u, g_d, gain = res
    return (out[:, None], ig[:, None], g_q[:, 0:H], g_q[:, HP:HP + H], g_q[:, HP + H:W], g_o[:, HP - H:],
            g_g, g_u, g_d, gain[0], gain[1])


def fits(dims, seqs):
    R, D, H, FF, C, NF, NT, MICRO = dims
    blocks = D % (16 * NF * C) == 0 and R % 256 == 0 and D % 256 == 0
    return (C, NT, NF % 2, H, MICRO, seqs) == (2, 4, 0, 192, 2, 1) and FF == R and R <= 512 and D <= 768 and blocks


SPECS = (
    P(None, "fsdp", "ctx", None),
    P(None, "fsdp", None),
    P(None, "fsdp", "ctx", None),
) + (P(("fsdp", "ctx"), "tp"),) * 7 + (P(("fsdp", "ctx")),) * 2
OUT_SPECS = (P(None, "fsdp", "ctx", None),) * 2 + (P(("fsdp", "ctx"), "tp"),) * 7 + (P(("fsdp", "ctx")),) * 2


def solution(mesh):
    nf, nc, nt = mesh.shape["fsdp"], mesh.shape["ctx"], mesh.shape["tp"]

    def chosen(*args):
        tokens, weight, ffw = args[0], args[3], args[7]
        micro, seqs, rows, width = tokens.shape
        dims = (rows, width, weight.shape[1], ffw.shape[1], nc, nf, nt, micro)
        return fused_shards(dims, *args) if fits(dims, seqs) else shards(*args)

    return jax.shard_map(chosen, mesh=mesh, in_specs=SPECS, out_specs=OUT_SPECS, check_vma=False)
```

```python
import functools

import jax
import jax.numpy as jnp
from jax import lax
from jax.experimental import pallas as pl
from jax.experimental.pallas import tpu as pltpu
from jax.sharding import PartitionSpec as P

HEAD_DIM = 64


EPS = 1e-06


def gather_weights(
    query_weight,
    key_weight,
    value_weight,
    out_weight,
    gate_weight,
    up_weight,
    down_weight,
    attn_gain,
    ffn_gain,
):
    return (
        lax.all_gather(query_weight, ("fsdp", "ctx"), axis=0, tiled=True),
        lax.all_gather(key_weight, ("fsdp", "ctx"), axis=0, tiled=True),
        lax.all_gather(value_weight, ("fsdp", "ctx"), axis=0, tiled=True),
        lax.all_gather(out_weight, ("fsdp", "ctx"), axis=0, tiled=True),
        lax.all_gather(gate_weight, ("fsdp", "ctx"), axis=0, tiled=True),
        lax.all_gather(up_weight, ("fsdp", "ctx"), axis=0, tiled=True),
        lax.all_gather(down_weight, ("fsdp", "ctx"), axis=0, tiled=True),
        lax.all_gather(attn_gain, ("fsdp", "ctx"), axis=0, tiled=True),
        lax.all_gather(ffn_gain, ("fsdp", "ctx"), axis=0, tiled=True),
    )


def tensor_sum(partial_value):
    return lax.psum(partial_value, "tp")


def normalize(values, gain_vec):
    return values * lax.rsqrt(jnp.mean(values * values, -1, keepdims=True) + EPS) * gain_vec


def gelu_mix(gate_act, up_act):
    return jax.nn.gelu(gate_act, approximate=True) * up_act


def contract_last(left_op, right_op):
    return lax.dot_general(
        left_op, right_op, (((1,), (1,)), ((), ())), preferred_element_type=jnp.float32
    )


def contract_first(left_op, right_op):
    return lax.dot_general(
        left_op, right_op, (((0,), (0,)), ((), ())), preferred_element_type=jnp.float32
    )


def masked_scores(queries, key_whole, query_seg, seg_all, head_count):
    local_rows = queries.shape[0]
    query_heads = queries.reshape(local_rows, head_count, HEAD_DIM)
    key_heads = key_whole.reshape(key_whole.shape[0], head_count, HEAD_DIM)
    products = jnp.einsum(
        "qhd,khd->hqk", query_heads, key_heads, preferred_element_type=jnp.float32
    ) * HEAD_DIM ** (-0.5)
    same_doc = query_seg[:, None] == seg_all[None, :]
    return jnp.where(same_doc[None], products, -1e30)


def forward_pass(inputs, seg_all, gathered, ctx_pos):
    w_query, w_key, w_value, w_out, w_gate, w_up, w_down, gain_attn, gain_ffn = gathered
    head_count = w_query.shape[1] // HEAD_DIM
    local_rows = inputs.shape[0]
    query_seg = lax.dynamic_slice_in_dim(seg_all, ctx_pos * local_rows, local_rows)
    inputs_f = inputs.astype(jnp.float32)
    normed_one = normalize(inputs_f, gain_attn.astype(jnp.float32)).astype(jnp.bfloat16)
    queries = jnp.dot(normed_one, w_query, preferred_element_type=jnp.float32).astype(jnp.bfloat16)
    key_local = jnp.dot(normed_one, w_key, preferred_element_type=jnp.float32).astype(jnp.bfloat16)
    value_local = jnp.dot(normed_one, w_value, preferred_element_type=jnp.float32).astype(
        jnp.bfloat16
    )
    key_whole, value_whole = (
        lax.all_gather(key_local, "ctx", axis=0, tiled=True),
        lax.all_gather(value_local, "ctx", axis=0, tiled=True),
    )
    scores = masked_scores(queries, key_whole, query_seg, seg_all, head_count)
    row_max = jnp.max(scores, -1, keepdims=True)
    row_total = jnp.sum(jnp.exp(scores - row_max), -1, keepdims=True)
    log_total = row_max + jnp.log(row_total)
    probs_low = jnp.exp(scores - log_total).astype(jnp.bfloat16)
    value_heads = value_whole.reshape(value_whole.shape[0], head_count, HEAD_DIM)
    attn_mixed = jnp.einsum(
        "hqk,khd->qhd", probs_low, value_heads, preferred_element_type=jnp.float32
    )
    attn_mixed = attn_mixed.reshape(local_rows, head_count * HEAD_DIM).astype(jnp.bfloat16)
    attn_partial = contract_last(attn_mixed, w_out)
    residual = inputs_f + tensor_sum(attn_partial)
    normed_two = normalize(residual, gain_ffn.astype(jnp.float32)).astype(jnp.bfloat16)
    gate_act = jnp.dot(normed_two, w_gate, preferred_element_type=jnp.float32)
    up_act = jnp.dot(normed_two, w_up, preferred_element_type=jnp.float32)
    hidden = gelu_mix(gate_act, up_act).astype(jnp.bfloat16)
    ffn_partial = contract_last(hidden, w_down)
    result = (residual + tensor_sum(ffn_partial)).astype(jnp.bfloat16)
    stored = (
        inputs_f,
        normed_one,
        queries,
        key_whole,
        value_whole,
        log_total,
        attn_mixed,
        residual,
        normed_two,
        gate_act,
        up_act,
        hidden,
        query_seg,
    )
    return (result, stored)


def backward_pass(cot_rows, stored, gathered, seg_all, ctx_pos):
    w_query, w_key, w_value, w_out, w_gate, w_up, w_down, gain_attn, gain_ffn = gathered
    (
        inputs_f,
        normed_one,
        queries,
        key_whole,
        value_whole,
        log_total,
        attn_mixed,
        residual,
        normed_two,
        gate_act,
        up_act,
        hidden,
        query_seg,
    ) = stored
    head_count = w_query.shape[1] // HEAD_DIM
    local_rows = queries.shape[0]
    seq_rows = key_whole.shape[0]
    scale = HEAD_DIM ** (-0.5)
    dout = cot_rows.astype(jnp.float32)
    dout_low = dout.astype(jnp.bfloat16)
    grad_down = contract_first(dout_low, hidden)
    dhidden = jnp.dot(dout_low, w_down, preferred_element_type=jnp.float32)
    mixed_unused, mix_back = jax.vjp(gelu_mix, gate_act, up_act)
    dgate, dup = mix_back(dhidden)
    dgate_low = dgate.astype(jnp.bfloat16)
    dup_low = dup.astype(jnp.bfloat16)
    grad_gate = contract_first(normed_two, dgate_low)
    grad_up = contract_first(normed_two, dup_low)
    dn2_partial = contract_last(dgate_low, w_gate) + contract_last(dup_low, w_up)
    norm_unused, norm_back = jax.vjp(normalize, residual, gain_ffn.astype(jnp.float32))
    dresid_norm, grad_gain_ffn = norm_back(tensor_sum(dn2_partial))
    dresidual = dout + dresid_norm
    dres_low = dresidual.astype(jnp.bfloat16)
    grad_out = contract_first(dres_low, attn_mixed)
    dmixed = jnp.dot(dres_low, w_out, preferred_element_type=jnp.float32).astype(jnp.bfloat16)
    dmixed_heads = dmixed.reshape(local_rows, head_count, HEAD_DIM)
    scores = masked_scores(queries, key_whole, query_seg, seg_all, head_count)
    prob_full = jnp.exp(scores - log_total)
    key_heads = key_whole.reshape(seq_rows, head_count, HEAD_DIM)
    value_heads = value_whole.reshape(seq_rows, head_count, HEAD_DIM)
    dprobs = jnp.einsum(
        "qhd,khd->hqk", dmixed_heads, value_heads, preferred_element_type=jnp.float32
    )
    row_delta = jnp.sum(prob_full * dprobs, -1, keepdims=True)
    dscores = (prob_full * (dprobs - row_delta)).astype(jnp.bfloat16)
    dquery = (
        jnp.einsum("hqk,khd->qhd", dscores, key_heads, preferred_element_type=jnp.float32) * scale
    )
    query_all, dmixed_all = (
        lax.all_gather(queries, "ctx", axis=0, tiled=True),
        lax.all_gather(dmixed, "ctx", axis=0, tiled=True),
    )
    log_all, delta_all = (
        lax.all_gather(log_total, "ctx", axis=1, tiled=True),
        lax.all_gather(row_delta, "ctx", axis=1, tiled=True),
    )
    start = ctx_pos * local_rows
    key_own = lax.dynamic_slice_in_dim(key_whole, start, local_rows)
    value_own = lax.dynamic_slice_in_dim(value_whole, start, local_rows).reshape(
        local_rows, head_count, HEAD_DIM
    )
    scores_own = masked_scores(query_all, key_own, seg_all, query_seg, head_count)
    prob_own = jnp.exp(scores_own - log_all)
    dmixed_all_heads = dmixed_all.reshape(seq_rows, head_count, HEAD_DIM)
    query_all_heads = query_all.reshape(seq_rows, head_count, HEAD_DIM)
    dprobs_own = jnp.einsum(
        "qhd,khd->hqk", dmixed_all_heads, value_own, preferred_element_type=jnp.float32
    )
    dscores_own = (prob_own * (dprobs_own - delta_all)).astype(jnp.bfloat16)
    dkey_local = (
        jnp.einsum("hqk,qhd->khd", dscores_own, query_all_heads, preferred_element_type=jnp.float32)
        * scale
    ).reshape(local_rows, head_count * HEAD_DIM)
    dvalue_local = jnp.einsum(
        "hqk,qhd->khd",
        prob_own.astype(jnp.bfloat16),
        dmixed_all_heads,
        preferred_element_type=jnp.float32,
    ).reshape(local_rows, head_count * HEAD_DIM)
    dquery_low = dquery.reshape(local_rows, head_count * HEAD_DIM).astype(jnp.bfloat16)
    dkey_low = dkey_local.astype(jnp.bfloat16)
    dvalue_low = dvalue_local.astype(jnp.bfloat16)
    grad_query = contract_first(normed_one, dquery_low)
    grad_key = contract_first(normed_one, dkey_low)
    grad_value = contract_first(normed_one, dvalue_low)
    dn1_partial = (
        contract_last(dquery_low, w_query)
        + contract_last(dkey_low, w_key)
        + contract_last(dvalue_low, w_value)
    )
    norm_unused_two, norm_back_two = jax.vjp(normalize, inputs_f, gain_attn.astype(jnp.float32))
    dinput_norm, grad_gain_attn = norm_back_two(tensor_sum(dn1_partial))
    input_grad = dresidual + dinput_norm
    grad_terms = (
        grad_query,
        grad_key,
        grad_value,
        grad_out,
        grad_gate,
        grad_up,
        grad_down,
        grad_gain_attn,
        grad_gain_ffn,
    )
    return (input_grad, grad_terms)


def shards(
    tokens,
    segments,
    cotangent,
    query_weight,
    key_weight,
    value_weight,
    out_weight,
    gate_weight,
    up_weight,
    down_weight,
    attn_gain,
    ffn_gain,
):
    ctx_pos = lax.axis_index("ctx")
    results = []
    input_grads = []
    total_grads = None
    for micro_step in range(tokens.shape[0]):
        seg_all = segments[micro_step, 0]
        gathered = gather_weights(
            query_weight,
            key_weight,
            value_weight,
            out_weight,
            gate_weight,
            up_weight,
            down_weight,
            attn_gain,
            ffn_gain,
        )
        result, stored = forward_pass(tokens[micro_step, 0], seg_all, gathered, ctx_pos)
        gathered = gather_weights(
            query_weight,
            key_weight,
            value_weight,
            out_weight,
            gate_weight,
            up_weight,
            down_weight,
            attn_gain,
            ffn_gain,
        )
        input_grad, grad_terms = backward_pass(
            cotangent[micro_step, 0], stored, gathered, seg_all, ctx_pos
        )
        results.append(result)
        input_grads.append(input_grad)
        total_grads = (
            grad_terms if total_grads is None else jax.tree.map(jnp.add, total_grads, grad_terms)
        )
    gain_attn_total = total_grads[7]
    gain_ffn_total = total_grads[8]
    owned = (
        lax.psum_scatter(total_grads[0], ("fsdp", "ctx"), scatter_dimension=0, tiled=True),
        lax.psum_scatter(total_grads[1], ("fsdp", "ctx"), scatter_dimension=0, tiled=True),
        lax.psum_scatter(total_grads[2], ("fsdp", "ctx"), scatter_dimension=0, tiled=True),
        lax.psum_scatter(total_grads[3], ("fsdp", "ctx"), scatter_dimension=0, tiled=True),
        lax.psum_scatter(total_grads[4], ("fsdp", "ctx"), scatter_dimension=0, tiled=True),
        lax.psum_scatter(total_grads[5], ("fsdp", "ctx"), scatter_dimension=0, tiled=True),
        lax.psum_scatter(total_grads[6], ("fsdp", "ctx"), scatter_dimension=0, tiled=True),
        lax.psum_scatter(gain_attn_total, ("fsdp", "ctx"), scatter_dimension=0, tiled=True),
        lax.psum_scatter(gain_ffn_total, ("fsdp", "ctx"), scatter_dimension=0, tiled=True),
    )
    output = jnp.stack(results)[:, None]
    input_grad_all = jnp.stack(input_grads)[:, None]
    return (
        output,
        input_grad_all,
        owned[0],
        owned[1],
        owned[2],
        owned[3],
        owned[4],
        owned[5],
        owned[6],
        owned[7],
        owned[8],
    )


NEG = -1e30
MESH = pl.DeviceIdType.MESH
BF = jnp.bfloat16
F32 = jnp.float32
GELU_K = 0.7978845608028654
GELU_A = 0.044715
ORDER = (
    ("wS", "u"), ("prep",), ("wS", "d"), ("qR",), ("P", 0), ("wX", "u"), ("wX", "d"), ("wS", "o"), ("wY", "d"),
    ("wY", "u"), ("AT", 0, 0), ("wS", "g"), ("P", 1), ("wX", "o"), ("wX", "g"), ("O", 0, 0), ("AT", 0, 1),
    ("AT", 1, 0), ("wY", "o"), ("wY", "g"), ("wF",), ("F", 0, 0), ("AT", 1, 1), ("O", 0, 1), ("A", "n", 0, 0),
    ("A", "n", 0, 1), ("F", 0, 1), ("O", 1, 0), ("F", 1, 0), ("A", "n", 0, 2), ("O", 1, 1), ("F", 1, 1),
    ("B", "n", 0, 1), ("fB", 0), ("fB", 1), ("A", "n", 0, 3), ("G", "g"), ("A", "n", 1, 0), ("B", "n", 0, 2),
    ("B", "n", 0, 0), ("B", "n", 0, 3), ("A", "n", 1, 1), ("A", "n", 1, 3), ("B", "n", 1, 0), ("G", "u"), ("G", "d"),
    ("B", "n", 1, 1), ("A", "n", 1, 2), ("B", "n", 1, 3), ("BN", 0), ("A", "f", 0, 1), ("A", "f", 0, 0), ("SQ", "g"),
    ("PE", 0), ("B", "n", 1, 2), ("A", "f", 0, 2), ("B", "f", 0, 1), ("A", "f", 0, 3), ("OW", 0), ("A", "f", 1, 0),
    ("B", "f", 0, 0), ("B", "f", 0, 2), ("SQ", "u"), ("SQ", "d"), ("BN", 1), ("J", 0), ("A", "f", 1, 2),
    ("A", "f", 1, 1), ("B", "f", 0, 3), ("PE", 1), ("B", "f", 1, 0), ("SF", "g"), ("B", "f", 1, 2), ("OUT", 0, 1),
    ("A", "d", 0, 0), ("A", "f", 1, 3), ("OUT", 0, 0), ("OW", 1), ("B", "f", 1, 1), ("A", "d", 0, 1),
    ("B", "d", 0, 0), ("Go",), ("J", 1), ("A", "d", 0, 2), ("B", "f", 1, 3), ("SQ", "o"), ("OUT", 0, 2), ("SF", "d"),
    ("Gq",), ("OUT", 1, 2), ("B", "d", 0, 1), ("A", "d", 1, 0), ("A", "d", 0, 3), ("FIN", 0, 0), ("B", "d", 0, 2),
    ("FIN", 0, 1), ("B", "d", 1, 0), ("OUT", 1, 0), ("SQ", "q"), ("OUT", 0, 3), ("GZ",), ("SF", "o"), ("OUT", 1, 3),
    ("FIN", 1, 0), ("FIN", 0, 2), ("SF", "u"), ("A", "d", 1, 2), ("A", "d", 1, 3), ("GR",), ("B", "d", 0, 3),
    ("OUT", 1, 1), ("SF", "q"), ("A", "d", 1, 1), ("B", "d", 1, 2), ("B", "d", 1, 3), ("FIN", 0, 3), ("FIN", 1, 3),
    ("GF",), ("B", "d", 1, 1), ("FIN", 1, 2), ("FIN", 1, 1),
)


def dot_nn(a, b):
    return lax.dot_general(a, b, (((1,), (0,)), ((), ())), preferred_element_type=F32)


def dot_nt(a, b):
    return lax.dot_general(a, b, (((1,), (1,)), ((), ())), preferred_element_type=F32)


def dot_tn(a, b):
    return lax.dot_general(a, b, (((0,), (0,)), ((), ())), preferred_element_type=F32)


def at(i, n):
    return pl.ds(pl.multiple_of(i, n), n)


def layer_kernel(dims, names, *refs):
    r = dict(zip(names, refs))
    R, D, H, FF, C, NF, NT, MICRO = dims
    L = C * R
    NH = H // HEAD_DIM
    HP = 256
    KV = 2 * H
    Y = NF // 2
    SR = D // (NF * C)
    RT = 256
    CH = 128
    NCH = R // CH
    f = lax.axis_index("fsdp")
    c = lax.axis_index("ctx")
    t = lax.axis_index("tp")
    core = lax.rem(f, 2)
    y = f // 2
    shard = f * C + c
    partner = {"fsdp": f + 1 - 2 * core}
    ssem, rsem = r["ssem"], r["rsem"]
    counter = [0]

    def slot():
        counter[0] += 1
        return counter[0] - 1

    def copy_to(src, dst, idx, dev):
        return pltpu.make_async_remote_copy(
            src_ref=src, dst_ref=dst, send_sem=ssem.at[idx], recv_sem=rsem.at[idx],
            device_id=dev, device_id_type=MESH)

    offsets = [(dy, dc) for dy in range(Y) for dc in range(C) if (dy, dc) != (0, 0)]

    def square(off):
        dy, dc = off
        return (2 * lax.rem(y + dy, Y) + core, lax.rem(c + dc, C))

    def square_from(off):
        dy, dc = off
        return (2 * lax.rem(y + Y - dy, Y) + core, lax.rem(c + C - dc, C))

    def dev_sq(off):
        pf, pc = square(off)
        return {"fsdp": pf, "ctx": pc}

    def z_to(k):
        return {"tp": lax.rem(t + k, NT)}

    group = [(df, dc) for df in range(NF) for dc in range(C) if (df, dc) != (0, 0)]

    def dev_group(off):
        return {"fsdp": lax.rem(f + off[0], NF), "ctx": lax.rem(c + off[1], C)}

    outer = (t == 0) | (t == NT - 1)
    inner = (t != 0) & (t != NT - 1)
    side = jnp.where(t == 0, 1, jnp.where(t == NT - 1, NT - 2, jnp.where(t == 1, 0, NT - 1)))
    mid = NT - 1 - t

    local = r["lsem"]
    load_tok = pltpu.make_async_copy(r["tok_in"], r["tok"], local.at[0])
    load_cot = pltpu.make_async_copy(r["cot_in"], r["cot"], local.at[1])
    load_tok.start()
    load_cot.start()

    bar = pltpu.get_barrier_semaphore()
    for off in group:
        pl.semaphore_signal(bar, inc=1, device_id=dev_group(off), device_id_type=MESH)
    for k in range(1, NT):
        pl.semaphore_signal(bar, inc=1, device_id=z_to(k), device_id_type=MESH)
    pl.semaphore_wait(bar, len(group) + NT - 1)

    sends = []

    def send(src, dst, idx, dev):
        cp = copy_to(src, dst, idx, dev)
        cp.start()
        sends.append(cp)
        return cp

    def rows_of(off):
        pf, pc = square_from(off)
        return at((pf * C + pc) * SR, SR)

    own_rows = at(shard * SR, SR)

    class Spread:
        def __init__(self, buf, view, far):
            self.buf, self.view, self.far = buf, view, far
            self.ix = {off: slot() for off in offsets}
            self.px = slot()
            self.rx = {off: slot() for off in offsets}

        def rows(self, off):
            return self.view(self.buf, rows_of(off))

        def start(self):
            w = self.view(self.buf, own_rows)
            for off in offsets:
                if self.far or 0 in off:
                    send(w, w, self.ix[off], dev_sq(off))
            if self.far:
                self.near()

        def near(self):
            w = self.view(self.buf, own_rows)
            send(w, w, self.px, partner)

        def relay_x(self):
            w = self.rows((0, 1))
            copy_to(w, w, self.ix[(0, 1)], partner).wait_recv()
            if not self.far:
                send(w, w, self.ix[(1, 1)], dev_sq((1, 0)))
            send(w, w, self.rx[(0, 1)], partner)

        def relay_y(self):
            for off in ((1, 0), (1, 1)):
                w = self.rows(off)
                copy_to(w, w, self.ix[off], partner).wait_recv()
                send(w, w, self.rx[off], partner)

        def finish(self):
            w = self.view(self.buf, own_rows)
            copy_to(w, w, self.px, partner).wait_recv()
            for off in offsets:
                copy_to(w, w, self.rx[off], partner).wait_recv()

    flat = lambda buf, rows: buf.at[rows]
    deep = lambda buf, rows: buf.at[:, rows]
    wqkv, wo, wg, wu, wd = r["wqkv"], r["wo"], r["wg"], r["wu"], r["wd"]
    def spot(width, shift):
        i = lax.broadcasted_iota(jnp.int32, (H, width), 0)
        j = lax.broadcasted_iota(jnp.int32, (H, width), 1)
        return (j == i + shift).astype(BF)

    W = HP + KV
    VOFF = HP - H
    wqkv[own_rows, :] = (dot_nn(r["wq_in"][...], spot(W, 0)) + dot_nn(r["wk_in"][...], spot(W, HP))
                         + dot_nn(r["wv_in"][...], spot(W, HP + H))).astype(BF)
    qkv_sp = Spread(wqkv, flat, True)
    qkv_sp.start()
    wo[t, own_rows, :] = dot_nn(r["wo_in"][...], spot(HP, VOFF)).astype(BF)
    wo_ix = [slot() for _ in range(1, NT)]
    for k, i in zip(range(1, NT), wo_ix):
        w = wo.at[t, own_rows]
        send(w, w, i, z_to(k))
    gm = r["gmine"]
    cols = lax.broadcasted_iota(jnp.int32, (SR, D), 1)
    rows = lax.broadcasted_iota(jnp.int32, (SR, D), 0)
    place = (cols == rows + shard * SR).astype(BF)
    gm[...] = jnp.zeros_like(gm)
    gm[0:1, :] = dot_nn(r["gain_a"][...], place)
    gm[1:2, :] = dot_nn(r["gain_f"][...], place)
    gall = r["gall"]
    gain_cp = []
    for n, off in enumerate(group):
        gain_cp.append(send(gm, gall.at[n], slot(), dev_group(off)))

    wg[own_rows, :] = r["wg_in"][...]
    wu[own_rows, :] = r["wu_in"][...]
    wd[own_rows, :] = r["wd_in"][...]
    wo_sp, wg_sp, wu_sp, wd_sp = (Spread(b, v, False) for b, v in ((wo, deep), (wg, flat), (wu, flat), (wd, flat)))
    spreads = {"o": wo_sp, "g": wg_sp, "u": wu_sp, "d": wd_sp}
    for w in "gud":
        spreads[w].near()

    segr, segc = r["segr"].at[:, 0], r["segc"]
    gains, gacc, oT = r["gains"], r["gacc"], r["oT"]
    tok, cot, n1 = r["tok"], r["cot"], r["n1"]

    def prepare():
        for m in range(MICRO):
            for b in range(L // 128):
                row = segr[m:m + 1, 128 * b:128 * b + 128].astype(F32)
                segc[m, 128 * b:128 * b + 128, :] = jnp.broadcast_to(row, (128, 128)).T.astype(jnp.int32)
        for m in range(MICRO):
            oT[m, :, 0:VOFF, :] = jnp.zeros((NT, VOFF, R), BF)
        for cp in gain_cp:
            cp.wait_recv()
        gsum = gm[...]
        for n in range(len(group)):
            gsum = gsum + gall[n]
        gains[...] = gsum
        load_tok.wait()
        for m in range(MICRO):
            norm_one(m)
        gacc[...] = jnp.zeros_like(gacc)

    def norm_one(m):
        @pl.loop(0, R // CH)
        def _(i):
            xf = tok[m, at(i * CH, CH), :].astype(F32)
            rs = lax.rsqrt(jnp.mean(xf * xf, -1, keepdims=True) + EPS)
            n1[at(m * R + i * CH, CH), :] = (xf * rs * gains[0:1, :]).astype(BF)

    q, kv, kvT = r["q"], r["kv"], r["kvT"]
    scale = HEAD_DIM ** -0.5
    def qkv_ready():
        qkv_sp.relay_x()
        qkv_sp.relay_y()
        qkv_sp.finish()

    kv_ix = [slot() for _ in range(MICRO)]
    other = {"ctx": lax.rem(c + 1, C)}

    def project(m):
        @pl.loop(0, R // RT)
        def _(i):
            acc = dot_nn(n1[at(m * R + i * RT, RT), :], wqkv[...])
            q[m, at(i * RT, RT), :] = (acc[:, 0:HP] * scale).astype(BF)
            kv[m, at(c * R + i * RT, RT), :] = acc[:, HP:HP + KV].astype(BF)
        w = kv.at[m, at(c * R, R)]
        send(w, w, kv_ix[m], other)
        flip(m, c * R)

    def spread(w):
        if w == "o":
            for k, i in zip(range(1, NT), wo_ix):
                v = wo.at[t, own_rows]
                copy_to(v, v, i, z_to(k)).wait_recv()
            wo_sp.near()
        spreads[w].start()

    def weights_ready():
        for sp in spreads.values():
            sp.finish()

    oT, onat, oown, lse = r["oT"], r["onat"], r["oown"], r["lse"]
    lanes = lax.broadcasted_iota(jnp.int32, (RT, HP), 1)

    def head_mask(v, h, shift):
        lo = shift + h * HEAD_DIM
        return jnp.where((lanes >= lo) & (lanes < lo + HEAD_DIM), v, jnp.zeros_like(v))

    def flip(m, start):
        @pl.loop(0, R // RT)
        def _(i):
            kvT[m, :, at(start + i * RT, RT)] = kv[m, at(start + i * RT, RT), :].T

    def attend(m, i):
        kk = kv[m, :, 0:HP]
        sc = segc[m]
        sc = jnp.concatenate([sc] * (RT // 128), axis=1)
        sr = segr[m:m + 1, at(c * R + i * RT, RT)]
        qq = q[m, pl.ds(i * RT, RT), :]
        for h in range(NH):
            s = dot_nt(kk, head_mask(qq, h, 0))
            s = jnp.where(sc == sr, s, NEG)
            mx = jnp.max(s, axis=0, keepdims=True)
            e = jnp.exp(s - mx)
            tot = jnp.sum(e, axis=0, keepdims=True)
            p = (e * (1.0 / tot)).astype(BF)
            vT = kvT[m, H + h * HEAD_DIM:H + (h + 1) * HEAD_DIM, :]
            lo = VOFF + h * HEAD_DIM
            oT[m, t, lo:lo + HEAD_DIM, pl.ds(i * RT, RT)] = dot_nn(vT, p).astype(BF)
            lse[m, h, :, pl.ds(i * RT, RT)] = mx + jnp.log(tot)

    tiles = [(m, i) for m in range(MICRO) for i in range(R // RT)]
    o_ix = {n: [slot() for _ in range(NT)] for n in tiles}

    def o_part(n, k):
        return oT.at[n[0], k, pl.ds(VOFF, H), pl.ds(n[1] * RT, RT)]

    ends = NT - 1 - side

    def share_o(n):
        w = o_part(n, t)
        for k in range(1, NT):
            cp = copy_to(w, w, o_ix[n][k], z_to(k))
            if k == NT // 2:
                cp.start()
            else:
                @pl.when(jnp.abs(lax.rem(t + k, NT) - t) != NT - 1)
                def _(cp=cp):
                    cp.start()

    def wait_o(n):
        for k in range(1, NT):
            src = lax.rem(t + NT - k, NT)
            w = o_part(n, t)
            if k == NT // 2:
                copy_to(w, w, o_ix[n][k], z_to(k)).wait_recv()
            else:
                @pl.when(jnp.abs(src - t) != NT - 1)
                def _(w=w, k=k):
                    copy_to(w, w, o_ix[n][k], z_to(k)).wait_recv()

        @pl.when(inner)
        def _():
            far = o_part(n, lax.rem(t + NT // 2, NT))
            copy_to(far, far, o_ix[n][0], {"tp": side}).start()

        @pl.when(outer)
        def _():
            w = o_part(n, t)
            copy_to(w, w, o_ix[n][0], {"tp": side}).wait_recv()

    def close_o(n):
        w = o_part(n, t)
        for k in range(1, NT):
            cp = copy_to(w, w, o_ix[n][k], z_to(k))
            if k == NT // 2:
                cp.wait_send()
            else:
                @pl.when(jnp.abs(lax.rem(t + k, NT) - t) != NT - 1)
                def _(cp=cp):
                    cp.wait_send()

        @pl.when(inner)
        def _():
            copy_to(w, w, o_ix[n][0], {"tp": side}).wait_send()

    def attend_tile(m, i):
        if i == 0:
            w = kv.at[m, at(c * R, R)]
            copy_to(w, w, kv_ix[m], other).wait_recv()
            flip(m, lax.rem(c + 1, C) * R)
        attend(m, i)
        share_o((m, i))

    snd, rc1, rc2 = r["snd"], r["rc1"], r["rc2"]

    class Sum:
        def __init__(self, a, b, d):
            self.a, self.b, self.d = a, b, d
            self.ix = [[slot() for _ in range(3)] for _ in range(NCH)]

        def part(self, ref, j):
            a = self.a if ref is snd else self.b if ref is rc1 else self.d
            return ref.at[a, pl.ds(j * CH, CH)]

        def begin(self, j):
            @pl.when(outer)
            def _():
                copy_to(self.part(snd, j), self.part(rc1, j), self.ix[j][0], {"tp": side}).start()

        def step_a(self, j):
            @pl.when(inner)
            def _():
                copy_to(self.part(snd, j), self.part(rc1, j), self.ix[j][0], {"tp": side}).wait_recv()
                s = pl.ds(j * CH, CH)
                snd[self.a, s, :] = (snd[self.a, s, :].astype(F32) + rc1[self.b, s, :].astype(F32)).astype(BF)
                copy_to(self.part(snd, j), self.part(rc2, j), self.ix[j][1], {"tp": mid}).start()

        def step_b(self, j):
            @pl.when(inner)
            def _():
                copy_to(self.part(snd, j), self.part(rc2, j), self.ix[j][1], {"tp": mid}).wait_recv()
                s = pl.ds(j * CH, CH)
                rc2[self.d, s, :] = (snd[self.a, s, :].astype(F32) + rc2[self.d, s, :].astype(F32)).astype(BF)
                copy_to(self.part(rc2, j), self.part(rc2, j), self.ix[j][2], {"tp": side}).start()

        def wait(self, *which):
            @pl.when(outer)
            def _():
                for j in which or range(NCH):
                    copy_to(self.part(rc2, j), self.part(rc2, j), self.ix[j][2], {"tp": side}).wait_recv()

        def close(self):
            @pl.when(outer)
            def _():
                for j in range(NCH):
                    copy_to(self.part(snd, j), self.part(rc1, j), self.ix[j][0], {"tp": side}).wait_send()

            @pl.when(inner)
            def _():
                for j in range(NCH):
                    copy_to(self.part(snd, j), self.part(rc2, j), self.ix[j][1], {"tp": mid}).wait_send()
                    copy_to(self.part(rc2, j), self.part(rc2, j), self.ix[j][2], {"tp": side}).wait_send()

    dn2_sum = [Sum(m, m, m) for m in range(MICRO)]
    ffn_sum = [Sum(MICRO + m, MICRO + m, MICRO + m) for m in range(MICRO)]
    dn1_sum = [Sum(m, m, 2 * MICRO + m) for m in range(MICRO)]
    sums = {"n": dn2_sum, "f": ffn_sum, "d": dn1_sum}

    y1, n2, big = r["y1"], r["n2"], r["big"]
    hid, dg, du = big.at[0], big.at[1], big.at[2]

    def flip_o(m, i):
        for k in range(NT):
            onat[k] = oT[m, k, :, pl.ds(i * RT, RT)].T
        oown[m, pl.ds(i * RT, RT), :] = onat[t]

    def ffn_rows(m, i):
        rr = pl.ds(i * RT, RT)
        gr = pl.ds(m * R + i * RT, RT)
        acc = tok[m, rr, :].astype(F32)
        att = dot_nt(onat[0], wo[0])
        for k in range(1, NT):
            att = att + dot_nt(onat[k], wo[k])
        acc = acc + att
        y1[m, rr, :] = acc
        rs = lax.rsqrt(jnp.mean(acc * acc, -1, keepdims=True) + EPS)
        n2v = (acc * rs * gains[1:2, :]).astype(BF)
        n2[gr, :] = n2v
        g = dot_nn(n2v, wg[...])
        u = dot_nn(n2v, wu[...])
        th = jnp.tanh(GELU_K * (g + GELU_A * g * g * g))
        half = 0.5 * (1.0 + th)
        gl = g * half
        hv = (gl * u).astype(BF)
        hid[gr, :] = hv
        dh = dot_nn(cot[gr, :], wd[...])
        dgl = half + 0.5 * g * (1.0 - th * th) * (GELU_K * (1.0 + 3.0 * GELU_A * g * g))
        dgv = (dh * u * dgl).astype(BF)
        duv = (dh * gl).astype(BF)
        dg[gr, :] = dgv
        du[gr, :] = duv
        d2 = dot_nt(dgv, wg[...]) + dot_nt(duv, wu[...])
        snd[m, rr, :] = d2.astype(BF)
        gacc[1:2, :] += jnp.sum(d2 * (acc * rs), axis=0, keepdims=True)
        for j in range(RT // CH):
            dn2_sum[m].begin(i * (RT // CH) + j)
        snd[MICRO + m, rr, :] = dot_nt(hv, wd[...]).astype(BF)

    def feed(m, i):
        flip_o(m, i)
        if (m, i) == fed[0]:
            load_cot.wait()
        ffn_rows(m, i)

    def ffn_begin(m):
        for j in range(NCH):
            ffn_sum[m].begin(j)

    gq, gg, gu, gd = r["gq"], r["gg"], r["gu"], r["gd"]
    go = gd.at[:, pl.ds(0, HP)]

    def grad(dst, left, right):
        @pl.loop(0, D // RT)
        def _(i):
            dst[at(i * RT, RT), :] = dot_tn(left[:, at(i * RT, RT)], right[...])

    class Reduce:
        def __init__(self, g, recv, stage, parts, out):
            self.g, self.recv, self.stage, self.parts, self.out = g, recv, stage, parts, out
            self.px = [slot() for _ in range(Y)]
            self.ix = [slot() for _ in offsets]

        def pair(self):
            for n in range(Y):
                self.pair_copy(n).start()

        def pair_copy(self, n):
            src = self.g.at[at((2 * n + 1 - core) * C * SR, C * SR)]
            return copy_to(src, self.recv.at[pl.ds(n * C * SR, C * SR)], self.px[n], partner)

        def square(self):
            for n in range(Y):
                rows = at((2 * n + core) * C * SR, C * SR)
                self.pair_copy(n).wait()
                tot = self.g[rows, :] + self.recv[n * C * SR:(n + 1) * C * SR, :]
                self.recv[n * C * SR:(n + 1) * C * SR, :] = tot
                self.stage[n * C * SR:(n + 1) * C * SR, :] = tot.astype(BF)
            for n, off in enumerate(offsets):
                pf, pc = square(off)
                src = self.stage.at[at(((pf // 2) * C + pc) * SR, SR)]
                send(src, self.parts.at[n], self.ix[n], dev_sq(off))

        def finish(self):
            tot = self.recv[at((y * C + c) * SR, SR), :]
            for n, off in enumerate(offsets):
                copy_to(self.parts.at[n], self.parts.at[n], self.ix[n], dev_sq(off)).wait_recv()
            for n in range(len(offsets)):
                tot = tot + self.parts[n].astype(F32)
            self.out(tot)

    acc = {"q": gq, "o": go, "g": gg, "u": gu, "d": gd}
    def whole(name):
        def put(tot):
            r[name][...] = tot
        return put

    def split_qkv(tot):
        r["out_q"][...] = tot[:, 0:H]
        r["out_k"][...] = tot[:, HP:HP + H]
        r["out_v"][...] = pltpu.roll(tot[:, W - HP:W], HP - VOFF, 1)[:, 0:H]

    def shift_o(tot):
        r["out_o"][...] = pltpu.roll(tot, HP - VOFF, 1)[:, 0:H]

    puts = {"d": whole("out_d"), "g": whole("out_g"), "u": whole("out_u"), "q": split_qkv, "o": shift_o}
    reds = {k: Reduce(acc[k], r["rv_" + k], r["st_" + k], r["pt_" + k], puts[k]) for k in ("d", "g", "u", "q", "o")}
    def grad_ffn(w):
        if w == "d":
            grad(gd, cot, hid)
        elif w == "g":
            grad(gg, n2, dg)
        else:
            grad(gu, n2, du)
        reds[w].pair()

    ig = r["dy"]
    qm_all, dom_all = r["qm_all"], r["dom_all"]
    delta, dqT, dkv, dkv_in = r["delta"], r["dqT"], r["dkv"], r["dkv_in"]
    dqkv = n2.at[:, pl.ds(0, HP + KV)]

    def back_norm(m):
        dn2_sum[m].wait()

        @pl.loop(0, R // RT)
        def _(i):
            rr = at(i * RT, RT)
            yv = y1[m, rr, :]
            d2 = rc2[m, rr, :].astype(F32)
            tv = lax.rsqrt(jnp.mean(yv * yv, -1, keepdims=True) + EPS)
            e2 = gains[1:2, :] * d2
            dot = jnp.mean(yv * e2, -1, keepdims=True)
            dy = cot[at(m * R + i * RT, RT), :].astype(F32) + tv * e2 - yv * (tv * tv * tv * dot)
            ig[m, rr, :] = dy
            ar = dy.astype(BF)
            dov = dot_nn(ar, wo[t]).astype(BF)
            doT = dov.T
            for h in range(NH):
                lo = VOFF + h * HEAD_DIM
                prod = doT[lo:lo + HEAD_DIM, :].astype(F32) * oT[m, t, lo:lo + HEAD_DIM, rr].astype(F32)
                delta[h, :, rr] = jnp.sum(prod, axis=0, keepdims=True)
                dom_all[at(h * R + i * RT, RT), :] = head_mask(dov, h, VOFF)
                qm_all[at(h * R + i * RT, RT), :] = head_mask(q[m, rr, :], h, 0)

    def back_half(m, key0, first):
        @pl.loop(0, R // RT)
        def _(i):
            sc = segc[m, at(key0, R), :]
            sc = jnp.concatenate([sc] * (RT // 128), axis=1)
            sr = segr[m:m + 1, at(c * R + i * RT, RT)]
            for h in range(NH):
                qs = at(h * R + i * RT, RT)
                s = dot_nt(kv[m, at(key0, R), 0:HP], qm_all[qs, :])
                s = jnp.where(sc == sr, s, NEG)
                p = jnp.exp(s - lse[m, h, :, at(i * RT, RT)])
                dp = dot_nt(kv[m, at(key0, R), KV - HP:KV], dom_all[qs, :])
                cs = at(i * RT, RT)
                big[h, pl.ds(R, R), cs] = p.astype(BF)
                big[h, pl.ds(0, R), cs] = (p * (dp - delta[h, :, at(i * RT, RT)])).astype(BF)

        @pl.loop(0, R // RT)
        def _(i):
            rr = at(i * RT, RT)
            r2 = pl.ds(pl.multiple_of(R + i * RT, RT), RT)
            dk = dot_nn(big[0, rr, :], qm_all[pl.ds(0, R), :])
            dv = dot_nn(big[0, r2, :], dom_all[pl.ds(0, R), :])
            for h in range(1, NH):
                dk = dk + dot_nn(big[h, rr, :], qm_all[pl.ds(h * R, R), :])
                dv = dv + dot_nn(big[h, r2, :], dom_all[pl.ds(h * R, R), :])
            dkv[rr, 0:128] = dk[:, 0:128]
            dkv[rr, 128:256] = dk[:, 128:256] + dv[:, 0:128]
            dkv[rr, 256:384] = dv[:, 128:256]
        for h in range(NH):
            hs = pl.ds(h * HEAD_DIM, HEAD_DIM)
            part = dot_nn(kvT[m, hs, at(key0, R)], big[h, pl.ds(0, R), :])
            if first:
                dqT[hs, :] = part
            else:
                dqT[hs, :] = dqT[hs, :] + part

    dkv_ix = [slot() for _ in range(MICRO)]
    dkv_out, dkv_own = r["dkv_out"], r["dkv_own"]

    def back_peer(m):
        back_half(m, lax.rem(c + 1, C) * R, True)
        dkv_out[m] = dkv[...].astype(BF)
        send(dkv_out.at[m], dkv_in.at[m], dkv_ix[m], other)

    def back_own(m):
        back_half(m, c * R, False)
        dqkv[pl.ds(m * R, R), 0:HP] = jnp.zeros((R, HP), BF)
        dqkv[pl.ds(m * R, R), 0:H] = (dqT[...] * scale).T.astype(BF)
        dkv_own[m] = dkv[...]

    def join(m):
        copy_to(dkv_out.at[m], dkv_in.at[m], dkv_ix[m], other).wait_recv()
        dn2_sum[m].close()

        for i in range(R // RT):
            rr = pl.ds(i * RT, RT)
            gr = pl.ds(m * R + i * RT, RT)
            dqkv[gr, HP:HP + KV] = (dkv_own[m, rr, :] + dkv_in[m, rr, :].astype(F32)).astype(BF)
            d1 = dot_nt(dqkv[gr, :], wqkv[...])
            snd[m, rr, :] = d1.astype(BF)
            xv = tok[m, rr, :].astype(F32)
            rs = lax.rsqrt(jnp.mean(xv * xv, -1, keepdims=True) + EPS)
            gacc[0:1, :] += jnp.sum(d1 * (xv * rs), axis=0, keepdims=True)
            for j in range(RT // CH):
                dn1_sum[m].begin(i * (RT // CH) + j)

    def grad_qkv():
        grad(gq, n1, dqkv)
        reds["q"].pair()

    def grad_out():
        @pl.loop(0, D // RT)
        def _(i):
            cs = at(i * RT, RT)
            acc = dot_tn(ig[0, :, cs].astype(BF), oown[0])
            for m in range(1, MICRO):
                acc = acc + dot_tn(ig[m, :, cs].astype(BF), oown[m])
            go[cs, :] = acc
        reds["o"].pair()

    gz, gz_ix = r["gz"], [slot() for _ in range(NT)]
    gin, gpart = r["gin"], r["gpart"]
    gain_ix = [slot() for _ in group]

    def gain_z():
        for k in range(1, NT):
            send(gacc, gz.at[k], gz_ix[k], z_to(k))

    def gain_group():
        for k in range(1, NT):
            copy_to(gacc, gz.at[k], gz_ix[k], z_to(k)).wait_recv()
        tot = gacc[...]
        for k in range(1, NT):
            tot = tot + gz[k]
        gpart[...] = tot
        for n, off in enumerate(group):
            send(gpart, gin.at[n], gain_ix[n], dev_group(off))

    def gain_final():
        for n, off in enumerate(group):
            copy_to(gpart, gin.at[n], gain_ix[n], dev_group(off)).wait_recv()
        tot = gpart[...]
        for n in range(len(group)):
            tot = tot + gin[n]
        tot = lax.dot_general(
            tot, place.astype(F32), (((1,), (1,)), ((), ())), precision=lax.Precision.HIGHEST,
            preferred_element_type=F32)
        r["out_ga"][...] = tot[0:1, :]
        r["out_gf"][...] = tot[1:2, :]

    out = r["outv"]
    stores = []

    def store(src, dst):
        cp = pltpu.make_async_copy(src, dst, local.at[2 + len(stores)])
        cp.start()
        stores.append(cp)

    def output(m, j):
        ffn_sum[m].wait(j)
        rr = pl.ds(j * CH, CH)
        out[m, rr, :] = (y1[m, rr, :] + rc2[MICRO + m, rr, :].astype(F32)).astype(BF)
        store(out.at[m, rr], r["out"].at[m, 0, rr])

    def final(m, j):
        dn1_sum[m].wait(j)
        rr = pl.ds(j * CH, CH)
        xv = tok[m, rr, :].astype(F32)
        d1 = rc2[2 * MICRO + m, rr, :].astype(F32)
        tv = lax.rsqrt(jnp.mean(xv * xv, -1, keepdims=True) + EPS)
        e1 = gains[0:1, :] * d1
        dot = jnp.mean(xv * e1, -1, keepdims=True)
        ig[m, rr, :] = ig[m, rr, :] + tv * e1 - xv * (tv * tv * tv * dot)
        store(ig.at[m, rr], r["ig"].at[m, 0, rr])

    fed = [step[1:] for step in ORDER if step[0] == "F"]
    acts = {
        "prep": prepare, "qR": qkv_ready, "wF": weights_ready, "P": project, "wS": spread,
        "wX": lambda w: spreads[w].relay_x(), "wY": lambda w: spreads[w].relay_y(), "AT": attend_tile,
        "O": lambda m, i: wait_o((m, i)), "F": feed, "fB": ffn_begin,
        "A": lambda k, m, j: sums[k][m].step_a(j), "B": lambda k, m, j: sums[k][m].step_b(j),
        "G": grad_ffn, "Gq": grad_qkv, "Go": grad_out, "SQ": lambda w: reds[w].square(),
        "SF": lambda w: reds[w].finish(), "BN": back_norm, "PE": back_peer, "OW": back_own, "J": join,
        "OUT": output, "FIN": final, "GZ": gain_z, "GR": gain_group, "GF": gain_final,
    }
    for step in ORDER:
        acts[step[0]](*step[1:])
    for cp in stores:
        cp.wait()
    for n in tiles:
        close_o(n)

    for cp in sends:
        cp.wait_send()
    for s in ffn_sum + dn1_sum:
        s.close()
    assert counter[0] <= ssem.shape[0]


def fused_shards(dims, tokens, segments, cotangent, query_weight, key_weight, value_weight, out_weight,
                 gate_weight, up_weight, down_weight, attn_gain, ffn_gain):
    R, D, H, FF, C, NF, NT, MICRO = dims
    L = C * R
    SR = D // (NF * C)
    NH = H // HEAD_DIM
    HP, KV, Y = 256, 2 * H, NF // 2
    HALF = Y * C * SR
    NO = Y * C - 1
    NG = NF * C - 1
    W = HP + KV
    ins = [
        ("tok_in", tokens.reshape(MICRO, R, D)),
        ("segr", segments),
        ("cot_in", cotangent.reshape(MICRO * R, D)),
        ("wq_in", query_weight),
        ("wk_in", key_weight),
        ("wv_in", value_weight),
        ("wo_in", out_weight),
        ("wg_in", gate_weight),
        ("wu_in", up_weight),
        ("wd_in", down_weight),
        ("gain_a", attn_gain[None]),
        ("gain_f", ffn_gain[None]),
    ]
    far = ("tok_in", "cot_in", "out", "ig")
    outs = [
        ("out", (MICRO, 1, R, D), BF),
        ("ig", (MICRO, 1, R, D), F32),
        ("out_q", (SR, H), F32),
        ("out_k", (SR, H), F32),
        ("out_v", (SR, H), F32),
        ("out_o", (SR, H), F32),
        ("out_g", (SR, FF), F32),
        ("out_u", (SR, FF), F32),
        ("out_d", (SR, FF), F32),
        ("out_ga", (1, SR), F32),
        ("out_gf", (1, SR), F32),
    ]
    v = pltpu.VMEM
    scratch = [
        ("tok", v((MICRO, R, D), BF)), ("cot", v((MICRO * R, D), BF)), ("dy", v((MICRO, R, D), F32)),
        ("outv", v((MICRO, R, D), BF)), ("gz", v((NT, 8, D), F32)), ("gpart", v((8, D), F32)),
        ("lsem", pltpu.SemaphoreType.DMA((24,))),
        ("gmine", v((8, D), F32)), ("gall", v((NG, 8, D), F32)), ("gains", v((8, D), F32)),
        ("gacc", v((8, D), F32)), ("gin", v((NG, 8, D), F32)),
        ("wqkv", v((D, W), BF)), ("wo", v((NT, D, HP), BF)),
        ("wg", v((D, FF), BF)), ("wu", v((D, FF), BF)), ("wd", v((D, FF), BF)),
        ("segc", v((MICRO, L, 128), jnp.int32)),
        ("n1", v((MICRO * R, D), BF)), ("q", v((MICRO, R, HP), BF)),
        ("kv", v((MICRO, L, KV), BF)), ("kvT", v((MICRO, KV, L), BF)),
        ("oT", v((MICRO, NT, HP, R), BF)), ("onat", v((NT, 256, HP), BF)), ("oown", v((MICRO, R, HP), BF)),
        ("lse", v((MICRO, NH, 1, R), F32)),
        ("snd", v((2 * MICRO, R, D), BF)), ("rc1", v((2 * MICRO, R, D), BF)), ("rc2", v((3 * MICRO, R, D), BF)),
        ("y1", v((MICRO, R, D), F32)), ("n2", v((MICRO * R, D), BF)),
        ("big", v((3, MICRO * R, FF), BF)),
        ("qm_all", v((NH * R, HP), BF)), ("dom_all", v((NH * R, HP), BF)),
        ("delta", v((NH, 1, R), F32)), ("dqT", v((H, R), F32)),
        ("dkv", v((R, KV), F32)), ("dkv_own", v((MICRO, R, KV), F32)),
        ("dkv_in", v((MICRO, R, KV), BF)), ("dkv_out", v((MICRO, R, KV), BF)),
    ]
    for k, cols in (("q", W), ("o", HP), ("g", FF), ("u", FF), ("d", FF)):
        if k != "o":
            scratch += [("g" + k, v((D, cols), F32))]
        scratch += [("rv_" + k, v((HALF, cols), F32)),
                    ("st_" + k, v((HALF, cols), BF)), ("pt_" + k, v((NO, SR, cols), BF))]
    nsem = 256
    scratch += [("ssem", pltpu.SemaphoreType.DMA((nsem,))), ("rsem", pltpu.SemaphoreType.DMA((nsem,)))]
    names = [n for n, _ in ins] + [n for n, _, _ in outs] + [n for n, _ in scratch]
    def spec(name):
        return pl.BlockSpec(memory_space=pl.ANY if name in far else pltpu.VMEM)

    res = pl.pallas_call(
        functools.partial(layer_kernel, dims, names),
        out_shape=[jax.ShapeDtypeStruct(s, d) for _, s, d in outs],
        in_specs=[spec(n) for n, _ in ins],
        out_specs=[spec(n) for n, _, _ in outs],
        scratch_shapes=[s for _, s in scratch],
        compiler_params=pltpu.CompilerParams(
            collective_id=0, has_side_effects=True, vmem_limit_bytes=67043328),
    )(*[a for _, a in ins])
    res = settle(res)
    return tuple(res[:9]) + (res[9].reshape(SR), res[10].reshape(SR))


def settle(arrays):
    pieces = []
    for n, a in enumerate(arrays):
        if a.ndim == 4:
            pieces += [(n, (m, 0, pl.ds(k * 256, 256))) for m in range(a.shape[0]) for k in range(a.shape[2] // 256)]
        else:
            pieces.append((n, None))

    def kernel(*refs):
        k = len(arrays)
        src, dst, buf, sem = refs[:k], refs[k:2 * k], refs[2 * k:3 * k], refs[3 * k:]
        pick = lambda ref, at: ref if at is None else ref.at[at]
        come = [pltpu.make_async_copy(pick(src[n], at), pick(buf[n], at), sem[0].at[i]) for i, (n, at) in enumerate(pieces)]
        go = [pltpu.make_async_copy(pick(buf[n], at), pick(dst[n], at), sem[1].at[i]) for i, (n, at) in enumerate(pieces)]
        for cp in come:
            cp.start()
        for a, b in zip(come, go):
            a.wait()
            b.start()
        for cp in go:
            cp.wait()

    hbm = pl.BlockSpec(memory_space=pl.ANY)
    return pl.pallas_call(
        kernel,
        out_shape=[jax.ShapeDtypeStruct(a.shape, a.dtype) for a in arrays],
        in_specs=[hbm] * len(arrays),
        out_specs=[hbm] * len(arrays),
        scratch_shapes=[pltpu.VMEM(a.shape, a.dtype) for a in arrays] + [pltpu.SemaphoreType.DMA((len(pieces),))] * 2,
    )(*arrays)


def fits(dims, seqs):
    R, D, H, FF, C, NF, NT, MICRO = dims
    blocks = D % (16 * NF * C) == 0 and R % 256 == 0 and D % 256 == 0
    return (C, NT, NF % 2, H, MICRO, seqs) == (2, 4, 0, 192, 2, 1) and FF == R and R <= 512 and D <= 768 and blocks


SPECS = (
    P(None, "fsdp", "ctx", None),
    P(None, "fsdp", None),
    P(None, "fsdp", "ctx", None),
) + (P(("fsdp", "ctx"), "tp"),) * 7 + (P(("fsdp", "ctx")),) * 2
OUT_SPECS = (P(None, "fsdp", "ctx", None),) * 2 + (P(("fsdp", "ctx"), "tp"),) * 7 + (P(("fsdp", "ctx")),) * 2


def solution(mesh):
    nf, nc, nt = mesh.shape["fsdp"], mesh.shape["ctx"], mesh.shape["tp"]

    def chosen(*args):
        tokens, weight, ffw = args[0], args[3], args[7]
        micro, seqs, rows, width = tokens.shape
        dims = (rows, width, weight.shape[1], ffw.shape[1], nc, nf, nt, micro)
        return fused_shards(dims, *args) if fits(dims, seqs) else shards(*args)

    return jax.shard_map(chosen, mesh=mesh, in_specs=SPECS, out_specs=OUT_SPECS, check_vma=False)
```

```python
import functools

import jax
import jax.numpy as jnp
from jax import lax
from jax.experimental import pallas as pl
from jax.experimental.pallas import tpu as pltpu
from jax.sharding import PartitionSpec as P

HEAD_DIM = 64


EPS = 1e-06


def gather_weights(
    query_weight,
    key_weight,
    value_weight,
    out_weight,
    gate_weight,
    up_weight,
    down_weight,
    attn_gain,
    ffn_gain,
):
    return (
        lax.all_gather(query_weight, ("fsdp", "ctx"), axis=0, tiled=True),
        lax.all_gather(key_weight, ("fsdp", "ctx"), axis=0, tiled=True),
        lax.all_gather(value_weight, ("fsdp", "ctx"), axis=0, tiled=True),
        lax.all_gather(out_weight, ("fsdp", "ctx"), axis=0, tiled=True),
        lax.all_gather(gate_weight, ("fsdp", "ctx"), axis=0, tiled=True),
        lax.all_gather(up_weight, ("fsdp", "ctx"), axis=0, tiled=True),
        lax.all_gather(down_weight, ("fsdp", "ctx"), axis=0, tiled=True),
        lax.all_gather(attn_gain, ("fsdp", "ctx"), axis=0, tiled=True),
        lax.all_gather(ffn_gain, ("fsdp", "ctx"), axis=0, tiled=True),
    )


def tensor_sum(partial_value):
    return lax.psum(partial_value, "tp")


def normalize(values, gain_vec):
    return values * lax.rsqrt(jnp.mean(values * values, -1, keepdims=True) + EPS) * gain_vec


def gelu_mix(gate_act, up_act):
    return jax.nn.gelu(gate_act, approximate=True) * up_act


def contract_last(left_op, right_op):
    return lax.dot_general(
        left_op, right_op, (((1,), (1,)), ((), ())), preferred_element_type=jnp.float32
    )


def contract_first(left_op, right_op):
    return lax.dot_general(
        left_op, right_op, (((0,), (0,)), ((), ())), preferred_element_type=jnp.float32
    )


def masked_scores(queries, key_whole, query_seg, seg_all, head_count):
    local_rows = queries.shape[0]
    query_heads = queries.reshape(local_rows, head_count, HEAD_DIM)
    key_heads = key_whole.reshape(key_whole.shape[0], head_count, HEAD_DIM)
    products = jnp.einsum(
        "qhd,khd->hqk", query_heads, key_heads, preferred_element_type=jnp.float32
    ) * HEAD_DIM ** (-0.5)
    same_doc = query_seg[:, None] == seg_all[None, :]
    return jnp.where(same_doc[None], products, -1e30)


def forward_pass(inputs, seg_all, gathered, ctx_pos):
    w_query, w_key, w_value, w_out, w_gate, w_up, w_down, gain_attn, gain_ffn = gathered
    head_count = w_query.shape[1] // HEAD_DIM
    local_rows = inputs.shape[0]
    query_seg = lax.dynamic_slice_in_dim(seg_all, ctx_pos * local_rows, local_rows)
    inputs_f = inputs.astype(jnp.float32)
    normed_one = normalize(inputs_f, gain_attn.astype(jnp.float32)).astype(jnp.bfloat16)
    queries = jnp.dot(normed_one, w_query, preferred_element_type=jnp.float32).astype(jnp.bfloat16)
    key_local = jnp.dot(normed_one, w_key, preferred_element_type=jnp.float32).astype(jnp.bfloat16)
    value_local = jnp.dot(normed_one, w_value, preferred_element_type=jnp.float32).astype(
        jnp.bfloat16
    )
    key_whole, value_whole = (
        lax.all_gather(key_local, "ctx", axis=0, tiled=True),
        lax.all_gather(value_local, "ctx", axis=0, tiled=True),
    )
    scores = masked_scores(queries, key_whole, query_seg, seg_all, head_count)
    row_max = jnp.max(scores, -1, keepdims=True)
    row_total = jnp.sum(jnp.exp(scores - row_max), -1, keepdims=True)
    log_total = row_max + jnp.log(row_total)
    probs_low = jnp.exp(scores - log_total).astype(jnp.bfloat16)
    value_heads = value_whole.reshape(value_whole.shape[0], head_count, HEAD_DIM)
    attn_mixed = jnp.einsum(
        "hqk,khd->qhd", probs_low, value_heads, preferred_element_type=jnp.float32
    )
    attn_mixed = attn_mixed.reshape(local_rows, head_count * HEAD_DIM).astype(jnp.bfloat16)
    attn_partial = contract_last(attn_mixed, w_out)
    residual = inputs_f + tensor_sum(attn_partial)
    normed_two = normalize(residual, gain_ffn.astype(jnp.float32)).astype(jnp.bfloat16)
    gate_act = jnp.dot(normed_two, w_gate, preferred_element_type=jnp.float32)
    up_act = jnp.dot(normed_two, w_up, preferred_element_type=jnp.float32)
    hidden = gelu_mix(gate_act, up_act).astype(jnp.bfloat16)
    ffn_partial = contract_last(hidden, w_down)
    result = (residual + tensor_sum(ffn_partial)).astype(jnp.bfloat16)
    stored = (
        inputs_f,
        normed_one,
        queries,
        key_whole,
        value_whole,
        log_total,
        attn_mixed,
        residual,
        normed_two,
        gate_act,
        up_act,
        hidden,
        query_seg,
    )
    return (result, stored)


def backward_pass(cot_rows, stored, gathered, seg_all, ctx_pos):
    w_query, w_key, w_value, w_out, w_gate, w_up, w_down, gain_attn, gain_ffn = gathered
    (
        inputs_f,
        normed_one,
        queries,
        key_whole,
        value_whole,
        log_total,
        attn_mixed,
        residual,
        normed_two,
        gate_act,
        up_act,
        hidden,
        query_seg,
    ) = stored
    head_count = w_query.shape[1] // HEAD_DIM
    local_rows = queries.shape[0]
    seq_rows = key_whole.shape[0]
    scale = HEAD_DIM ** (-0.5)
    dout = cot_rows.astype(jnp.float32)
    dout_low = dout.astype(jnp.bfloat16)
    grad_down = contract_first(dout_low, hidden)
    dhidden = jnp.dot(dout_low, w_down, preferred_element_type=jnp.float32)
    mixed_unused, mix_back = jax.vjp(gelu_mix, gate_act, up_act)
    dgate, dup = mix_back(dhidden)
    dgate_low = dgate.astype(jnp.bfloat16)
    dup_low = dup.astype(jnp.bfloat16)
    grad_gate = contract_first(normed_two, dgate_low)
    grad_up = contract_first(normed_two, dup_low)
    dn2_partial = contract_last(dgate_low, w_gate) + contract_last(dup_low, w_up)
    norm_unused, norm_back = jax.vjp(normalize, residual, gain_ffn.astype(jnp.float32))
    dresid_norm, grad_gain_ffn = norm_back(tensor_sum(dn2_partial))
    dresidual = dout + dresid_norm
    dres_low = dresidual.astype(jnp.bfloat16)
    grad_out = contract_first(dres_low, attn_mixed)
    dmixed = jnp.dot(dres_low, w_out, preferred_element_type=jnp.float32).astype(jnp.bfloat16)
    dmixed_heads = dmixed.reshape(local_rows, head_count, HEAD_DIM)
    scores = masked_scores(queries, key_whole, query_seg, seg_all, head_count)
    prob_full = jnp.exp(scores - log_total)
    key_heads = key_whole.reshape(seq_rows, head_count, HEAD_DIM)
    value_heads = value_whole.reshape(seq_rows, head_count, HEAD_DIM)
    dprobs = jnp.einsum(
        "qhd,khd->hqk", dmixed_heads, value_heads, preferred_element_type=jnp.float32
    )
    row_delta = jnp.sum(prob_full * dprobs, -1, keepdims=True)
    dscores = (prob_full * (dprobs - row_delta)).astype(jnp.bfloat16)
    dquery = (
        jnp.einsum("hqk,khd->qhd", dscores, key_heads, preferred_element_type=jnp.float32) * scale
    )
    query_all, dmixed_all = (
        lax.all_gather(queries, "ctx", axis=0, tiled=True),
        lax.all_gather(dmixed, "ctx", axis=0, tiled=True),
    )
    log_all, delta_all = (
        lax.all_gather(log_total, "ctx", axis=1, tiled=True),
        lax.all_gather(row_delta, "ctx", axis=1, tiled=True),
    )
    start = ctx_pos * local_rows
    key_own = lax.dynamic_slice_in_dim(key_whole, start, local_rows)
    value_own = lax.dynamic_slice_in_dim(value_whole, start, local_rows).reshape(
        local_rows, head_count, HEAD_DIM
    )
    scores_own = masked_scores(query_all, key_own, seg_all, query_seg, head_count)
    prob_own = jnp.exp(scores_own - log_all)
    dmixed_all_heads = dmixed_all.reshape(seq_rows, head_count, HEAD_DIM)
    query_all_heads = query_all.reshape(seq_rows, head_count, HEAD_DIM)
    dprobs_own = jnp.einsum(
        "qhd,khd->hqk", dmixed_all_heads, value_own, preferred_element_type=jnp.float32
    )
    dscores_own = (prob_own * (dprobs_own - delta_all)).astype(jnp.bfloat16)
    dkey_local = (
        jnp.einsum("hqk,qhd->khd", dscores_own, query_all_heads, preferred_element_type=jnp.float32)
        * scale
    ).reshape(local_rows, head_count * HEAD_DIM)
    dvalue_local = jnp.einsum(
        "hqk,qhd->khd",
        prob_own.astype(jnp.bfloat16),
        dmixed_all_heads,
        preferred_element_type=jnp.float32,
    ).reshape(local_rows, head_count * HEAD_DIM)
    dquery_low = dquery.reshape(local_rows, head_count * HEAD_DIM).astype(jnp.bfloat16)
    dkey_low = dkey_local.astype(jnp.bfloat16)
    dvalue_low = dvalue_local.astype(jnp.bfloat16)
    grad_query = contract_first(normed_one, dquery_low)
    grad_key = contract_first(normed_one, dkey_low)
    grad_value = contract_first(normed_one, dvalue_low)
    dn1_partial = (
        contract_last(dquery_low, w_query)
        + contract_last(dkey_low, w_key)
        + contract_last(dvalue_low, w_value)
    )
    norm_unused_two, norm_back_two = jax.vjp(normalize, inputs_f, gain_attn.astype(jnp.float32))
    dinput_norm, grad_gain_attn = norm_back_two(tensor_sum(dn1_partial))
    input_grad = dresidual + dinput_norm
    grad_terms = (
        grad_query,
        grad_key,
        grad_value,
        grad_out,
        grad_gate,
        grad_up,
        grad_down,
        grad_gain_attn,
        grad_gain_ffn,
    )
    return (input_grad, grad_terms)


def shards(
    tokens,
    segments,
    cotangent,
    query_weight,
    key_weight,
    value_weight,
    out_weight,
    gate_weight,
    up_weight,
    down_weight,
    attn_gain,
    ffn_gain,
):
    ctx_pos = lax.axis_index("ctx")
    results = []
    input_grads = []
    total_grads = None
    for micro_step in range(tokens.shape[0]):
        seg_all = segments[micro_step, 0]
        gathered = gather_weights(
            query_weight,
            key_weight,
            value_weight,
            out_weight,
            gate_weight,
            up_weight,
            down_weight,
            attn_gain,
            ffn_gain,
        )
        result, stored = forward_pass(tokens[micro_step, 0], seg_all, gathered, ctx_pos)
        gathered = gather_weights(
            query_weight,
            key_weight,
            value_weight,
            out_weight,
            gate_weight,
            up_weight,
            down_weight,
            attn_gain,
            ffn_gain,
        )
        input_grad, grad_terms = backward_pass(
            cotangent[micro_step, 0], stored, gathered, seg_all, ctx_pos
        )
        results.append(result)
        input_grads.append(input_grad)
        total_grads = (
            grad_terms if total_grads is None else jax.tree.map(jnp.add, total_grads, grad_terms)
        )
    gain_attn_total = total_grads[7]
    gain_ffn_total = total_grads[8]
    owned = (
        lax.psum_scatter(total_grads[0], ("fsdp", "ctx"), scatter_dimension=0, tiled=True),
        lax.psum_scatter(total_grads[1], ("fsdp", "ctx"), scatter_dimension=0, tiled=True),
        lax.psum_scatter(total_grads[2], ("fsdp", "ctx"), scatter_dimension=0, tiled=True),
        lax.psum_scatter(total_grads[3], ("fsdp", "ctx"), scatter_dimension=0, tiled=True),
        lax.psum_scatter(total_grads[4], ("fsdp", "ctx"), scatter_dimension=0, tiled=True),
        lax.psum_scatter(total_grads[5], ("fsdp", "ctx"), scatter_dimension=0, tiled=True),
        lax.psum_scatter(total_grads[6], ("fsdp", "ctx"), scatter_dimension=0, tiled=True),
        lax.psum_scatter(gain_attn_total, ("fsdp", "ctx"), scatter_dimension=0, tiled=True),
        lax.psum_scatter(gain_ffn_total, ("fsdp", "ctx"), scatter_dimension=0, tiled=True),
    )
    output = jnp.stack(results)[:, None]
    input_grad_all = jnp.stack(input_grads)[:, None]
    return (
        output,
        input_grad_all,
        owned[0],
        owned[1],
        owned[2],
        owned[3],
        owned[4],
        owned[5],
        owned[6],
        owned[7],
        owned[8],
    )


NEG = -1e30
MESH = pl.DeviceIdType.MESH
BF = jnp.bfloat16
F32 = jnp.float32
GELU_K = 0.7978845608028654
GELU_A = 0.044715
ORDER = (
    ("prep",), ("qR",), ("wX", "g0"), ("P", 0), ("wX", "u0"), ("wX", "d0"), ("wS", "d1"), ("wS", "o"), ("wY", "u0"),
    ("P", 1), ("wX", "d1"), ("AT", 0, 0), ("wS", "u1"), ("wX", "o"), ("wS", "g1"), ("AT", 0, 1), ("wY", "o"),
    ("AT", 1, 0), ("wX", "u1"), ("AT", 1, 1), ("wX", "g1"), ("wY", "u1"), ("wY", "g1"), ("wY", "d0"), ("wY", "d1"),
    ("O", 0), ("wY", "g0"), ("wF",), ("F", 0), ("FP", 0), ("O", 1), ("F", 1), ("BN", 0, 0), ("G", "d"), ("BN", 0, 1),
    ("SQ", "d"), ("ON", 0, 0), ("G", "u"), ("FP", 1), ("G", "g"), ("ON", 0, 1), ("BS", 0), ("PE", 0), ("OF", 0, 0),
    ("OW", 0), ("OF", 0, 1), ("BN", 1, 0), ("BN", 1, 1), ("G", "o"), ("SF", "d"), ("J", 0), ("BS", 1), ("ON", 1, 0),
    ("PE", 1), ("ON", 1, 1), ("OW", 1), ("SQ", "o"), ("OF", 1, 0), ("X", 0, 0), ("OF", 1, 1), ("X", 0, 1), ("J", 1),
    ("SZ", "d"), ("IN", 0, 0), ("G", "q"), ("IN", 0, 1), ("SQ", "u"), ("SQ", "q"), ("IF", 0, 0), ("SQ", "g"),
    ("SF", "o"), ("X", 1, 0), ("IF", 0, 1), ("X", 1, 1), ("GZ",), ("SZ", "o"), ("IN", 1, 0), ("SF", "u"),
    ("IF", 1, 0), ("IN", 1, 1), ("SF", "q"), ("SF", "g"), ("GR",), ("GF",), ("SZ", "u"), ("IF", 1, 1), ("SZ", "g"),
)


def dot_nn(a, b):
    return lax.dot_general(a, b, (((1,), (0,)), ((), ())), preferred_element_type=F32)


def dot_nt(a, b):
    return lax.dot_general(a, b, (((1,), (1,)), ((), ())), preferred_element_type=F32)


def dot_tn(a, b):
    return lax.dot_general(a, b, (((0,), (0,)), ((), ())), preferred_element_type=F32)


def at(i, n):
    return pl.ds(pl.multiple_of(i, n), n)


def layer_kernel(dims, names, *refs):
    r = dict(zip(names, refs))
    R, D, H, FF, C, NF, NT, MICRO = dims
    L = C * R
    NH = H // HEAD_DIM
    HP = 256
    KV = 2 * H
    Y = NF // 2
    SR = D // (NF * C)
    RT = 256
    CH = 128
    UNIT = 64
    NCH = R // CH
    f = lax.axis_index("fsdp")
    c = lax.axis_index("ctx")
    t = lax.axis_index("tp")
    core = lax.rem(f, 2)
    y = f // 2
    shard = f * C + c
    partner = {"fsdp": f + 1 - 2 * core}
    ssem, rsem = r["ssem"], r["rsem"]
    counter = [0]

    def slot():
        counter[0] += 1
        return counter[0] - 1

    def copy_to(src, dst, idx, dev, sidx=None):
        return pltpu.make_async_remote_copy(
            src_ref=src, dst_ref=dst, send_sem=ssem.at[idx if sidx is None else sidx], recv_sem=rsem.at[idx],
            device_id=dev, device_id_type=MESH)

    offsets = [(dy, dc) for dy in range(Y) for dc in range(C) if (dy, dc) != (0, 0)]

    def square(off):
        dy, dc = off
        return (2 * lax.rem(y + dy, Y) + core, lax.rem(c + dc, C))

    def square_from(off):
        dy, dc = off
        return (2 * lax.rem(y + Y - dy, Y) + core, lax.rem(c + C - dc, C))

    def dev_sq(off):
        pf, pc = square(off)
        return {"fsdp": pf, "ctx": pc}

    def z_to(k):
        return {"tp": lax.rem(t + k, NT)}

    group = [(df, dc) for df in range(NF) for dc in range(C) if (df, dc) != (0, 0)]

    def dev_group(off):
        return {"fsdp": lax.rem(f + off[0], NF), "ctx": lax.rem(c + off[1], C)}

    half = t // 2
    inner = (t == 1) | (t == 2)
    outer = (t == 0) | (t == 3)
    mate = {"tp": t + 1 - 2 * lax.rem(t, 2)}
    twin_t = lax.rem(t + 2, NT)
    twin = {"tp": twin_t}
    cross = {"tp": NT - 1 - t}
    HR = R // 2
    SUB = HR // CH
    hrows = at(half * HR, HR)

    def both(do_inner, do_outer):
        pl.when(inner)(do_inner)
        pl.when(outer)(do_outer)

    local = r["lsem"]
    load_tok = pltpu.make_async_copy(r["tok_in"], r["tok"], local.at[0])
    load_cot = [
        pltpu.make_async_copy(r["cot_in"].at[m, hrows], r["cot"].at[pl.ds(m * HR, HR)], local.at[1 + m]) for m in range(MICRO)]
    load_tok.start()
    for cp in load_cot:
        cp.start()

    bar = pltpu.get_barrier_semaphore()
    for off in group:
        pl.semaphore_signal(bar, inc=1, device_id=dev_group(off), device_id_type=MESH)
    for k in range(1, NT):
        pl.semaphore_signal(bar, inc=1, device_id=z_to(k), device_id_type=MESH)
    pl.semaphore_wait(bar, len(group) + NT - 1)

    sends, weight_sends = [], []

    def send(src, dst, idx, dev, group=None):
        cp = copy_to(src, dst, idx, dev)
        cp.start()
        (sends if group is None else group).append(cp)
        return cp

    def rows_of(off):
        pf, pc = square_from(off)
        return at((pf * C + pc) * SR, SR)

    own_rows = at(shard * SR, SR)

    class Spread:
        def __init__(self, buf, view, far, group):
            self.buf, self.view, self.far, self.group = buf, view, far, group
            self.ix = {off: slot() for off in offsets}
            self.px = slot()
            self.rx = {off: slot() for off in offsets}

        def rows(self, off):
            return self.view(self.buf, rows_of(off))

        def start(self):
            w = self.view(self.buf, own_rows)
            for off in offsets:
                if self.far or 0 in off:
                    send(w, w, self.ix[off], dev_sq(off), self.group)
            send(w, w, self.px, partner, self.group)

        def relay_x(self):
            w = self.rows((0, 1))
            copy_to(w, w, self.ix[(0, 1)], partner).wait_recv()
            if not self.far:
                send(w, w, self.ix[(1, 1)], dev_sq((1, 0)), self.group)
            send(w, w, self.rx[(0, 1)], partner, self.group)

        def relay_y(self):
            for off in ((1, 0), (1, 1)):
                w = self.rows(off)
                copy_to(w, w, self.ix[off], partner).wait_recv()
                send(w, w, self.rx[off], partner, self.group)

        def finish(self):
            w = self.view(self.buf, own_rows)
            copy_to(w, w, self.px, partner).wait_recv()
            for off in offsets:
                copy_to(w, w, self.rx[off], partner).wait_recv()

    flat = lambda buf, rows: buf.at[rows]
    deep = lambda buf, rows: buf.at[:, rows]
    wqkv, wo, wg, wu, wd = r["wqkv"], r["wo"], r["wg"], r["wu"], r["wd"]
    def spot(width, shift):
        i = lax.broadcasted_iota(jnp.int32, (H, width), 0)
        j = lax.broadcasted_iota(jnp.int32, (H, width), 1)
        return (j == i + shift).astype(BF)

    W = HP + KV
    VOFF = HP - H
    gm = r["gmine"]
    cols = lax.broadcasted_iota(jnp.int32, (SR, D), 1)
    rows = lax.broadcasted_iota(jnp.int32, (SR, D), 0)
    place = (cols == rows + shard * SR).astype(BF)
    gm[...] = jnp.zeros_like(gm)
    gm[0:1, :] = dot_nn(r["gain_a"][...], place)
    gm[1:2, :] = dot_nn(r["gain_f"][...], place)
    gall = r["gall"]
    gain_cp = []
    for n, off in enumerate(group):
        gain_cp.append(send(gm, gall.at[n], slot(), dev_group(off)))

    wqkv[own_rows, :] = (dot_nn(r["wq_in"][...], spot(W, 0)) + dot_nn(r["wk_in"][...], spot(W, HP))
                         + dot_nn(r["wv_in"][...], spot(W, HP + H))).astype(BF)
    qkv_sp = Spread(wqkv, flat, True, sends)
    qkv_sp.start()
    wo[t, own_rows, :] = dot_nn(r["wo_in"][...], spot(HP, VOFF)).astype(BF)
    twin_ix = {}
    for k, buf in (("g", wg), ("u", wu), ("d", wd)):
        buf[0, own_rows, :] = r["w" + k + "_in"][...]
        twin_ix[k] = slot()
        send(buf.at[0, own_rows], buf.at[1, own_rows], twin_ix[k], twin, weight_sends)
    spreads = {k + str(n): Spread(b.at[n], flat, False, weight_sends) for n in range(2) for k, b in (("g", wg), ("u", wu), ("d", wd))}
    spreads["o"] = Spread(wo, deep, False, sends)
    for k in "gud":
        spreads[k + "0"].start()
    wo_ix = [slot() for _ in range(1, NT)]
    for k, i in zip(range(1, NT), wo_ix):
        w = wo.at[t, own_rows]
        send(w, w, i, z_to(k))
    segr, segc = r["segr"].at[:, 0], r["segc"]
    gains, gacc, oT, oX = r["gains"], r["gacc"], r["oT"], r["oX"]
    tok, cot, n1 = r["tok"], r["cot"], r["n1"]

    def prepare():
        for m in range(MICRO):
            for b in range(L // 128):
                row = segr[m:m + 1, 128 * b:128 * b + 128].astype(F32)
                segc[m, 128 * b:128 * b + 128, :] = jnp.broadcast_to(row, (128, 128)).T.astype(jnp.int32)
        for m in range(MICRO):
            oX[m, :, 0:VOFF, :] = jnp.zeros((NT, VOFF, HR), BF)
        for cp in gain_cp:
            cp.wait_recv()
        gsum = gm[...]
        for n in range(len(group)):
            gsum = gsum + gall[n]
        gains[...] = gsum
        load_tok.wait()
        for m in range(MICRO):
            norm_one(m)
        gacc[...] = jnp.zeros_like(gacc)

    def norm_one(m):
        @pl.loop(0, R // CH)
        def _(i):
            xf = tok[m, at(i * CH, CH), :].astype(F32)
            rs = lax.rsqrt(jnp.mean(xf * xf, -1, keepdims=True) + EPS)
            n1[at(m * R + i * CH, CH), :] = (xf * rs * gains[0:1, :]).astype(BF)

    q, kv, kvT = r["q"], r["kv"], r["kvT"]
    scale = HEAD_DIM ** -0.5
    def qkv_ready():
        qkv_sp.relay_x()
        qkv_sp.relay_y()
        qkv_sp.finish()

    kv_ix = [slot() for _ in range(MICRO)]
    other = {"ctx": lax.rem(c + 1, C)}

    def project(m):
        @pl.loop(0, R // RT)
        def _(i):
            acc = dot_nn(n1[at(m * R + i * RT, RT), :], wqkv[...])
            q[m, at(i * RT, RT), :] = (acc[:, 0:HP] * scale).astype(BF)
            kv[m, at(c * R + i * RT, RT), :] = acc[:, HP:HP + KV].astype(BF)
        w = kv.at[m, at(c * R, R)]
        send(w, w, kv_ix[m], other)
        flip(m, c * R)

    def spread(w):
        if w == "o":
            for k, i in zip(range(1, NT), wo_ix):
                v = wo.at[t, own_rows]
                copy_to(v, v, i, z_to(k)).wait_recv()
        else:
            v = {"g": wg, "u": wu, "d": wd}[w[0]].at[0, own_rows]
            copy_to(v, v, twin_ix[w[0]], twin).wait_recv()
        spreads[w].start()

    def weights_ready():
        for sp in spreads.values():
            sp.finish()

    onat, lse = r["onat"], r["lse"]
    lanes = lax.broadcasted_iota(jnp.int32, (RT, HP), 1)

    def head_mask(v, h, shift):
        lo = shift + h * HEAD_DIM
        return jnp.where((lanes >= lo) & (lanes < lo + HEAD_DIM), v, jnp.zeros_like(v))

    def flip(m, start):
        @pl.loop(0, R // RT)
        def _(i):
            kvT[m, :, at(start + i * RT, RT)] = kv[m, at(start + i * RT, RT), :].T

    def attend(m, i):
        kk = kv[m, :, 0:HP]
        sc = segc[m]
        sc = jnp.concatenate([sc] * (RT // 128), axis=1)
        sr = segr[m:m + 1, at(c * R + i * RT, RT)]
        qq = q[m, pl.ds(i * RT, RT), :]
        for h in range(NH):
            s = dot_nt(kk, head_mask(qq, h, 0))
            s = jnp.where(sc == sr, s, NEG)
            mx = jnp.max(s, axis=0, keepdims=True)
            e = jnp.exp(s - mx)
            tot = jnp.sum(e, axis=0, keepdims=True)
            p = (e * (1.0 / tot)).astype(BF)
            vT = kvT[m, H + h * HEAD_DIM:H + (h + 1) * HEAD_DIM, :]
            lo = VOFF + h * HEAD_DIM
            oT[m, lo:lo + HEAD_DIM, pl.ds(i * RT, RT)] = dot_nn(vT, p).astype(BF)
            lse[m, h, :, pl.ds(i * RT, RT)] = mx + jnp.log(tot)

    o_ix = [[slot() for _ in range(3)] for _ in range(MICRO)]

    def o_send(m, i, n):
        src = oT.at[m, pl.ds(VOFF, H), pl.ds(i * HR, HR)]
        return copy_to(src, oX.at[m, t, pl.ds(VOFF, H)], o_ix[m][n], (mate, twin, cross)[n])

    def share_o(m, i):
        @pl.when(half == i)
        def _():
            o_send(m, i, 0).start()

        @pl.when(half != i)
        def _():
            o_send(m, i, 1).start()
            o_send(m, i, 2).start()

    def wait_o(m):
        for n in range(3):
            o_send(m, 0, n).wait_recv()

    def close_o(m):
        for n in range(3):
            o_send(m, 0, n).wait_send()

    def attend_tile(m, i):
        if i == 0:
            w = kv.at[m, at(c * R, R)]
            copy_to(w, w, kv_ix[m], other).wait_recv()
            flip(m, lax.rem(c + 1, C) * R)
        attend(m, i)
        share_o(m, i)

    y1, n2, big = r["y1"], r["n2"], r["big"]
    d2s, d2r, fps, fpr = r["d2s"], r["d2r"], r["fps"], r["fpr"]
    d2_ix = [[slot() for _ in range(SUB)] for _ in range(MICRO)]
    fp_ix = [[slot() for _ in range(SUB)] for _ in range(MICRO)]

    def to_mate(src, dst, ix, m, j):
        rr = pl.ds(j * CH, CH)
        return copy_to(src.at[m, rr], dst.at[m, rr], ix[m][j], mate)

    def feed(m):
        if m == fed[0]:
            for cp in load_cot:
                cp.wait()
        oX[m, t, VOFF:HP, :] = oT[m, VOFF:HP, hrows]
        mr = pl.ds(m * HR, HR)
        for k in range(NT):
            onat[k, mr, :] = oX[m, k].T
        acc = tok[m, hrows, :].astype(F32)
        att = dot_nt(onat[0, mr, :], wo[0])
        for k in range(1, NT):
            att = att + dot_nt(onat[k, mr, :], wo[k])
        acc = acc + att
        y1[m] = acc
        rs = lax.rsqrt(jnp.mean(acc * acc, -1, keepdims=True) + EPS)
        n2v = (acc * rs * gains[1:2, :]).astype(BF)
        n2[mr, :] = n2v
        for n in range(2):
            g = dot_nn(n2v, wg[n])
            u = dot_nn(n2v, wu[n])
            th = jnp.tanh(GELU_K * (g + GELU_A * g * g * g))
            hf = 0.5 * (1.0 + th)
            gl = g * hf
            hv = (gl * u).astype(BF)
            big[0, n, mr, :] = hv
            dh = dot_nn(cot[mr, :], wd[n])
            dgl = hf + 0.5 * g * (1.0 - th * th) * (GELU_K * (1.0 + 3.0 * GELU_A * g * g))
            dgv = (dh * u * dgl).astype(BF)
            duv = (dh * gl).astype(BF)
            big[1, n, mr, :] = dgv
            big[2, n, mr, :] = duv
            more = dot_nt(dgv, wg[n]) + dot_nt(duv, wu[n])
            d2 = more if n == 0 else d2 + more
        d2s[m] = d2.astype(BF)

        @pl.when(outer)
        def _():
            for j in range(SUB):
                to_mate(d2s, d2r, d2_ix, m, j).start()

        yn = y1[m]
        rs = lax.rsqrt(jnp.mean(yn * yn, -1, keepdims=True) + EPS)
        gacc[1:2, :] += jnp.sum(d2 * (yn * rs), axis=0, keepdims=True)
        fps[m] = (dot_nt(big[0, 0, mr, :], wd[0]) + dot_nt(big[0, 1, mr, :], wd[1])).astype(BF)

    def feed_out(m):
        @pl.when(outer)
        def _():
            for j in range(SUB):
                to_mate(fps, fpr, fp_ix, m, j).start()

    class Reduce:
        def __init__(self, k, pieces, put):
            self.own, self.half, self.recv, self.parts = r["own_" + k], r["st_" + k], r["rv_" + k], r["pt_" + k]
            self.pieces, self.put = pieces, put
            self.px = slot()
            self.ix = [slot() for _ in offsets]

        def pair_copy(self):
            return copy_to(self.half, self.recv, self.px, partner)

        def pair(self):
            tmp = r["tmp"]
            for left, right, c0, width in self.pieces:
                @pl.loop(0, D // RT)
                def _(i, left=left, right=right, c0=c0, width=width):
                    tmp[:, 0:width] = dot_tn(left[:, at(i * RT, RT)], right[...])

                    @pl.loop(0, RT // UNIT)
                    def _(p):
                        row = i * RT + p * UNIT
                        b = row // (C * SR)
                        to = at((b // 2) * C * SR + lax.rem(row, C * SR), UNIT)
                        part = tmp[at(p * UNIT, UNIT), 0:width]

                        @pl.when(lax.rem(b, 2) == core)
                        def _():
                            self.own[to, c0:c0 + width] = part

                        @pl.when(lax.rem(b, 2) != core)
                        def _():
                            self.half[to, c0:c0 + width] = part.astype(BF)
            self.pair_copy().start()

        def block(self, n):
            pf, pc = square(offsets[n])
            src = self.half.at[at(((pf // 2) * C + pc) * SR, SR)]
            return copy_to(src, self.parts.at[n], self.ix[n], dev_sq(offsets[n]))

        def square(self):
            self.pair_copy().wait()
            tot = self.own[...] + self.recv[...].astype(F32)
            self.own[...] = tot
            self.half[...] = tot.astype(BF)
            for n in range(len(offsets)):
                self.block(n).start()

        def finish(self):
            tot = self.own[at((y * C + c) * SR, SR), :]
            for n in range(len(offsets)):
                self.block(n).wait()
            for n in range(len(offsets)):
                tot = tot + self.parts[n].astype(F32)
            self.put(tot)

    zs_ix = {k: slot() for k in "gud"}

    def twin_sum(k):
        def put(tot):
            r["out_" + k][...] = tot[:, 0:FF]
            r["zs_" + k][...] = tot[:, FF:2 * FF].astype(BF)
            send(r["zs_" + k], r["zr_" + k], zs_ix[k], twin)
        return put

    def split_qkv(tot):
        r["out_q"][...] = tot[:, 0:H]
        r["out_k"][...] = tot[:, HP:HP + H]
        r["out_v"][...] = pltpu.roll(tot[:, W - HP:W], HP - VOFF, 1)[:, 0:H]

    zo, zq = r["zo"], r["zq"]
    zo_ix, zo_sx = [slot(), slot()], slot()

    def zo_copies():
        out = []
        for dev, ix, sx in ((mate, zo_ix[0], None), (twin, zo_ix[1], None), (cross, zo_ix[1], zo_sx)):
            out.append(copy_to(zq.at[dev["tp"]], zo.at[half], ix, dev, sx))
        return out

    def out_sum(tot):
        for k in range(NT):
            zq[k] = tot[:, k * HP:(k + 1) * HP].astype(BF)
        zo[half] = zq[t]
        for cp in zo_copies():
            cp.start()

    dqkv, ar = r["dqkv"], r["ar"]
    pieces = {
        "d": [(cot, big.at[0, n], n * FF, FF) for n in range(2)],
        "g": [(n2, big.at[1, n], n * FF, FF) for n in range(2)],
        "u": [(n2, big.at[2, n], n * FF, FF) for n in range(2)],
        "q": [(n1, dqkv.at[:, pl.ds(0, 512)], 0, 512), (n1, dqkv.at[:, pl.ds(512, W - 512)], 512, W - 512)],
        "o": [(ar, onat.at[k], k * HP, HP) for k in range(NT)],
    }
    puts = {"d": twin_sum("d"), "g": twin_sum("g"), "u": twin_sum("u"), "q": split_qkv, "o": out_sum}
    reds = {k: Reduce(k, pieces[k], puts[k]) for k in "dguqo"}

    def reduce_step(k, what):
        if k == "o":
            pl.when(inner)(lambda: getattr(reds[k], what)())
        else:
            getattr(reds[k], what)()

    def last_sum(k):
        if k == "o":
            both(lambda: zo_copies()[1].wait_recv(), lambda: [cp.wait_recv() for cp in zo_copies()[:2]] and None)
            tot = zo[0].astype(F32) + zo[1].astype(F32)
            r["out_o"][...] = pltpu.roll(tot, HP - VOFF, 1)[:, 0:H]
        elif k != "q":
            copy_to(r["zs_" + k], r["zr_" + k], zs_ix[k], twin).wait_recv()
            r["out_" + k][...] += r["zr_" + k][...].astype(F32)

    dy, doT, doS = r["dy"], r["doT"], r["doS"]
    do_ix = [[[slot(), slot()] for _ in range(SUB)] for _ in range(MICRO)]
    do_sx = [[slot() for _ in range(SUB)] for _ in range(MICRO)]

    def do_copies(m, j):
        out = []
        to = doT.at[m, pl.ds(VOFF, H), pl.ds(pl.multiple_of(half * HR + j * CH, CH), CH)]
        for dev, n, sx in ((mate, 0, None), (twin, 1, None), (cross, 1, do_sx[m][j])):
            src = doS.at[dev["tp"], pl.ds(VOFF, H), pl.ds(j * CH, CH)]
            out.append(copy_to(src, to, do_ix[m][j][n], dev, sx))
        return out

    def back_norm(m, j):
        @pl.when(inner)
        def _():
            to_mate(d2s, d2r, d2_ix, m, j).wait_recv()
            if m:
                for cp in do_copies(m - 1, j):
                    cp.wait_send()
            rr = pl.ds(j * CH, CH)
            gr = pl.ds(m * HR + j * CH, CH)
            yv = y1[m, rr, :]
            d2 = d2s[m, rr, :].astype(F32) + d2r[m, rr, :].astype(F32)
            tv = lax.rsqrt(jnp.mean(yv * yv, -1, keepdims=True) + EPS)
            e2 = gains[1:2, :] * d2
            dot = jnp.mean(yv * e2, -1, keepdims=True)
            dv = cot[gr, :].astype(F32) + tv * e2 - yv * (tv * tv * tv * dot)
            dy[m, rr, :] = dv
            av = dv.astype(BF)
            ar[gr, :] = av
            for k in range(NT):
                doS[k, :, rr] = dot_nn(av, wo[k]).astype(BF).T
            doT[m, :, pl.ds(pl.multiple_of(half * HR + j * CH, CH), CH)] = doS[t, :, rr]
            for cp in do_copies(m, j):
                cp.start()

    delta, dqT, dkv_in, dkv_own = r["delta"], r["dqT"], r["dkv_in"], r["dkv_own"]
    dkv_out = wg.at[:, pl.ds(0, R), pl.ds(0, KV)]
    lay = [(0, 0), (0, HP), (1, 0)]
    qm = [wd.at[a, pl.ds(0, R), pl.ds(b, HP)] for a, b in lay]
    dom = [wu.at[a, pl.ds(0, R), pl.ds(b, HP)] for a, b in lay]

    def back_start(m):
        if m == 0:
            for cp in weight_sends:
                cp.wait_send()
        for j in range(SUB):
            cps = do_copies(m, j)
            both(lambda: cps[1].wait_recv(), lambda: [cp.wait_recv() for cp in cps[:2]] and None)

        @pl.loop(0, R // RT)
        def _(i):
            rr = at(i * RT, RT)
            dov = doT[m, :, rr].T
            for h in range(NH):
                lo = VOFF + h * HEAD_DIM
                prod = doT[m, lo:lo + HEAD_DIM, rr].astype(F32) * oT[m, lo:lo + HEAD_DIM, rr].astype(F32)
                delta[h, :, rr] = jnp.sum(prod, axis=0, keepdims=True)
                dom[h][rr, :] = head_mask(dov, h, VOFF)
                qm[h][rr, :] = head_mask(q[m, rr, :], h, 0)

    def back_half(m, key0, first):
        @pl.loop(0, R // RT)
        def _(i):
            sc = segc[m, at(key0, R), :]
            sc = jnp.concatenate([sc] * (RT // 128), axis=1)
            sr = segr[m:m + 1, at(c * R + i * RT, RT)]
            cs = at(i * RT, RT)
            for h in range(NH):
                s = dot_nt(kv[m, at(key0, R), 0:HP], qm[h][cs, :])
                s = jnp.where(sc == sr, s, NEG)
                p = jnp.exp(s - lse[m, h, :, cs])
                dp = dot_nt(kv[m, at(key0, R), KV - HP:KV], dom[h][cs, :])
                big[h, 1, :, cs] = p.astype(BF)
                big[h, 0, :, cs] = (p * (dp - delta[h, :, cs])).astype(BF)

        dst = dkv_out if first else dkv_own

        @pl.loop(0, R // RT)
        def _(i):
            rr = at(i * RT, RT)
            dk = dot_nn(big[0, 0, rr, :], qm[0][...])
            dv = dot_nn(big[0, 1, rr, :], dom[0][...])
            for h in range(1, NH):
                dk = dk + dot_nn(big[h, 0, rr, :], qm[h][...])
                dv = dv + dot_nn(big[h, 1, rr, :], dom[h][...])
            dst[m, rr, 0:128] = dk[:, 0:128].astype(dst.dtype)
            dst[m, rr, 128:256] = (dk[:, 128:256] + dv[:, 0:128]).astype(dst.dtype)
            dst[m, rr, 256:384] = dv[:, 128:256].astype(dst.dtype)
        for h in range(NH):
            hs = pl.ds(h * HEAD_DIM, HEAD_DIM)
            part = dot_nn(kvT[m, hs, at(key0, R)], big[h, 0])
            if first:
                dqT[hs, :] = part
            else:
                dqT[hs, :] = dqT[hs, :] + part

    dkv_ix = [slot() for _ in range(MICRO)]

    def back_peer(m):
        back_half(m, lax.rem(c + 1, C) * R, True)
        send(dkv_out.at[m], dkv_in.at[m], dkv_ix[m], other)

    def back_own(m):
        back_half(m, c * R, False)
        dqkv[pl.ds(m * R, R), 0:HP] = jnp.zeros((R, HP), BF)
        dqkv[pl.ds(m * R, R), 0:H] = (dqT[...] * scale).T.astype(BF)

    snd, rc1, rc2, igb = r["snd"], r["rc1"], r["rc2"], r["igb"]
    in_ix = [[[slot() for _ in range(SUB)] for _ in range(2)] for _ in range(MICRO)]
    sw_ix = [[slot() for _ in range(SUB)] for _ in range(MICRO)]

    def piece(own, j):
        return pl.ds(pl.multiple_of((half if own else 1 - half) * HR + j * CH, CH), CH)

    def inward(m, own, j):
        rr = piece(own, j)
        return copy_to(snd.at[m, rr], rc1.at[m, rr], in_ix[m][own][j], mate)

    def swap(m, j):
        return copy_to(snd.at[m, piece(0, j)], rc2.at[m, pl.ds(j * CH, CH)], sw_ix[m][j], cross)

    def join(m):
        copy_to(dkv_out.at[m], dkv_in.at[m], dkv_ix[m], other).wait_recv()
        for own in range(2):
            base = (half if own else 1 - half) * HR
            rr = at(base, HR)
            gr = pl.ds(pl.multiple_of(m * R + base, HR), HR)
            dqkv[gr, HP:HP + KV] = (dkv_own[m, rr, :] + dkv_in[m, rr, :].astype(F32)).astype(BF)
            d1 = dot_nt(dqkv[gr, :], wqkv[...])
            snd[m, rr, :] = d1.astype(BF)

            @pl.when(outer)
            def _(own=own):
                for j in range(SUB):
                    inward(m, own, j).start()

            xv = tok[m, rr, :].astype(F32)
            rs = lax.rsqrt(jnp.mean(xv * xv, -1, keepdims=True) + EPS)
            gacc[0:1, :] += jnp.sum(d1 * (xv * rs), axis=0, keepdims=True)

    def cross_over(m, j):
        @pl.when(inner)
        def _():
            inward(m, 0, j).wait_recv()
            rr = piece(0, j)
            snd[m, rr, :] = (snd[m, rr, :].astype(F32) + rc1[m, rr, :].astype(F32)).astype(BF)
            swap(m, j).start()

    class Result:
        def __init__(self, buf, name):
            self.buf, self.name = buf, name
            self.ix = [[[slot() for _ in range(3)] for _ in range(SUB)] for _ in range(MICRO)]

        def copy(self, m, j, n):
            at_ = self.buf.at[m, piece(n != 2, j)]
            return copy_to(at_, at_, self.ix[m][j][n], cross if n == 1 else mate)

        def arrived(self, m, j, n):
            at_ = self.buf.at[m, piece(0, j)]
            copy_to(at_, at_, self.ix[m][j][n], mate).wait_recv()

        def store(self, m, j, own):
            rr = piece(own, j)
            store(self.buf.at[m, rr], r[self.name].at[m, 0, rr])

        def near(self, m, j, make):
            def one():
                make(m, j)
                self.copy(m, j, 1).start()
                self.copy(m, j, 0).start()
            both(one, lambda: self.arrived(m, j, 0))
            self.store(m, j, 1)

        def far(self, m, j):
            def one():
                self.arrived(m, j, 1)
                self.copy(m, j, 2).start()
            both(one, lambda: self.arrived(m, j, 2))
            self.store(m, j, 0)

        def close(self, m, j):
            @pl.when(inner)
            def _():
                for n in range(3):
                    self.copy(m, j, n).wait_send()

    stores = []

    def store(src, dst):
        cp = pltpu.make_async_copy(src, dst, local.at[8 + len(stores)])
        cp.start()
        stores.append(cp)

    def make_output(m, j):
        to_mate(fps, fpr, fp_ix, m, j).wait_recv()
        rr = pl.ds(j * CH, CH)
        tot = y1[m, rr, :] + (fps[m, rr, :].astype(F32) + fpr[m, rr, :].astype(F32))
        r["outv"][m, piece(1, j), :] = tot.astype(BF)

    def make_input_grad(m, j):
        inward(m, 1, j).wait_recv()
        swap(m, j).wait_recv()
        rr = pl.ds(j * CH, CH)
        here = piece(1, j)
        xv = tok[m, here, :].astype(F32)
        d1 = snd[m, here, :].astype(F32) + rc1[m, here, :].astype(F32) + rc2[m, rr, :].astype(F32)
        tv = lax.rsqrt(jnp.mean(xv * xv, -1, keepdims=True) + EPS)
        e1 = gains[0:1, :] * d1
        dot = jnp.mean(xv * e1, -1, keepdims=True)
        igb[m, here, :] = (dy[m, rr, :] + tv * e1 - xv * (tv * tv * tv * dot)).astype(BF)

    out_res, ig_res = Result(r["outv"], "out"), Result(igb, "ig")

    gz, gz_ix = r["gz"], [slot() for _ in range(NT)]
    gin, gpart = r["gin"], r["gpart"]
    gain_ix = [slot() for _ in group]

    def gain_z():
        for k in range(1, NT):
            send(gacc, gz.at[k], gz_ix[k], z_to(k))

    def gain_group():
        for k in range(1, NT):
            copy_to(gacc, gz.at[k], gz_ix[k], z_to(k)).wait_recv()
        tot = gacc[...]
        for k in range(1, NT):
            tot = tot + gz[k]
        gpart[...] = tot
        for n, off in enumerate(group):
            send(gpart, gin.at[n], gain_ix[n], dev_group(off))

    def gain_final():
        for n, off in enumerate(group):
            copy_to(gpart, gin.at[n], gain_ix[n], dev_group(off)).wait_recv()
        tot = gpart[...]
        for n in range(len(group)):
            tot = tot + gin[n]
        tot = lax.dot_general(
            tot, place.astype(F32), (((1,), (1,)), ((), ())), precision=lax.Precision.HIGHEST,
            preferred_element_type=F32)
        r["out_ga"][...] = tot[0:1, :]
        r["out_gf"][...] = tot[1:2, :]

    fed = [step[1] for step in ORDER if step[0] == "F"]
    acts = {
        "prep": prepare, "qR": qkv_ready, "wF": weights_ready, "P": project, "wS": spread,
        "wX": lambda w: spreads[w].relay_x(), "wY": lambda w: spreads[w].relay_y(), "AT": attend_tile,
        "O": wait_o, "F": feed, "FP": feed_out, "G": lambda k: reduce_step(k, "pair"), "SQ": lambda k: reduce_step(k, "square"),
        "SF": lambda k: reduce_step(k, "finish"), "SZ": last_sum, "BN": back_norm, "BS": back_start,
        "PE": back_peer, "OW": back_own, "J": join, "X": cross_over,
        "ON": lambda m, j: out_res.near(m, j, make_output), "OF": out_res.far,
        "IN": lambda m, j: ig_res.near(m, j, make_input_grad), "IF": ig_res.far,
        "GZ": gain_z, "GR": gain_group, "GF": gain_final,
    }
    for step in ORDER:
        acts[step[0]](*step[1:])
    for cp in stores:
        cp.wait()
    for cp in sends:
        cp.wait_send()
    for m in range(MICRO):
        close_o(m)
        for j in range(SUB):
            out_res.close(m, j)
            ig_res.close(m, j)

            def inner_done(m=m, j=j):
                if m == MICRO - 1:
                    for cp in do_copies(m, j):
                        cp.wait_send()
                swap(m, j).wait_send()

            def outer_done(m=m, j=j):
                to_mate(d2s, d2r, d2_ix, m, j).wait_send()
                to_mate(fps, fpr, fp_ix, m, j).wait_send()
                inward(m, 0, j).wait_send()
                inward(m, 1, j).wait_send()

            both(inner_done, outer_done)

    @pl.when(inner)
    def _():
        for cp in zo_copies():
            cp.wait_send()

    assert counter[0] <= ssem.shape[0]


def fused_shards(dims, tokens, segments, cotangent, query_weight, key_weight, value_weight, out_weight,
                 gate_weight, up_weight, down_weight, attn_gain, ffn_gain):
    R, D, H, FF, C, NF, NT, MICRO = dims
    L = C * R
    SR = D // (NF * C)
    NH = H // HEAD_DIM
    HP, KV, Y = 256, 2 * H, NF // 2
    HALF = Y * C * SR
    NO = Y * C - 1
    NG = NF * C - 1
    W = HP + KV
    ins = [
        ("tok_in", tokens.reshape(MICRO, R, D)),
        ("segr", segments),
        ("cot_in", cotangent.reshape(MICRO, R, D)),
        ("wq_in", query_weight),
        ("wk_in", key_weight),
        ("wv_in", value_weight),
        ("wo_in", out_weight),
        ("wg_in", gate_weight),
        ("wu_in", up_weight),
        ("wd_in", down_weight),
        ("gain_a", attn_gain[None]),
        ("gain_f", ffn_gain[None]),
    ]
    far = ("tok_in", "cot_in", "out", "ig")
    outs = [
        ("out", (MICRO, 1, R, D), BF),
        ("ig", (MICRO, 1, R, D), BF),
        ("out_q", (SR, H), F32),
        ("out_k", (SR, H), F32),
        ("out_v", (SR, H), F32),
        ("out_o", (SR, H), F32),
        ("out_g", (SR, FF), F32),
        ("out_u", (SR, FF), F32),
        ("out_d", (SR, FF), F32),
        ("out_ga", (1, SR), F32),
        ("out_gf", (1, SR), F32),
    ]
    v = pltpu.VMEM
    HR = R // 2
    scratch = [
        ("tok", v((MICRO, R, D), BF)), ("cot", v((MICRO * HR, D), BF)), ("dy", v((MICRO, HR, D), F32)),
        ("outv", v((MICRO, R, D), BF)), ("igb", v((MICRO, R, D), BF)),
        ("gz", v((NT, 2, D), F32)), ("gpart", v((2, D), F32)),
        ("lsem", pltpu.SemaphoreType.DMA((32,))),
        ("gmine", v((2, D), F32)), ("gall", v((NG, 2, D), F32)), ("gains", v((2, D), F32)),
        ("gacc", v((2, D), F32)), ("gin", v((NG, 2, D), F32)),
        ("wqkv", v((D, W), BF)), ("wo", v((NT, D, HP), BF)),
        ("wg", v((2, D, FF), BF)), ("wu", v((2, D, FF), BF)), ("wd", v((2, D, FF), BF)),
        ("segc", v((MICRO, L, 128), jnp.int32)),
        ("n1", v((MICRO * R, D), BF)), ("q", v((MICRO, R, HP), BF)),
        ("kv", v((MICRO, L, KV), BF)), ("kvT", v((MICRO, KV, L), BF)),
        ("oT", v((MICRO, HP, R), BF)), ("oX", v((MICRO, NT, HP, HR), BF)), ("onat", v((NT, MICRO * HR, HP), BF)),
        ("lse", v((MICRO, NH, 1, R), F32)),
        ("d2s", v((MICRO, HR, D), BF)), ("d2r", v((MICRO, HR, D), BF)),
        ("fps", v((MICRO, HR, D), BF)), ("fpr", v((MICRO, HR, D), BF)),
        ("snd", v((MICRO, R, D), BF)), ("rc1", v((MICRO, R, D), BF)), ("rc2", v((MICRO, HR, D), BF)),
        ("y1", v((MICRO, HR, D), F32)), ("n2", v((MICRO * HR, D), BF)), ("ar", v((MICRO * HR, D), BF)),
        ("big", v((3, 2, R, FF), BF)),
        ("doT", v((MICRO, HP, R), BF)), ("doS", v((NT, HP, HR), BF)),
        ("delta", v((NH, 1, R), F32)), ("dqT", v((H, R), F32)), ("dqkv", v((MICRO * R, W), BF)),
        ("dkv_own", v((MICRO, R, KV), F32)), ("dkv_in", v((MICRO, R, KV), BF)),
        ("tmp", v((256, 512), F32)), ("zo", v((2, SR, HP), BF)), ("zq", v((NT, SR, HP), BF)),
    ]
    for k, cols in (("q", W), ("o", NT * HP), ("g", 2 * FF), ("u", 2 * FF), ("d", 2 * FF)):
        scratch += [("own_" + k, v((HALF, cols), F32)), ("rv_" + k, v((HALF, cols), BF)),
                    ("st_" + k, v((HALF, cols), BF)), ("pt_" + k, v((NO, SR, cols), BF))]
    for k in "gud":
        scratch += [("zs_" + k, v((SR, FF), BF)), ("zr_" + k, v((SR, FF), BF))]
    nsem = 320
    scratch += [("ssem", pltpu.SemaphoreType.DMA((nsem,))), ("rsem", pltpu.SemaphoreType.DMA((nsem,)))]
    names = [n for n, _ in ins] + [n for n, _, _ in outs] + [n for n, _ in scratch]
    def spec(name):
        return pl.BlockSpec(memory_space=pl.ANY if name in far else pltpu.VMEM)

    res = pl.pallas_call(
        functools.partial(layer_kernel, dims, names),
        out_shape=[jax.ShapeDtypeStruct(s, d) for _, s, d in outs],
        in_specs=[spec(n) for n, _ in ins],
        out_specs=[spec(n) for n, _, _ in outs],
        scratch_shapes=[s for _, s in scratch],
        compiler_params=pltpu.CompilerParams(
            collective_id=0, has_side_effects=True, vmem_limit_bytes=67043328),
    )(*[a for _, a in ins])
    res = settle(res)
    return tuple(res[:9]) + (res[9].reshape(SR), res[10].reshape(SR))


def settle(arrays):
    pieces = []
    for n, a in enumerate(arrays):
        if a.ndim == 4:
            pieces += [(n, (m, 0, pl.ds(k * 256, 256))) for m in range(a.shape[0]) for k in range(a.shape[2] // 256)]
        else:
            pieces.append((n, None))

    kinds = [F32] * len(arrays)
    kinds[0] = arrays[0].dtype
    wide = [n for n, a in enumerate(arrays) if a.dtype != kinds[n]]

    def kernel(*refs):
        k = len(arrays)
        src, dst, buf, sem = refs[:k], refs[k:2 * k], refs[2 * k:3 * k], refs[3 * k:]
        last = list(buf)
        for i, n in enumerate(wide):
            last[n] = sem[2 + i]
        pick = lambda ref, at: ref if at is None else ref.at[at]
        come = [pltpu.make_async_copy(pick(src[n], at), pick(buf[n], at), sem[0].at[i]) for i, (n, at) in enumerate(pieces)]
        go = [pltpu.make_async_copy(pick(last[n], at), pick(dst[n], at), sem[1].at[i]) for i, (n, at) in enumerate(pieces)]
        for cp in come:
            cp.start()
        for a, b, (n, at) in zip(come, go, pieces):
            a.wait()
            if n in wide:
                last[n][at] = buf[n][at].astype(F32)
            b.start()
        for cp in go:
            cp.wait()

    hbm = pl.BlockSpec(memory_space=pl.ANY)
    return pl.pallas_call(
        kernel,
        out_shape=[jax.ShapeDtypeStruct(a.shape, d) for a, d in zip(arrays, kinds)],
        in_specs=[hbm] * len(arrays),
        out_specs=[hbm] * len(arrays),
        scratch_shapes=[pltpu.VMEM(a.shape, a.dtype) for a in arrays] + [pltpu.SemaphoreType.DMA((len(pieces),))] * 2
        + [pltpu.VMEM(arrays[n].shape, F32) for n in wide],
    )(*arrays)


def fits(dims, seqs):
    R, D, H, FF, C, NF, NT, MICRO = dims
    blocks = D % (16 * NF * C) == 0 and D % 256 == 0
    return (C, NT, NF, H, MICRO, seqs, R, FF) == (2, 4, 4, 192, 2, 1, 512, 512) and D <= 768 and blocks


SPECS = (
    P(None, "fsdp", "ctx", None),
    P(None, "fsdp", None),
    P(None, "fsdp", "ctx", None),
) + (P(("fsdp", "ctx"), "tp"),) * 7 + (P(("fsdp", "ctx")),) * 2
OUT_SPECS = (P(None, "fsdp", "ctx", None),) * 2 + (P(("fsdp", "ctx"), "tp"),) * 7 + (P(("fsdp", "ctx")),) * 2


def solution(mesh):
    nf, nc, nt = mesh.shape["fsdp"], mesh.shape["ctx"], mesh.shape["tp"]

    def chosen(*args):
        tokens, weight, ffw = args[0], args[3], args[7]
        micro, seqs, rows, width = tokens.shape
        dims = (rows, width, weight.shape[1], ffw.shape[1], nc, nf, nt, micro)
        return fused_shards(dims, *args) if fits(dims, seqs) else shards(*args)

    return jax.shard_map(chosen, mesh=mesh, in_specs=SPECS, out_specs=OUT_SPECS, check_vma=False)
```

```python
import functools

import jax
import jax.numpy as jnp
from jax import lax
from jax.experimental import pallas as pl
from jax.experimental.pallas import tpu as pltpu
from jax.sharding import PartitionSpec as P

HEAD_DIM = 64


EPS = 1e-06


def gather_weights(
    query_weight,
    key_weight,
    value_weight,
    out_weight,
    gate_weight,
    up_weight,
    down_weight,
    attn_gain,
    ffn_gain,
):
    return (
        lax.all_gather(query_weight, ("fsdp", "ctx"), axis=0, tiled=True),
        lax.all_gather(key_weight, ("fsdp", "ctx"), axis=0, tiled=True),
        lax.all_gather(value_weight, ("fsdp", "ctx"), axis=0, tiled=True),
        lax.all_gather(out_weight, ("fsdp", "ctx"), axis=0, tiled=True),
        lax.all_gather(gate_weight, ("fsdp", "ctx"), axis=0, tiled=True),
        lax.all_gather(up_weight, ("fsdp", "ctx"), axis=0, tiled=True),
        lax.all_gather(down_weight, ("fsdp", "ctx"), axis=0, tiled=True),
        lax.all_gather(attn_gain, ("fsdp", "ctx"), axis=0, tiled=True),
        lax.all_gather(ffn_gain, ("fsdp", "ctx"), axis=0, tiled=True),
    )


def tensor_sum(partial_value):
    return lax.psum(partial_value, "tp")


def normalize(values, gain_vec):
    return values * lax.rsqrt(jnp.mean(values * values, -1, keepdims=True) + EPS) * gain_vec


def gelu_mix(gate_act, up_act):
    return jax.nn.gelu(gate_act, approximate=True) * up_act


def contract_last(left_op, right_op):
    return lax.dot_general(
        left_op, right_op, (((1,), (1,)), ((), ())), preferred_element_type=jnp.float32
    )


def contract_first(left_op, right_op):
    return lax.dot_general(
        left_op, right_op, (((0,), (0,)), ((), ())), preferred_element_type=jnp.float32
    )


def masked_scores(queries, key_whole, query_seg, seg_all, head_count):
    local_rows = queries.shape[0]
    query_heads = queries.reshape(local_rows, head_count, HEAD_DIM)
    key_heads = key_whole.reshape(key_whole.shape[0], head_count, HEAD_DIM)
    products = jnp.einsum(
        "qhd,khd->hqk", query_heads, key_heads, preferred_element_type=jnp.float32
    ) * HEAD_DIM ** (-0.5)
    same_doc = query_seg[:, None] == seg_all[None, :]
    return jnp.where(same_doc[None], products, -1e30)


def forward_pass(inputs, seg_all, gathered, ctx_pos):
    w_query, w_key, w_value, w_out, w_gate, w_up, w_down, gain_attn, gain_ffn = gathered
    head_count = w_query.shape[1] // HEAD_DIM
    local_rows = inputs.shape[0]
    query_seg = lax.dynamic_slice_in_dim(seg_all, ctx_pos * local_rows, local_rows)
    inputs_f = inputs.astype(jnp.float32)
    normed_one = normalize(inputs_f, gain_attn.astype(jnp.float32)).astype(jnp.bfloat16)
    queries = jnp.dot(normed_one, w_query, preferred_element_type=jnp.float32).astype(jnp.bfloat16)
    key_local = jnp.dot(normed_one, w_key, preferred_element_type=jnp.float32).astype(jnp.bfloat16)
    value_local = jnp.dot(normed_one, w_value, preferred_element_type=jnp.float32).astype(
        jnp.bfloat16
    )
    key_whole, value_whole = (
        lax.all_gather(key_local, "ctx", axis=0, tiled=True),
        lax.all_gather(value_local, "ctx", axis=0, tiled=True),
    )
    scores = masked_scores(queries, key_whole, query_seg, seg_all, head_count)
    row_max = jnp.max(scores, -1, keepdims=True)
    row_total = jnp.sum(jnp.exp(scores - row_max), -1, keepdims=True)
    log_total = row_max + jnp.log(row_total)
    probs_low = jnp.exp(scores - log_total).astype(jnp.bfloat16)
    value_heads = value_whole.reshape(value_whole.shape[0], head_count, HEAD_DIM)
    attn_mixed = jnp.einsum(
        "hqk,khd->qhd", probs_low, value_heads, preferred_element_type=jnp.float32
    )
    attn_mixed = attn_mixed.reshape(local_rows, head_count * HEAD_DIM).astype(jnp.bfloat16)
    attn_partial = contract_last(attn_mixed, w_out)
    residual = inputs_f + tensor_sum(attn_partial)
    normed_two = normalize(residual, gain_ffn.astype(jnp.float32)).astype(jnp.bfloat16)
    gate_act = jnp.dot(normed_two, w_gate, preferred_element_type=jnp.float32)
    up_act = jnp.dot(normed_two, w_up, preferred_element_type=jnp.float32)
    hidden = gelu_mix(gate_act, up_act).astype(jnp.bfloat16)
    ffn_partial = contract_last(hidden, w_down)
    result = (residual + tensor_sum(ffn_partial)).astype(jnp.bfloat16)
    stored = (
        inputs_f,
        normed_one,
        queries,
        key_whole,
        value_whole,
        log_total,
        attn_mixed,
        residual,
        normed_two,
        gate_act,
        up_act,
        hidden,
        query_seg,
    )
    return (result, stored)


def backward_pass(cot_rows, stored, gathered, seg_all, ctx_pos):
    w_query, w_key, w_value, w_out, w_gate, w_up, w_down, gain_attn, gain_ffn = gathered
    (
        inputs_f,
        normed_one,
        queries,
        key_whole,
        value_whole,
        log_total,
        attn_mixed,
        residual,
        normed_two,
        gate_act,
        up_act,
        hidden,
        query_seg,
    ) = stored
    head_count = w_query.shape[1] // HEAD_DIM
    local_rows = queries.shape[0]
    seq_rows = key_whole.shape[0]
    scale = HEAD_DIM ** (-0.5)
    dout = cot_rows.astype(jnp.float32)
    dout_low = dout.astype(jnp.bfloat16)
    grad_down = contract_first(dout_low, hidden)
    dhidden = jnp.dot(dout_low, w_down, preferred_element_type=jnp.float32)
    mixed_unused, mix_back = jax.vjp(gelu_mix, gate_act, up_act)
    dgate, dup = mix_back(dhidden)
    dgate_low = dgate.astype(jnp.bfloat16)
    dup_low = dup.astype(jnp.bfloat16)
    grad_gate = contract_first(normed_two, dgate_low)
    grad_up = contract_first(normed_two, dup_low)
    dn2_partial = contract_last(dgate_low, w_gate) + contract_last(dup_low, w_up)
    norm_unused, norm_back = jax.vjp(normalize, residual, gain_ffn.astype(jnp.float32))
    dresid_norm, grad_gain_ffn = norm_back(tensor_sum(dn2_partial))
    dresidual = dout + dresid_norm
    dres_low = dresidual.astype(jnp.bfloat16)
    grad_out = contract_first(dres_low, attn_mixed)
    dmixed = jnp.dot(dres_low, w_out, preferred_element_type=jnp.float32).astype(jnp.bfloat16)
    dmixed_heads = dmixed.reshape(local_rows, head_count, HEAD_DIM)
    scores = masked_scores(queries, key_whole, query_seg, seg_all, head_count)
    prob_full = jnp.exp(scores - log_total)
    key_heads = key_whole.reshape(seq_rows, head_count, HEAD_DIM)
    value_heads = value_whole.reshape(seq_rows, head_count, HEAD_DIM)
    dprobs = jnp.einsum(
        "qhd,khd->hqk", dmixed_heads, value_heads, preferred_element_type=jnp.float32
    )
    row_delta = jnp.sum(prob_full * dprobs, -1, keepdims=True)
    dscores = (prob_full * (dprobs - row_delta)).astype(jnp.bfloat16)
    dquery = (
        jnp.einsum("hqk,khd->qhd", dscores, key_heads, preferred_element_type=jnp.float32) * scale
    )
    query_all, dmixed_all = (
        lax.all_gather(queries, "ctx", axis=0, tiled=True),
        lax.all_gather(dmixed, "ctx", axis=0, tiled=True),
    )
    log_all, delta_all = (
        lax.all_gather(log_total, "ctx", axis=1, tiled=True),
        lax.all_gather(row_delta, "ctx", axis=1, tiled=True),
    )
    start = ctx_pos * local_rows
    key_own = lax.dynamic_slice_in_dim(key_whole, start, local_rows)
    value_own = lax.dynamic_slice_in_dim(value_whole, start, local_rows).reshape(
        local_rows, head_count, HEAD_DIM
    )
    scores_own = masked_scores(query_all, key_own, seg_all, query_seg, head_count)
    prob_own = jnp.exp(scores_own - log_all)
    dmixed_all_heads = dmixed_all.reshape(seq_rows, head_count, HEAD_DIM)
    query_all_heads = query_all.reshape(seq_rows, head_count, HEAD_DIM)
    dprobs_own = jnp.einsum(
        "qhd,khd->hqk", dmixed_all_heads, value_own, preferred_element_type=jnp.float32
    )
    dscores_own = (prob_own * (dprobs_own - delta_all)).astype(jnp.bfloat16)
    dkey_local = (
        jnp.einsum("hqk,qhd->khd", dscores_own, query_all_heads, preferred_element_type=jnp.float32)
        * scale
    ).reshape(local_rows, head_count * HEAD_DIM)
    dvalue_local = jnp.einsum(
        "hqk,qhd->khd",
        prob_own.astype(jnp.bfloat16),
        dmixed_all_heads,
        preferred_element_type=jnp.float32,
    ).reshape(local_rows, head_count * HEAD_DIM)
    dquery_low = dquery.reshape(local_rows, head_count * HEAD_DIM).astype(jnp.bfloat16)
    dkey_low = dkey_local.astype(jnp.bfloat16)
    dvalue_low = dvalue_local.astype(jnp.bfloat16)
    grad_query = contract_first(normed_one, dquery_low)
    grad_key = contract_first(normed_one, dkey_low)
    grad_value = contract_first(normed_one, dvalue_low)
    dn1_partial = (
        contract_last(dquery_low, w_query)
        + contract_last(dkey_low, w_key)
        + contract_last(dvalue_low, w_value)
    )
    norm_unused_two, norm_back_two = jax.vjp(normalize, inputs_f, gain_attn.astype(jnp.float32))
    dinput_norm, grad_gain_attn = norm_back_two(tensor_sum(dn1_partial))
    input_grad = dresidual + dinput_norm
    grad_terms = (
        grad_query,
        grad_key,
        grad_value,
        grad_out,
        grad_gate,
        grad_up,
        grad_down,
        grad_gain_attn,
        grad_gain_ffn,
    )
    return (input_grad, grad_terms)


def shards(
    tokens,
    segments,
    cotangent,
    query_weight,
    key_weight,
    value_weight,
    out_weight,
    gate_weight,
    up_weight,
    down_weight,
    attn_gain,
    ffn_gain,
):
    ctx_pos = lax.axis_index("ctx")
    results = []
    input_grads = []
    total_grads = None
    for micro_step in range(tokens.shape[0]):
        seg_all = segments[micro_step, 0]
        gathered = gather_weights(
            query_weight,
            key_weight,
            value_weight,
            out_weight,
            gate_weight,
            up_weight,
            down_weight,
            attn_gain,
            ffn_gain,
        )
        result, stored = forward_pass(tokens[micro_step, 0], seg_all, gathered, ctx_pos)
        gathered = gather_weights(
            query_weight,
            key_weight,
            value_weight,
            out_weight,
            gate_weight,
            up_weight,
            down_weight,
            attn_gain,
            ffn_gain,
        )
        input_grad, grad_terms = backward_pass(
            cotangent[micro_step, 0], stored, gathered, seg_all, ctx_pos
        )
        results.append(result)
        input_grads.append(input_grad)
        total_grads = (
            grad_terms if total_grads is None else jax.tree.map(jnp.add, total_grads, grad_terms)
        )
    gain_attn_total = total_grads[7]
    gain_ffn_total = total_grads[8]
    owned = (
        lax.psum_scatter(total_grads[0], ("fsdp", "ctx"), scatter_dimension=0, tiled=True),
        lax.psum_scatter(total_grads[1], ("fsdp", "ctx"), scatter_dimension=0, tiled=True),
        lax.psum_scatter(total_grads[2], ("fsdp", "ctx"), scatter_dimension=0, tiled=True),
        lax.psum_scatter(total_grads[3], ("fsdp", "ctx"), scatter_dimension=0, tiled=True),
        lax.psum_scatter(total_grads[4], ("fsdp", "ctx"), scatter_dimension=0, tiled=True),
        lax.psum_scatter(total_grads[5], ("fsdp", "ctx"), scatter_dimension=0, tiled=True),
        lax.psum_scatter(total_grads[6], ("fsdp", "ctx"), scatter_dimension=0, tiled=True),
        lax.psum_scatter(gain_attn_total, ("fsdp", "ctx"), scatter_dimension=0, tiled=True),
        lax.psum_scatter(gain_ffn_total, ("fsdp", "ctx"), scatter_dimension=0, tiled=True),
    )
    output = jnp.stack(results)[:, None]
    input_grad_all = jnp.stack(input_grads)[:, None]
    return (
        output,
        input_grad_all,
        owned[0],
        owned[1],
        owned[2],
        owned[3],
        owned[4],
        owned[5],
        owned[6],
        owned[7],
        owned[8],
    )


NEG = -1e30
MESH = pl.DeviceIdType.MESH
BF = jnp.bfloat16
F32 = jnp.float32
GELU_K = 0.7978845608028654
GELU_A = 0.044715
ORDER = (
    ("prep",), ("qR",), ("P", 0), ("wS", "g1"), ("wX", "g0"), ("wX", "u0"), ("wS", "o"), ("P", 1), ("AT", 0, 0),
    ("wX", "d0"), ("wS", "d1"), ("wS", "u1"), ("AT", 0, 1), ("wX", "o"), ("wX", "g1"), ("AT", 1, 0), ("wY", "g0"),
    ("wY", "d0"), ("wY", "o"), ("wX", "d1"), ("AT", 1, 1), ("wY", "u0"), ("wX", "u1"), ("wY", "g1"), ("wF", "o"),
    ("O", 0), ("wY", "d1"), ("F1", 0), ("wF", 0), ("wY", "u1"), ("FS", 0, 0), ("wF", 1), ("FS", 0, 1), ("O", 1),
    ("FP", 0), ("F1", 1), ("FS", 1, 0), ("FS", 1, 1), ("BN", 0, 0), ("G", "d"), ("BN", 0, 1), ("G", "g"),
    ("ON", 0, 0), ("SQ", "d"), ("BS", 0), ("FP", 1), ("G", "u"), ("ON", 0, 1), ("PE", 0), ("OF", 0, 0), ("SQ", "g"),
    ("OW", 0), ("SF", "d"), ("BN", 1, 0), ("BN", 1, 1), ("G", "o"), ("OF", 0, 1), ("J", 0), ("BS", 1), ("ON", 1, 1),
    ("PE", 1), ("ON", 1, 0), ("OF", 1, 1), ("OW", 1), ("X", 0, 0), ("SQ", "o"), ("OF", 1, 0), ("J", 1), ("X", 0, 1),
    ("IN", 0, 0), ("IN", 0, 1), ("X", 1, 0), ("IF", 0, 0), ("IF", 0, 1), ("SQ", "u"), ("G", "q"), ("SF", "g"),
    ("SF", "o"), ("IN", 1, 0), ("SQ", "q"), ("GZ",), ("SZ", "o"), ("X", 1, 1), ("IF", 1, 0), ("IN", 1, 1),
    ("SZ", "d"), ("GR",), ("SZ", "g"), ("SF", "u"), ("SF", "q"), ("GF",), ("IF", 1, 1), ("SZ", "u"),
)


def dot_nn(a, b):
    return lax.dot_general(a, b, (((1,), (0,)), ((), ())), preferred_element_type=F32)


def dot_nt(a, b):
    return lax.dot_general(a, b, (((1,), (1,)), ((), ())), preferred_element_type=F32)


def dot_tn(a, b):
    return lax.dot_general(a, b, (((0,), (0,)), ((), ())), preferred_element_type=F32)


def at(i, n):
    return pl.ds(pl.multiple_of(i, n), n)


def layer_kernel(dims, names, *refs):
    r = dict(zip(names, refs))
    R, D, H, FF, C, NF, NT, MICRO = dims
    L = C * R
    NH = H // HEAD_DIM
    HP = 256
    KV = 2 * H
    Y = NF // 2
    SR = D // (NF * C)
    RT = 256
    CH = 128
    UNIT = 64
    NCH = R // CH
    f = lax.axis_index("fsdp")
    c = lax.axis_index("ctx")
    t = lax.axis_index("tp")
    core = lax.rem(f, 2)
    y = f // 2
    shard = f * C + c
    partner = {"fsdp": f + 1 - 2 * core}
    ssem, rsem = r["ssem"], r["rsem"]
    counter = [0]

    def slot():
        counter[0] += 1
        return counter[0] - 1

    def copy_to(src, dst, idx, dev, sidx=None):
        return pltpu.make_async_remote_copy(
            src_ref=src, dst_ref=dst, send_sem=ssem.at[idx if sidx is None else sidx], recv_sem=rsem.at[idx],
            device_id=dev, device_id_type=MESH)

    offsets = [(dy, dc) for dy in range(Y) for dc in range(C) if (dy, dc) != (0, 0)]

    def square(off):
        dy, dc = off
        return (2 * lax.rem(y + dy, Y) + core, lax.rem(c + dc, C))

    def square_from(off):
        dy, dc = off
        return (2 * lax.rem(y + Y - dy, Y) + core, lax.rem(c + C - dc, C))

    def dev_sq(off):
        pf, pc = square(off)
        return {"fsdp": pf, "ctx": pc}

    def z_to(k):
        return {"tp": lax.rem(t + k, NT)}

    group = [(df, dc) for df in range(NF) for dc in range(C) if (df, dc) != (0, 0)]

    def dev_group(off):
        return {"fsdp": lax.rem(f + off[0], NF), "ctx": lax.rem(c + off[1], C)}

    half = t // 2
    inner = (t == 1) | (t == 2)
    outer = (t == 0) | (t == 3)
    mate = {"tp": t + 1 - 2 * lax.rem(t, 2)}
    twin_t = lax.rem(t + 2, NT)
    twin = {"tp": twin_t}
    cross = {"tp": NT - 1 - t}
    HR = R // 2
    SUB = HR // CH
    hrows = at(half * HR, HR)

    def both(do_inner, do_outer):
        pl.when(inner)(do_inner)
        pl.when(outer)(do_outer)

    local = r["lsem"]

    def load(src, dst, n):
        cp = pltpu.make_async_copy(src, dst, local.at[n])
        cp.start()
        return cp

    own_rows = at(shard * SR, SR)
    wqkv, wo, woz, wg, wu, wd = r["wqkv"], r["wo"], r["woz"], r["wg"], r["wu"], r["wd"]
    load_first = [load(r[n + "_in"], r[n + "_own"], 3 + i) for i, n in enumerate(("gain_a", "gain_f", "wq", "wk", "wv"))]
    load_out = load(r["wo_in"], r["wo_own"], 8)
    load_ffn = [load(r[n + "_in"], r[n].at[0, own_rows], 9 + i) for i, n in enumerate(("wg", "wu", "wd"))]
    load_tok = load(r["tok_in"], r["tok"], 0)
    load_cot = [load(r["cot_in"].at[m, hrows], r["cot"].at[pl.ds(m * HR, HR)], 1 + m) for m in range(MICRO)]

    bar = pltpu.get_barrier_semaphore()
    for off in group:
        pl.semaphore_signal(bar, inc=1, device_id=dev_group(off), device_id_type=MESH)
    for k in range(1, NT):
        pl.semaphore_signal(bar, inc=1, device_id=z_to(k), device_id_type=MESH)

    def spot(width, shift):
        i = lax.broadcasted_iota(jnp.int32, (H, width), 0)
        j = lax.broadcasted_iota(jnp.int32, (H, width), 1)
        return (j == i + shift).astype(BF)

    W = HP + KV
    VOFF = HP - H
    gm = r["gmine"]
    cols = lax.broadcasted_iota(jnp.int32, (SR, D), 1)
    rows = lax.broadcasted_iota(jnp.int32, (SR, D), 0)
    place = (cols == rows + shard * SR).astype(BF)
    for cp in load_first:
        cp.wait()
    gm[...] = jnp.zeros_like(gm)
    gm[0:1, :] = dot_nn(r["gain_a_own"][...], place)
    gm[1:2, :] = dot_nn(r["gain_f_own"][...], place)
    wqkv[own_rows, :] = (dot_nn(r["wq_own"][...], spot(W, 0)) + dot_nn(r["wk_own"][...], spot(W, HP))
                         + dot_nn(r["wv_own"][...], spot(W, HP + H))).astype(BF)
    load_out.wait()
    woz[t] = dot_nn(r["wo_own"][...], spot(HP, 0)).astype(BF)
    for cp in load_ffn:
        cp.wait()
    pl.semaphore_wait(bar, len(group) + NT - 1)

    sends, weight_sends = [], []

    def send(src, dst, idx, dev, group=None):
        cp = copy_to(src, dst, idx, dev)
        cp.start()
        (sends if group is None else group).append(cp)
        return cp

    def rows_of(off):
        pf, pc = square_from(off)
        return at((pf * C + pc) * SR, SR)

    class Spread:
        def __init__(self, buf, view, far, group):
            self.buf, self.view, self.far, self.group = buf, view, far, group
            self.ix = {off: slot() for off in offsets}
            self.px = slot()
            self.rx = {off: slot() for off in offsets}

        def rows(self, off):
            return self.view(self.buf, rows_of(off))

        def start(self):
            w = self.view(self.buf, own_rows)
            for off in offsets:
                if self.far or 0 in off:
                    send(w, w, self.ix[off], dev_sq(off), self.group)
            send(w, w, self.px, partner, self.group)

        def relay_x(self):
            w = self.rows((0, 1))
            copy_to(w, w, self.ix[(0, 1)], partner).wait_recv()
            if not self.far:
                send(w, w, self.ix[(1, 1)], dev_sq((1, 0)), self.group)
            send(w, w, self.rx[(0, 1)], partner, self.group)

        def relay_y(self):
            for off in ((1, 0), (1, 1)):
                w = self.rows(off)
                copy_to(w, w, self.ix[off], partner).wait_recv()
                send(w, w, self.rx[off], partner, self.group)

        def finish(self):
            w = self.view(self.buf, own_rows)
            copy_to(w, w, self.px, partner).wait_recv()
            for off in offsets:
                copy_to(w, w, self.rx[off], partner).wait_recv()

    flat = lambda buf, rows: buf.at[rows]
    deep = lambda buf, rows: buf.at[:, rows]
    gall = r["gall"]
    gain_cp = [send(gm, gall.at[n], slot(), dev_group(off)) for n, off in enumerate(group)]
    qkv_sp = Spread(wqkv, flat, True, sends)
    qkv_sp.start()
    twin_ix = {}
    for k, buf in (("g", wg), ("u", wu), ("d", wd)):
        twin_ix[k] = slot()
        send(buf.at[0, own_rows], buf.at[1, own_rows], twin_ix[k], twin, weight_sends)
    spreads = {k + str(n): Spread(b.at[n], flat, False, weight_sends) for n in range(2) for k, b in (("g", wg), ("u", wu), ("d", wd))}
    spreads["o"] = Spread(wo, flat, False, sends)
    for k in "gud":
        spreads[k + "0"].start()
    wo_ix = [slot() for _ in range(1, NT)]
    for k, i in zip(range(1, NT), wo_ix):
        send(woz.at[t], woz.at[t], i, z_to(k))
    segr, segc = r["segr"].at[:, 0], r["segc"]
    gains, gacc, oT, oX = r["gains"], r["gacc"], r["oT"], r["oX"]
    tok, cot, n1 = r["tok"], r["cot"], r["n1"]

    def prepare():
        for m in range(MICRO):
            for b in range(L // 128):
                row = segr[m:m + 1, 128 * b:128 * b + 128].astype(F32)
                segc[m, 128 * b:128 * b + 128, :] = jnp.broadcast_to(row, (128, 128)).T.astype(jnp.int32)
        for cp in gain_cp:
            cp.wait_recv()
        gsum = gm[...]
        for n in range(len(group)):
            gsum = gsum + gall[n]
        gains[...] = gsum
        load_tok.wait()
        for m in range(MICRO):
            norm_one(m)
        gacc[...] = jnp.zeros_like(gacc)

    def norm_one(m):
        @pl.loop(0, R // CH)
        def _(i):
            xf = tok[m, at(i * CH, CH), :].astype(F32)
            rs = lax.rsqrt(jnp.mean(xf * xf, -1, keepdims=True) + EPS)
            n1[at(m * R + i * CH, CH), :] = (xf * rs * gains[0:1, :]).astype(BF)

    q, kv, kvT = r["q"], r["kv"], r["kvT"]
    scale = HEAD_DIM ** -0.5
    def qkv_ready():
        qkv_sp.relay_x()
        qkv_sp.relay_y()
        qkv_sp.finish()

    kv_ix = [slot() for _ in range(MICRO)]
    other = {"ctx": lax.rem(c + 1, C)}

    def project(m):
        @pl.loop(0, R // RT)
        def _(i):
            acc = dot_nn(n1[at(m * R + i * RT, RT), :], wqkv[...])
            q[m, at(i * RT, RT), :] = (acc[:, 0:HP] * scale).astype(BF)
            kv[m, at(c * R + i * RT, RT), :] = acc[:, HP:HP + KV].astype(BF)
        w = kv.at[m, at(c * R, R)]
        send(w, w, kv_ix[m], other)
        flip(m, c * R)

    def spread(w):
        if w == "o":
            for k, i in zip(range(1, NT), wo_ix):
                copy_to(woz.at[t], woz.at[t], i, z_to(k)).wait_recv()
            i = lax.broadcasted_iota(jnp.int32, (HP, D), 0)
            j = lax.broadcasted_iota(jnp.int32, (HP, D), 1)
            row = dot_nn(woz[0], (j == i).astype(BF))
            for k in range(1, NT):
                row = row + dot_nn(woz[k], (j == i + k * H).astype(BF))
            wo[own_rows, :] = row.astype(BF)
        else:
            v = {"g": wg, "u": wu, "d": wd}[w[0]].at[0, own_rows]
            copy_to(v, v, twin_ix[w[0]], twin).wait_recv()
        spreads[w].start()

    def weights_ready(n):
        for k in ["o"] if n == "o" else [w + str(n) for w in "gud"]:
            spreads[k].finish()

    onat, lse = r["onat"], r["lse"]
    lanes = lax.broadcasted_iota(jnp.int32, (RT, HP), 1)

    def head_mask(v, h, shift):
        lo = shift + h * HEAD_DIM
        return jnp.where((lanes >= lo) & (lanes < lo + HEAD_DIM), v, jnp.zeros_like(v))

    def flip(m, start):
        @pl.loop(0, R // RT)
        def _(i):
            kvT[m, :, at(start + i * RT, RT)] = kv[m, at(start + i * RT, RT), :].T

    def attend(m, i):
        kk = kv[m, :, 0:HP]
        sc = segc[m]
        sc = jnp.concatenate([sc] * (RT // 128), axis=1)
        sr = segr[m:m + 1, at(c * R + i * RT, RT)]
        qq = q[m, pl.ds(i * RT, RT), :]
        for h in range(NH):
            s = dot_nt(kk, head_mask(qq, h, 0))
            s = jnp.where(sc == sr, s, NEG)
            mx = jnp.max(s, axis=0, keepdims=True)
            e = jnp.exp(s - mx)
            tot = jnp.sum(e, axis=0, keepdims=True)
            p = (e * (1.0 / tot)).astype(BF)
            vT = kvT[m, H + h * HEAD_DIM:H + (h + 1) * HEAD_DIM, :]
            lo = VOFF + h * HEAD_DIM
            oT[m, lo:lo + HEAD_DIM, pl.ds(i * RT, RT)] = dot_nn(vT, p).astype(BF)
            lse[m, h, :, pl.ds(i * RT, RT)] = mx + jnp.log(tot)

    o_ix = [[slot() for _ in range(3)] for _ in range(MICRO)]

    def o_send(m, i, n):
        src = oT.at[m, pl.ds(VOFF, H), pl.ds(i * HR, HR)]
        return copy_to(src, oX.at[m, at(t * H, H)], o_ix[m][n], (mate, twin, cross)[n])

    def share_o(m, i):
        @pl.when(half == i)
        def _():
            o_send(m, i, 0).start()

        @pl.when(half != i)
        def _():
            o_send(m, i, 1).start()
            o_send(m, i, 2).start()

    def wait_o(m):
        for n in range(3):
            o_send(m, 0, n).wait_recv()

    def close_o(m):
        for n in range(3):
            o_send(m, 0, n).wait_send()

    def attend_tile(m, i):
        if i == 0:
            w = kv.at[m, at(c * R, R)]
            copy_to(w, w, kv_ix[m], other).wait_recv()
            flip(m, lax.rem(c + 1, C) * R)
        attend(m, i)
        share_o(m, i)

    y1, n2, big, dy = r["y1"], r["n2"], r["big"], r["dy"]
    d2s, d2r, fps, fpr = r["d2s"], r["d2r"], r["fps"], r["fpr"]
    d2_ix = [[slot() for _ in range(SUB)] for _ in range(MICRO)]
    fp_ix = [[slot() for _ in range(SUB)] for _ in range(MICRO)]

    def to_mate(src, dst, ix, m, j):
        rr = pl.ds(j * CH, CH)
        return copy_to(src.at[m, rr], dst.at[m, rr], ix[m][j], mate)

    def feed(m):
        oX[m, at(t * H, H), :] = oT[m, VOFF:HP, hrows]
        mr = pl.ds(m * HR, HR)
        onat[mr, :] = oX[m].T
        acc = tok[m, hrows, :].astype(F32)
        acc = acc + dot_nt(onat[mr, :], wo[...])
        y1[m] = acc
        rs = lax.rsqrt(jnp.mean(acc * acc, -1, keepdims=True) + EPS)
        n2[mr, :] = (acc * rs * gains[1:2, :]).astype(BF)

    def feed_slot(m, n):
        if (m, n) == fed[0]:
            for cp in load_cot:
                cp.wait()
        mr = pl.ds(m * HR, HR)
        n2v = n2[mr, :]
        g = dot_nn(n2v, wg[n])
        u = dot_nn(n2v, wu[n])
        th = jnp.tanh(GELU_K * (g + GELU_A * g * g * g))
        hf = 0.5 * (1.0 + th)
        gl = g * hf
        big[0, n, mr, :] = (gl * u).astype(BF)
        dh = dot_nn(cot[mr, :], wd[n])
        dgl = hf + 0.5 * g * (1.0 - th * th) * (GELU_K * (1.0 + 3.0 * GELU_A * g * g))
        dgv = (dh * u * dgl).astype(BF)
        duv = (dh * gl).astype(BF)
        big[1, n, mr, :] = dgv
        big[2, n, mr, :] = duv
        d2 = dot_nt(dgv, wg[n]) + dot_nt(duv, wu[n])
        if n == 0:
            dy[m] = d2
            return
        d2 = dy[m] + d2
        d2s[m] = d2.astype(BF)

        @pl.when(outer)
        def _():
            for j in range(SUB):
                to_mate(d2s, d2r, d2_ix, m, j).start()

        yn = y1[m]
        rs = lax.rsqrt(jnp.mean(yn * yn, -1, keepdims=True) + EPS)
        gacc[1:2, :] += jnp.sum(d2 * (yn * rs), axis=0, keepdims=True)
        fps[m] = (dot_nt(big[0, 0, mr, :], wd[0]) + dot_nt(big[0, 1, mr, :], wd[1])).astype(BF)

    def feed_out(m):
        @pl.when(outer)
        def _():
            for j in range(SUB):
                to_mate(fps, fpr, fp_ix, m, j).start()

    class Reduce:
        def __init__(self, k, pieces, put):
            self.own, self.half, self.recv, self.parts = r["own_" + k], r["st_" + k], r["rv_" + k], r["pt_" + k]
            self.pieces, self.put = pieces, put
            self.px = slot()
            self.ix = [slot() for _ in offsets]

        def pair_copy(self):
            return copy_to(self.half, self.recv, self.px, partner)

        def pair(self):
            tmp = r["tmp"]
            for left, right, c0, width in self.pieces:
                @pl.loop(0, D // RT)
                def _(i, left=left, right=right, c0=c0, width=width):
                    tmp[:, 0:width] = dot_tn(left[:, at(i * RT, RT)], right[...])

                    @pl.loop(0, RT // UNIT)
                    def _(p):
                        row = i * RT + p * UNIT
                        b = row // (C * SR)
                        to = at((b // 2) * C * SR + lax.rem(row, C * SR), UNIT)
                        part = tmp[at(p * UNIT, UNIT), 0:width]

                        @pl.when(lax.rem(b, 2) == core)
                        def _():
                            self.own[to, c0:c0 + width] = part

                        @pl.when(lax.rem(b, 2) != core)
                        def _():
                            self.half[to, c0:c0 + width] = part.astype(BF)
            self.pair_copy().start()

        def block(self, n):
            pf, pc = square(offsets[n])
            src = self.half.at[at(((pf // 2) * C + pc) * SR, SR)]
            return copy_to(src, self.parts.at[n], self.ix[n], dev_sq(offsets[n]))

        def square(self):
            self.pair_copy().wait()
            tot = self.own[...] + self.recv[...].astype(F32)
            self.own[...] = tot
            self.half[...] = tot.astype(BF)
            for n in range(len(offsets)):
                self.block(n).start()

        def finish(self):
            tot = self.own[at((y * C + c) * SR, SR), :]
            for n in range(len(offsets)):
                self.block(n).wait()
            for n in range(len(offsets)):
                tot = tot + self.parts[n].astype(F32)
            self.put(tot)

    zs_ix = {k: slot() for k in "gud"}

    def twin_sum(k):
        def put(tot):
            r["fin_" + k][...] = tot[:, 0:FF]
            r["zs_" + k][...] = tot[:, FF:2 * FF].astype(BF)
            send(r["zs_" + k], r["zr_" + k], zs_ix[k], twin)
        return put

    def split_qkv(tot):
        r["fin_qkv"][0] = tot[:, 0:H]
        r["fin_qkv"][1] = tot[:, HP:HP + H]
        r["fin_qkv"][2] = pltpu.roll(tot[:, W - HP:W], HP - VOFF, 1)[:, 0:H]
        for n, k in enumerate("qkv"):
            store(r["fin_qkv"].at[n], r["out_" + k])

    zo, zq = r["zo"], r["zq"]
    zo_ix, zo_sx = [slot(), slot()], slot()

    def zo_copies():
        out = []
        for dev, ix, sx in ((mate, zo_ix[0], None), (twin, zo_ix[1], None), (cross, zo_ix[1], zo_sx)):
            out.append(copy_to(zq.at[dev["tp"]], zo.at[half], ix, dev, sx))
        return out

    def out_sum(tot):
        for k in range(NT):
            base = k * H // 128 * 128
            part = tot[:, base:base + HP]
            zq[k] = (pltpu.roll(part, HP - (k * H - base), 1) if k * H > base else part).astype(BF)
        zo[half] = zq[t]
        for cp in zo_copies():
            cp.start()

    dqkv, ar = r["dqkv"], r["ar"]
    pieces = {
        "d": [(cot, big.at[0, n], n * FF, FF) for n in range(2)],
        "g": [(n2, big.at[1, n], n * FF, FF) for n in range(2)],
        "u": [(n2, big.at[2, n], n * FF, FF) for n in range(2)],
        "q": [(n1, dqkv.at[:, pl.ds(0, 512)], 0, 512), (n1, dqkv.at[:, pl.ds(512, W - 512)], 512, W - 512)],
        "o": [(ar, onat.at[:, pl.ds(0, 512)], 0, 512), (ar, onat.at[:, pl.ds(512, D - 512)], 512, D - 512)],
    }
    puts = {"d": twin_sum("d"), "g": twin_sum("g"), "u": twin_sum("u"), "q": split_qkv, "o": out_sum}
    reds = {k: Reduce(k, pieces[k], puts[k]) for k in "dguqo"}

    def reduce_step(k, what):
        if k == "o":
            pl.when(inner)(lambda: getattr(reds[k], what)())
        else:
            getattr(reds[k], what)()

    def last_sum(k):
        if k == "o":
            both(lambda: zo_copies()[1].wait_recv(), lambda: [cp.wait_recv() for cp in zo_copies()[:2]] and None)
            tot = zo[0].astype(F32) + zo[1].astype(F32)
            r["fin_o"][...] = tot[:, 0:H]
            store(r["fin_o"], r["out_o"])
        elif k != "q":
            copy_to(r["zs_" + k], r["zr_" + k], zs_ix[k], twin).wait_recv()
            r["fin_" + k][...] += r["zr_" + k][...].astype(F32)
            store(r["fin_" + k], r["out_" + k])

    doT, doS = r["doT"], r["doS"]
    do_ix = [[[slot(), slot()] for _ in range(SUB)] for _ in range(MICRO)]
    do_sx = [[slot() for _ in range(SUB)] for _ in range(MICRO)]

    def do_copies(m, j):
        out = []
        to = doT.at[m, pl.ds(VOFF, H), pl.ds(pl.multiple_of(half * HR + j * CH, CH), CH)]
        for dev, n, sx in ((mate, 0, None), (twin, 1, None), (cross, 1, do_sx[m][j])):
            src = doS.at[at(dev["tp"] * H, H), pl.ds(j * CH, CH)]
            out.append(copy_to(src, to, do_ix[m][j][n], dev, sx))
        return out

    def back_norm(m, j):
        @pl.when(inner)
        def _():
            to_mate(d2s, d2r, d2_ix, m, j).wait_recv()
            if m:
                for cp in do_copies(m - 1, j):
                    cp.wait_send()
            rr = pl.ds(j * CH, CH)
            gr = pl.ds(m * HR + j * CH, CH)
            yv = y1[m, rr, :]
            d2 = d2s[m, rr, :].astype(F32) + d2r[m, rr, :].astype(F32)
            tv = lax.rsqrt(jnp.mean(yv * yv, -1, keepdims=True) + EPS)
            e2 = gains[1:2, :] * d2
            dot = jnp.mean(yv * e2, -1, keepdims=True)
            dv = cot[gr, :].astype(F32) + tv * e2 - yv * (tv * tv * tv * dot)
            dy[m, rr, :] = dv
            av = dv.astype(BF)
            ar[gr, :] = av
            doS[:, rr] = dot_nn(av, wo[...]).astype(BF).T
            doT[m, VOFF:HP, pl.ds(pl.multiple_of(half * HR + j * CH, CH), CH)] = doS[at(t * H, H), rr]
            for cp in do_copies(m, j):
                cp.start()

    delta, dqT, dkv_in, dkv_own = r["delta"], r["dqT"], r["dkv_in"], r["dkv_own"]
    dkv_out = wg.at[:, pl.ds(0, R), pl.ds(0, KV)]
    lay = [(0, 0), (0, HP), (1, 0)]
    qm = [wd.at[a, pl.ds(0, R), pl.ds(b, HP)] for a, b in lay]
    dom = [wu.at[a, pl.ds(0, R), pl.ds(b, HP)] for a, b in lay]

    def back_start(m):
        if m == 0:
            for cp in weight_sends:
                cp.wait_send()
        for j in range(SUB):
            cps = do_copies(m, j)
            both(lambda: cps[1].wait_recv(), lambda: [cp.wait_recv() for cp in cps[:2]] and None)

        @pl.loop(0, R // RT)
        def _(i):
            rr = at(i * RT, RT)
            dov = doT[m, :, rr].T
            for h in range(NH):
                lo = VOFF + h * HEAD_DIM
                prod = doT[m, lo:lo + HEAD_DIM, rr].astype(F32) * oT[m, lo:lo + HEAD_DIM, rr].astype(F32)
                delta[h, :, rr] = jnp.sum(prod, axis=0, keepdims=True)
                dom[h][rr, :] = head_mask(dov, h, VOFF)
                qm[h][rr, :] = head_mask(q[m, rr, :], h, 0)

    def back_half(m, key0, first):
        @pl.loop(0, R // RT)
        def _(i):
            sc = segc[m, at(key0, R), :]
            sc = jnp.concatenate([sc] * (RT // 128), axis=1)
            sr = segr[m:m + 1, at(c * R + i * RT, RT)]
            cs = at(i * RT, RT)
            for h in range(NH):
                s = dot_nt(kv[m, at(key0, R), 0:HP], qm[h][cs, :])
                s = jnp.where(sc == sr, s, NEG)
                p = jnp.exp(s - lse[m, h, :, cs])
                dp = dot_nt(kv[m, at(key0, R), KV - HP:KV], dom[h][cs, :])
                big[h, 1, :, cs] = p.astype(BF)
                big[h, 0, :, cs] = (p * (dp - delta[h, :, cs])).astype(BF)

        dst = dkv_out if first else dkv_own

        @pl.loop(0, R // RT)
        def _(i):
            rr = at(i * RT, RT)
            dk = dot_nn(big[0, 0, rr, :], qm[0][...])
            dv = dot_nn(big[0, 1, rr, :], dom[0][...])
            for h in range(1, NH):
                dk = dk + dot_nn(big[h, 0, rr, :], qm[h][...])
                dv = dv + dot_nn(big[h, 1, rr, :], dom[h][...])
            dst[m, rr, 0:128] = dk[:, 0:128].astype(dst.dtype)
            dst[m, rr, 128:256] = (dk[:, 128:256] + dv[:, 0:128]).astype(dst.dtype)
            dst[m, rr, 256:384] = dv[:, 128:256].astype(dst.dtype)
        for h in range(NH):
            hs = pl.ds(h * HEAD_DIM, HEAD_DIM)
            part = dot_nn(kvT[m, hs, at(key0, R)], big[h, 0])
            if first:
                dqT[hs, :] = part
            else:
                dqT[hs, :] = dqT[hs, :] + part

    dkv_ix = [slot() for _ in range(MICRO)]

    def back_peer(m):
        back_half(m, lax.rem(c + 1, C) * R, True)
        send(dkv_out.at[m], dkv_in.at[m], dkv_ix[m], other)

    def back_own(m):
        back_half(m, c * R, False)
        dqkv[pl.ds(m * R, R), 0:HP] = jnp.zeros((R, HP), BF)
        dqkv[pl.ds(m * R, R), 0:H] = (dqT[...] * scale).T.astype(BF)

    snd, rc1, rc2, igb = r["snd"], r["rc1"], r["rc2"], r["igb"]
    in_ix = [[[slot() for _ in range(SUB)] for _ in range(2)] for _ in range(MICRO)]
    sw_ix = [[slot() for _ in range(SUB)] for _ in range(MICRO)]

    def piece(own, j):
        return pl.ds(pl.multiple_of((half if own else 1 - half) * HR + j * CH, CH), CH)

    def inward(m, own, j):
        rr = piece(own, j)
        return copy_to(snd.at[m, rr], rc1.at[m, rr], in_ix[m][own][j], mate)

    def swap(m, j):
        return copy_to(snd.at[m, piece(0, j)], rc2.at[m, pl.ds(j * CH, CH)], sw_ix[m][j], cross)

    def join(m):
        copy_to(dkv_out.at[m], dkv_in.at[m], dkv_ix[m], other).wait_recv()
        for own in range(2):
            base = (half if own else 1 - half) * HR
            rr = at(base, HR)
            gr = pl.ds(pl.multiple_of(m * R + base, HR), HR)
            dqkv[gr, HP:HP + KV] = (dkv_own[m, rr, :] + dkv_in[m, rr, :].astype(F32)).astype(BF)
            d1 = dot_nt(dqkv[gr, :], wqkv[...])
            snd[m, rr, :] = d1.astype(BF)

            @pl.when(outer)
            def _(own=own):
                for j in range(SUB):
                    inward(m, own, j).start()

            xv = tok[m, rr, :].astype(F32)
            rs = lax.rsqrt(jnp.mean(xv * xv, -1, keepdims=True) + EPS)
            gacc[0:1, :] += jnp.sum(d1 * (xv * rs), axis=0, keepdims=True)

    def cross_over(m, j):
        @pl.when(inner)
        def _():
            inward(m, 0, j).wait_recv()
            rr = piece(0, j)
            snd[m, rr, :] = (snd[m, rr, :].astype(F32) + rc1[m, rr, :].astype(F32)).astype(BF)
            swap(m, j).start()

    class Result:
        def __init__(self, buf, name):
            self.buf, self.name = buf, name
            self.ix = [[[slot() for _ in range(3)] for _ in range(SUB)] for _ in range(MICRO)]

        def copy(self, m, j, n):
            at_ = self.buf.at[m, piece(n != 2, j)]
            return copy_to(at_, at_, self.ix[m][j][n], cross if n == 1 else mate)

        def arrived(self, m, j, n):
            at_ = self.buf.at[m, piece(0, j)]
            copy_to(at_, at_, self.ix[m][j][n], mate).wait_recv()

        def store(self, m, j, own):
            rr = piece(own, j)
            store(self.buf.at[m, rr], r[self.name].at[m, 0, rr])

        def near(self, m, j, make):
            def one():
                make(m, j)
                self.copy(m, j, 1).start()
                self.copy(m, j, 0).start()
            both(one, lambda: self.arrived(m, j, 0))
            self.store(m, j, 1)

        def far(self, m, j):
            def one():
                self.arrived(m, j, 1)
                self.copy(m, j, 2).start()
            both(one, lambda: self.arrived(m, j, 2))
            self.store(m, j, 0)

        def close(self, m, j):
            @pl.when(inner)
            def _():
                for n in range(3):
                    self.copy(m, j, n).wait_send()

    stores = []

    def store(src, dst):
        cp = pltpu.make_async_copy(src, dst, local.at[12 + len(stores)])
        cp.start()
        stores.append(cp)

    def make_output(m, j):
        to_mate(fps, fpr, fp_ix, m, j).wait_recv()
        rr = pl.ds(j * CH, CH)
        tot = y1[m, rr, :] + (fps[m, rr, :].astype(F32) + fpr[m, rr, :].astype(F32))
        r["outv"][m, piece(1, j), :] = tot.astype(BF)

    def make_input_grad(m, j):
        inward(m, 1, j).wait_recv()
        swap(m, j).wait_recv()
        rr = pl.ds(j * CH, CH)
        here = piece(1, j)
        xv = tok[m, here, :].astype(F32)
        d1 = snd[m, here, :].astype(F32) + rc1[m, here, :].astype(F32) + rc2[m, rr, :].astype(F32)
        tv = lax.rsqrt(jnp.mean(xv * xv, -1, keepdims=True) + EPS)
        e1 = gains[0:1, :] * d1
        dot = jnp.mean(xv * e1, -1, keepdims=True)
        igb[m, here, :] = (dy[m, rr, :] + tv * e1 - xv * (tv * tv * tv * dot)).astype(BF)

    out_res, ig_res = Result(r["outv"], "out"), Result(igb, "ig")

    gz, gz_ix = r["gz"], [slot() for _ in range(NT)]
    gin, gpart = r["gin"], r["gpart"]
    gain_ix = [slot() for _ in group]

    def gain_z():
        for k in range(1, NT):
            send(gacc, gz.at[k], gz_ix[k], z_to(k))

    def gain_group():
        for k in range(1, NT):
            copy_to(gacc, gz.at[k], gz_ix[k], z_to(k)).wait_recv()
        tot = gacc[...]
        for k in range(1, NT):
            tot = tot + gz[k]
        gpart[...] = tot
        for n, off in enumerate(group):
            send(gpart, gin.at[n], gain_ix[n], dev_group(off))

    def gain_final():
        for n, off in enumerate(group):
            copy_to(gpart, gin.at[n], gain_ix[n], dev_group(off)).wait_recv()
        tot = gpart[...]
        for n in range(len(group)):
            tot = tot + gin[n]
        tot = lax.dot_general(
            tot, place.astype(F32), (((1,), (1,)), ((), ())), precision=lax.Precision.HIGHEST,
            preferred_element_type=F32)
        r["fin_gain"][0] = tot[0:1, :]
        r["fin_gain"][1] = tot[1:2, :]
        store(r["fin_gain"].at[0], r["out_ga"])
        store(r["fin_gain"].at[1], r["out_gf"])

    fed = [step[1:] for step in ORDER if step[0] == "FS"]
    acts = {
        "prep": prepare, "qR": qkv_ready, "wF": weights_ready, "P": project, "wS": spread,
        "wX": lambda w: spreads[w].relay_x(), "wY": lambda w: spreads[w].relay_y(), "AT": attend_tile,
        "O": wait_o, "F1": feed, "FS": feed_slot, "FP": feed_out, "G": lambda k: reduce_step(k, "pair"), "SQ": lambda k: reduce_step(k, "square"),
        "SF": lambda k: reduce_step(k, "finish"), "SZ": last_sum, "BN": back_norm, "BS": back_start,
        "PE": back_peer, "OW": back_own, "J": join, "X": cross_over,
        "ON": lambda m, j: out_res.near(m, j, make_output), "OF": out_res.far,
        "IN": lambda m, j: ig_res.near(m, j, make_input_grad), "IF": ig_res.far,
        "GZ": gain_z, "GR": gain_group, "GF": gain_final,
    }
    for step in ORDER:
        acts[step[0]](*step[1:])
    for cp in stores:
        cp.wait()
    for cp in sends:
        cp.wait_send()
    for m in range(MICRO):
        close_o(m)
        for j in range(SUB):
            out_res.close(m, j)
            ig_res.close(m, j)

            def inner_done(m=m, j=j):
                if m == MICRO - 1:
                    for cp in do_copies(m, j):
                        cp.wait_send()
                swap(m, j).wait_send()

            def outer_done(m=m, j=j):
                to_mate(d2s, d2r, d2_ix, m, j).wait_send()
                to_mate(fps, fpr, fp_ix, m, j).wait_send()
                inward(m, 0, j).wait_send()
                inward(m, 1, j).wait_send()

            both(inner_done, outer_done)

    @pl.when(inner)
    def _():
        for cp in zo_copies():
            cp.wait_send()

    assert counter[0] <= ssem.shape[0]


def fused_shards(dims, tokens, segments, cotangent, query_weight, key_weight, value_weight, out_weight,
                 gate_weight, up_weight, down_weight, attn_gain, ffn_gain):
    R, D, H, FF, C, NF, NT, MICRO = dims
    L = C * R
    SR = D // (NF * C)
    NH = H // HEAD_DIM
    HP, KV, Y = 256, 2 * H, NF // 2
    HALF = Y * C * SR
    NO = Y * C - 1
    NG = NF * C - 1
    W = HP + KV
    ins = [
        ("tok_in", tokens.reshape(MICRO, R, D)),
        ("segr", segments),
        ("cot_in", cotangent.reshape(MICRO, R, D)),
        ("wq_in", query_weight),
        ("wk_in", key_weight),
        ("wv_in", value_weight),
        ("wo_in", out_weight),
        ("wg_in", gate_weight),
        ("wu_in", up_weight),
        ("wd_in", down_weight),
        ("gain_a_in", attn_gain[None]),
        ("gain_f_in", ffn_gain[None]),
    ]
    outs = [
        ("out", (MICRO, 1, R, D), BF),
        ("ig", (MICRO, 1, R, D), BF),
        ("out_q", (SR, H), F32),
        ("out_k", (SR, H), F32),
        ("out_v", (SR, H), F32),
        ("out_o", (SR, H), F32),
        ("out_g", (SR, FF), F32),
        ("out_u", (SR, FF), F32),
        ("out_d", (SR, FF), F32),
        ("out_ga", (1, SR), F32),
        ("out_gf", (1, SR), F32),
    ]
    v = pltpu.VMEM
    HR = R // 2
    scratch = [
        ("tok", v((MICRO, R, D), BF)), ("cot", v((MICRO * HR, D), BF)), ("dy", v((MICRO, HR, D), F32)),
        ("outv", v((MICRO, R, D), BF)), ("igb", v((MICRO, R, D), BF)),
        ("gz", v((NT, 2, D), F32)), ("gpart", v((2, D), F32)),
        ("lsem", pltpu.SemaphoreType.DMA((48,))),
        ("gmine", v((2, D), F32)), ("gall", v((NG, 2, D), F32)), ("gains", v((2, D), F32)),
        ("gacc", v((2, D), F32)), ("gin", v((NG, 2, D), F32)),
        ("wqkv", v((D, W), BF)), ("wo", v((D, D), BF)), ("woz", v((NT, SR, HP), BF)),
        ("wg", v((2, D, FF), BF)), ("wu", v((2, D, FF), BF)), ("wd", v((2, D, FF), BF)),
        ("segc", v((MICRO, L, 128), jnp.int32)),
        ("n1", v((MICRO * R, D), BF)), ("q", v((MICRO, R, HP), BF)),
        ("kv", v((MICRO, L, KV), BF)), ("kvT", v((MICRO, KV, L), BF)),
        ("oT", v((MICRO, HP, R), BF)), ("oX", v((MICRO, D, HR), BF)), ("onat", v((MICRO * HR, D), BF)),
        ("lse", v((MICRO, NH, 1, R), F32)),
        ("d2s", v((MICRO, HR, D), BF)), ("d2r", v((MICRO, HR, D), BF)),
        ("fps", v((MICRO, HR, D), BF)), ("fpr", v((MICRO, HR, D), BF)),
        ("snd", v((MICRO, R, D), BF)), ("rc1", v((MICRO, R, D), BF)), ("rc2", v((MICRO, HR, D), BF)),
        ("y1", v((MICRO, HR, D), F32)), ("n2", v((MICRO * HR, D), BF)), ("ar", v((MICRO * HR, D), BF)),
        ("big", v((3, 2, R, FF), BF)),
        ("doT", v((MICRO, HP, R), BF)), ("doS", v((D, HR), BF)),
        ("delta", v((NH, 1, R), F32)), ("dqT", v((H, R), F32)), ("dqkv", v((MICRO * R, W), BF)),
        ("dkv_own", v((MICRO, R, KV), F32)), ("dkv_in", v((MICRO, R, KV), BF)),
        ("gain_a_own", v((1, SR), BF)), ("gain_f_own", v((1, SR), BF)), ("fin_gain", v((2, 1, SR), F32)),
        ("wq_own", v((SR, H), BF)), ("wk_own", v((SR, H), BF)), ("wv_own", v((SR, H), BF)), ("wo_own", v((SR, H), BF)),
        ("fin_g", v((SR, FF), F32)), ("fin_u", v((SR, FF), F32)), ("fin_d", v((SR, FF), F32)),
        ("fin_qkv", v((3, SR, H), F32)), ("fin_o", v((SR, H), F32)),
        ("tmp", v((256, 512), F32)), ("zo", v((2, SR, HP), BF)), ("zq", v((NT, SR, HP), BF)),
    ]
    for k, cols in (("q", W), ("o", D), ("g", 2 * FF), ("u", 2 * FF), ("d", 2 * FF)):
        scratch += [("own_" + k, v((HALF, cols), F32)), ("rv_" + k, v((HALF, cols), BF)),
                    ("st_" + k, v((HALF, cols), BF)), ("pt_" + k, v((NO, SR, cols), BF))]
    for k in "gud":
        scratch += [("zs_" + k, v((SR, FF), BF)), ("zr_" + k, v((SR, FF), BF))]
    nsem = 320
    scratch += [("ssem", pltpu.SemaphoreType.DMA((nsem,))), ("rsem", pltpu.SemaphoreType.DMA((nsem,)))]
    names = [n for n, _ in ins] + [n for n, _, _ in outs] + [n for n, _ in scratch]
    def spec(name):
        return pl.BlockSpec(memory_space=pltpu.VMEM if name == "segr" else pl.ANY)

    res = pl.pallas_call(
        functools.partial(layer_kernel, dims, names),
        out_shape=[jax.ShapeDtypeStruct(s, d) for _, s, d in outs],
        in_specs=[spec(n) for n, _ in ins],
        out_specs=[spec(n) for n, _, _ in outs],
        scratch_shapes=[s for _, s in scratch],
        compiler_params=pltpu.CompilerParams(
            collective_id=0, has_side_effects=True, vmem_limit_bytes=67043328),
    )(*[a for _, a in ins])
    res = settle(res)
    return tuple(res[:9]) + (res[9].reshape(SR), res[10].reshape(SR))


def settle(arrays):
    pieces = []
    for n, a in enumerate(arrays):
        if a.ndim == 4:
            pieces += [(n, (m, 0, pl.ds(k * 256, 256))) for m in range(a.shape[0]) for k in range(a.shape[2] // 256)]
        else:
            pieces.append((n, None))

    kinds = [F32] * len(arrays)
    kinds[0] = arrays[0].dtype
    wide = [n for n, a in enumerate(arrays) if a.dtype != kinds[n]]

    def kernel(*refs):
        k = len(arrays)
        src, dst, buf, sem = refs[:k], refs[k:2 * k], refs[2 * k:3 * k], refs[3 * k:]
        last = list(buf)
        for i, n in enumerate(wide):
            last[n] = sem[2 + i]
        pick = lambda ref, at: ref if at is None else ref.at[at]
        come = [pltpu.make_async_copy(pick(src[n], at), pick(buf[n], at), sem[0].at[i]) for i, (n, at) in enumerate(pieces)]
        go = [pltpu.make_async_copy(pick(last[n], at), pick(dst[n], at), sem[1].at[i]) for i, (n, at) in enumerate(pieces)]
        for cp in come:
            cp.start()
        for a, b, (n, at) in zip(come, go, pieces):
            a.wait()
            if n in wide:
                last[n][at] = buf[n][at].astype(F32)
            b.start()
        for cp in go:
            cp.wait()

    hbm = pl.BlockSpec(memory_space=pl.ANY)
    return pl.pallas_call(
        kernel,
        out_shape=[jax.ShapeDtypeStruct(a.shape, d) for a, d in zip(arrays, kinds)],
        in_specs=[hbm] * len(arrays),
        out_specs=[hbm] * len(arrays),
        scratch_shapes=[pltpu.VMEM(a.shape, a.dtype) for a in arrays] + [pltpu.SemaphoreType.DMA((len(pieces),))] * 2
        + [pltpu.VMEM(arrays[n].shape, F32) for n in wide],
    )(*arrays)


def fits(dims, seqs):
    R, D, H, FF, C, NF, NT, MICRO = dims
    blocks = D % (16 * NF * C) == 0 and D % 256 == 0
    return (C, NT, NF, H, MICRO, seqs, R, FF) == (2, 4, 4, 192, 2, 1, 512, 512) and D <= 768 and blocks


SPECS = (
    P(None, "fsdp", "ctx", None),
    P(None, "fsdp", None),
    P(None, "fsdp", "ctx", None),
) + (P(("fsdp", "ctx"), "tp"),) * 7 + (P(("fsdp", "ctx")),) * 2
OUT_SPECS = (P(None, "fsdp", "ctx", None),) * 2 + (P(("fsdp", "ctx"), "tp"),) * 7 + (P(("fsdp", "ctx")),) * 2


def solution(mesh):
    nf, nc, nt = mesh.shape["fsdp"], mesh.shape["ctx"], mesh.shape["tp"]

    def chosen(*args):
        tokens, weight, ffw = args[0], args[3], args[7]
        micro, seqs, rows, width = tokens.shape
        dims = (rows, width, weight.shape[1], ffw.shape[1], nc, nf, nt, micro)
        return fused_shards(dims, *args) if fits(dims, seqs) else shards(*args)

    return jax.shard_map(chosen, mesh=mesh, in_specs=SPECS, out_specs=OUT_SPECS, check_vma=False)
```

```python
import functools

import jax
import jax.numpy as jnp
from jax import lax
from jax.experimental import pallas as pl
from jax.experimental.pallas import tpu as pltpu
from jax.sharding import PartitionSpec as P

HEAD_DIM = 64


EPS = 1e-06


def gather_weights(
    query_weight,
    key_weight,
    value_weight,
    out_weight,
    gate_weight,
    up_weight,
    down_weight,
    attn_gain,
    ffn_gain,
):
    return (
        lax.all_gather(query_weight, ("fsdp", "ctx"), axis=0, tiled=True),
        lax.all_gather(key_weight, ("fsdp", "ctx"), axis=0, tiled=True),
        lax.all_gather(value_weight, ("fsdp", "ctx"), axis=0, tiled=True),
        lax.all_gather(out_weight, ("fsdp", "ctx"), axis=0, tiled=True),
        lax.all_gather(gate_weight, ("fsdp", "ctx"), axis=0, tiled=True),
        lax.all_gather(up_weight, ("fsdp", "ctx"), axis=0, tiled=True),
        lax.all_gather(down_weight, ("fsdp", "ctx"), axis=0, tiled=True),
        lax.all_gather(attn_gain, ("fsdp", "ctx"), axis=0, tiled=True),
        lax.all_gather(ffn_gain, ("fsdp", "ctx"), axis=0, tiled=True),
    )


def tensor_sum(partial_value):
    return lax.psum(partial_value, "tp")


def normalize(values, gain_vec):
    return values * lax.rsqrt(jnp.mean(values * values, -1, keepdims=True) + EPS) * gain_vec


def gelu_mix(gate_act, up_act):
    return jax.nn.gelu(gate_act, approximate=True) * up_act


def contract_last(left_op, right_op):
    return lax.dot_general(
        left_op, right_op, (((1,), (1,)), ((), ())), preferred_element_type=jnp.float32
    )


def contract_first(left_op, right_op):
    return lax.dot_general(
        left_op, right_op, (((0,), (0,)), ((), ())), preferred_element_type=jnp.float32
    )


def masked_scores(queries, key_whole, query_seg, seg_all, head_count):
    local_rows = queries.shape[0]
    query_heads = queries.reshape(local_rows, head_count, HEAD_DIM)
    key_heads = key_whole.reshape(key_whole.shape[0], head_count, HEAD_DIM)
    products = jnp.einsum(
        "qhd,khd->hqk", query_heads, key_heads, preferred_element_type=jnp.float32
    ) * HEAD_DIM ** (-0.5)
    same_doc = query_seg[:, None] == seg_all[None, :]
    return jnp.where(same_doc[None], products, -1e30)


def forward_pass(inputs, seg_all, gathered, ctx_pos):
    w_query, w_key, w_value, w_out, w_gate, w_up, w_down, gain_attn, gain_ffn = gathered
    head_count = w_query.shape[1] // HEAD_DIM
    local_rows = inputs.shape[0]
    query_seg = lax.dynamic_slice_in_dim(seg_all, ctx_pos * local_rows, local_rows)
    inputs_f = inputs.astype(jnp.float32)
    normed_one = normalize(inputs_f, gain_attn.astype(jnp.float32)).astype(jnp.bfloat16)
    queries = jnp.dot(normed_one, w_query, preferred_element_type=jnp.float32).astype(jnp.bfloat16)
    key_local = jnp.dot(normed_one, w_key, preferred_element_type=jnp.float32).astype(jnp.bfloat16)
    value_local = jnp.dot(normed_one, w_value, preferred_element_type=jnp.float32).astype(
        jnp.bfloat16
    )
    key_whole, value_whole = (
        lax.all_gather(key_local, "ctx", axis=0, tiled=True),
        lax.all_gather(value_local, "ctx", axis=0, tiled=True),
    )
    scores = masked_scores(queries, key_whole, query_seg, seg_all, head_count)
    row_max = jnp.max(scores, -1, keepdims=True)
    row_total = jnp.sum(jnp.exp(scores - row_max), -1, keepdims=True)
    log_total = row_max + jnp.log(row_total)
    probs_low = jnp.exp(scores - log_total).astype(jnp.bfloat16)
    value_heads = value_whole.reshape(value_whole.shape[0], head_count, HEAD_DIM)
    attn_mixed = jnp.einsum(
        "hqk,khd->qhd", probs_low, value_heads, preferred_element_type=jnp.float32
    )
    attn_mixed = attn_mixed.reshape(local_rows, head_count * HEAD_DIM).astype(jnp.bfloat16)
    attn_partial = contract_last(attn_mixed, w_out)
    residual = inputs_f + tensor_sum(attn_partial)
    normed_two = normalize(residual, gain_ffn.astype(jnp.float32)).astype(jnp.bfloat16)
    gate_act = jnp.dot(normed_two, w_gate, preferred_element_type=jnp.float32)
    up_act = jnp.dot(normed_two, w_up, preferred_element_type=jnp.float32)
    hidden = gelu_mix(gate_act, up_act).astype(jnp.bfloat16)
    ffn_partial = contract_last(hidden, w_down)
    result = (residual + tensor_sum(ffn_partial)).astype(jnp.bfloat16)
    stored = (
        inputs_f,
        normed_one,
        queries,
        key_whole,
        value_whole,
        log_total,
        attn_mixed,
        residual,
        normed_two,
        gate_act,
        up_act,
        hidden,
        query_seg,
    )
    return (result, stored)


def backward_pass(cot_rows, stored, gathered, seg_all, ctx_pos):
    w_query, w_key, w_value, w_out, w_gate, w_up, w_down, gain_attn, gain_ffn = gathered
    (
        inputs_f,
        normed_one,
        queries,
        key_whole,
        value_whole,
        log_total,
        attn_mixed,
        residual,
        normed_two,
        gate_act,
        up_act,
        hidden,
        query_seg,
    ) = stored
    head_count = w_query.shape[1] // HEAD_DIM
    local_rows = queries.shape[0]
    seq_rows = key_whole.shape[0]
    scale = HEAD_DIM ** (-0.5)
    dout = cot_rows.astype(jnp.float32)
    dout_low = dout.astype(jnp.bfloat16)
    grad_down = contract_first(dout_low, hidden)
    dhidden = jnp.dot(dout_low, w_down, preferred_element_type=jnp.float32)
    mixed_unused, mix_back = jax.vjp(gelu_mix, gate_act, up_act)
    dgate, dup = mix_back(dhidden)
    dgate_low = dgate.astype(jnp.bfloat16)
    dup_low = dup.astype(jnp.bfloat16)
    grad_gate = contract_first(normed_two, dgate_low)
    grad_up = contract_first(normed_two, dup_low)
    dn2_partial = contract_last(dgate_low, w_gate) + contract_last(dup_low, w_up)
    norm_unused, norm_back = jax.vjp(normalize, residual, gain_ffn.astype(jnp.float32))
    dresid_norm, grad_gain_ffn = norm_back(tensor_sum(dn2_partial))
    dresidual = dout + dresid_norm
    dres_low = dresidual.astype(jnp.bfloat16)
    grad_out = contract_first(dres_low, attn_mixed)
    dmixed = jnp.dot(dres_low, w_out, preferred_element_type=jnp.float32).astype(jnp.bfloat16)
    dmixed_heads = dmixed.reshape(local_rows, head_count, HEAD_DIM)
    scores = masked_scores(queries, key_whole, query_seg, seg_all, head_count)
    prob_full = jnp.exp(scores - log_total)
    key_heads = key_whole.reshape(seq_rows, head_count, HEAD_DIM)
    value_heads = value_whole.reshape(seq_rows, head_count, HEAD_DIM)
    dprobs = jnp.einsum(
        "qhd,khd->hqk", dmixed_heads, value_heads, preferred_element_type=jnp.float32
    )
    row_delta = jnp.sum(prob_full * dprobs, -1, keepdims=True)
    dscores = (prob_full * (dprobs - row_delta)).astype(jnp.bfloat16)
    dquery = (
        jnp.einsum("hqk,khd->qhd", dscores, key_heads, preferred_element_type=jnp.float32) * scale
    )
    query_all, dmixed_all = (
        lax.all_gather(queries, "ctx", axis=0, tiled=True),
        lax.all_gather(dmixed, "ctx", axis=0, tiled=True),
    )
    log_all, delta_all = (
        lax.all_gather(log_total, "ctx", axis=1, tiled=True),
        lax.all_gather(row_delta, "ctx", axis=1, tiled=True),
    )
    start = ctx_pos * local_rows
    key_own = lax.dynamic_slice_in_dim(key_whole, start, local_rows)
    value_own = lax.dynamic_slice_in_dim(value_whole, start, local_rows).reshape(
        local_rows, head_count, HEAD_DIM
    )
    scores_own = masked_scores(query_all, key_own, seg_all, query_seg, head_count)
    prob_own = jnp.exp(scores_own - log_all)
    dmixed_all_heads = dmixed_all.reshape(seq_rows, head_count, HEAD_DIM)
    query_all_heads = query_all.reshape(seq_rows, head_count, HEAD_DIM)
    dprobs_own = jnp.einsum(
        "qhd,khd->hqk", dmixed_all_heads, value_own, preferred_element_type=jnp.float32
    )
    dscores_own = (prob_own * (dprobs_own - delta_all)).astype(jnp.bfloat16)
    dkey_local = (
        jnp.einsum("hqk,qhd->khd", dscores_own, query_all_heads, preferred_element_type=jnp.float32)
        * scale
    ).reshape(local_rows, head_count * HEAD_DIM)
    dvalue_local = jnp.einsum(
        "hqk,qhd->khd",
        prob_own.astype(jnp.bfloat16),
        dmixed_all_heads,
        preferred_element_type=jnp.float32,
    ).reshape(local_rows, head_count * HEAD_DIM)
    dquery_low = dquery.reshape(local_rows, head_count * HEAD_DIM).astype(jnp.bfloat16)
    dkey_low = dkey_local.astype(jnp.bfloat16)
    dvalue_low = dvalue_local.astype(jnp.bfloat16)
    grad_query = contract_first(normed_one, dquery_low)
    grad_key = contract_first(normed_one, dkey_low)
    grad_value = contract_first(normed_one, dvalue_low)
    dn1_partial = (
        contract_last(dquery_low, w_query)
        + contract_last(dkey_low, w_key)
        + contract_last(dvalue_low, w_value)
    )
    norm_unused_two, norm_back_two = jax.vjp(normalize, inputs_f, gain_attn.astype(jnp.float32))
    dinput_norm, grad_gain_attn = norm_back_two(tensor_sum(dn1_partial))
    input_grad = dresidual + dinput_norm
    grad_terms = (
        grad_query,
        grad_key,
        grad_value,
        grad_out,
        grad_gate,
        grad_up,
        grad_down,
        grad_gain_attn,
        grad_gain_ffn,
    )
    return (input_grad, grad_terms)


def shards(
    tokens,
    segments,
    cotangent,
    query_weight,
    key_weight,
    value_weight,
    out_weight,
    gate_weight,
    up_weight,
    down_weight,
    attn_gain,
    ffn_gain,
):
    ctx_pos = lax.axis_index("ctx")
    results = []
    input_grads = []
    total_grads = None
    for micro_step in range(tokens.shape[0]):
        seg_all = segments[micro_step, 0]
        gathered = gather_weights(
            query_weight,
            key_weight,
            value_weight,
            out_weight,
            gate_weight,
            up_weight,
            down_weight,
            attn_gain,
            ffn_gain,
        )
        result, stored = forward_pass(tokens[micro_step, 0], seg_all, gathered, ctx_pos)
        gathered = gather_weights(
            query_weight,
            key_weight,
            value_weight,
            out_weight,
            gate_weight,
            up_weight,
            down_weight,
            attn_gain,
            ffn_gain,
        )
        input_grad, grad_terms = backward_pass(
            cotangent[micro_step, 0], stored, gathered, seg_all, ctx_pos
        )
        results.append(result)
        input_grads.append(input_grad)
        total_grads = (
            grad_terms if total_grads is None else jax.tree.map(jnp.add, total_grads, grad_terms)
        )
    gain_attn_total = total_grads[7]
    gain_ffn_total = total_grads[8]
    owned = (
        lax.psum_scatter(total_grads[0], ("fsdp", "ctx"), scatter_dimension=0, tiled=True),
        lax.psum_scatter(total_grads[1], ("fsdp", "ctx"), scatter_dimension=0, tiled=True),
        lax.psum_scatter(total_grads[2], ("fsdp", "ctx"), scatter_dimension=0, tiled=True),
        lax.psum_scatter(total_grads[3], ("fsdp", "ctx"), scatter_dimension=0, tiled=True),
        lax.psum_scatter(total_grads[4], ("fsdp", "ctx"), scatter_dimension=0, tiled=True),
        lax.psum_scatter(total_grads[5], ("fsdp", "ctx"), scatter_dimension=0, tiled=True),
        lax.psum_scatter(total_grads[6], ("fsdp", "ctx"), scatter_dimension=0, tiled=True),
        lax.psum_scatter(gain_attn_total, ("fsdp", "ctx"), scatter_dimension=0, tiled=True),
        lax.psum_scatter(gain_ffn_total, ("fsdp", "ctx"), scatter_dimension=0, tiled=True),
    )
    output = jnp.stack(results)[:, None]
    input_grad_all = jnp.stack(input_grads)[:, None]
    return (
        output,
        input_grad_all,
        owned[0],
        owned[1],
        owned[2],
        owned[3],
        owned[4],
        owned[5],
        owned[6],
        owned[7],
        owned[8],
    )


NEG = -1e30
MESH = pl.DeviceIdType.MESH
BF = jnp.bfloat16
F32 = jnp.float32
GELU_K = 0.7978845608028654
GELU_A = 0.044715
ORDER = (
    ("prep",), ("qR",), ("P", 0), ("wX", "g0"), ("wX", "d0"), ("wS", "g1"), ("wY", "g0"), ("P", 1), ("wS", "o"),
    ("wS", "u1"), ("wY", "d0"), ("wX", "g1"), ("wS", "d1"), ("AT", 0, 0), ("wX", "u0"), ("AT", 0, 1), ("AT", 1, 0),
    ("wX", "o"), ("wY", "g1"), ("wY", "u0"), ("AT", 1, 1), ("wX", "u1"), ("wF", 0), ("wX", "d1"), ("O", 0),
    ("wY", "o"), ("wY", "u1"), ("wF", "o"), ("F1", 0), ("wY", "d1"), ("FS", 0, 0), ("wF", 1), ("FS", 0, 1), ("O", 1),
    ("FP", 0), ("F1", 1), ("FS", 1, 0), ("FS", 1, 1), ("G", "d"), ("BN", 0, 0), ("BN", 0, 1), ("FP", 1), ("SQ", "d"),
    ("G", "g"), ("ON", 0, 0), ("BS", 0), ("G", "u"), ("ON", 0, 1), ("PE", 0), ("OF", 0, 0), ("OF", 0, 1), ("SF", "d"),
    ("BN", 1, 0), ("BN", 1, 1), ("OW", 0), ("J", 0), ("BS", 1), ("ON", 1, 0), ("PE", 1), ("G", "o"), ("ON", 1, 1),
    ("SQ", "o"), ("OF", 1, 0), ("X", 0, 0), ("OW", 1), ("OF", 1, 1), ("X", 0, 1), ("J", 1), ("IN", 0, 0), ("SF", "o"),
    ("SQ", "g"), ("IF", 0, 0), ("IN", 0, 1), ("G", "q"), ("X", 1, 0), ("GZ",), ("SQ", "u"), ("IF", 0, 1), ("X", 1, 1),
    ("IN", 1, 0), ("SF", "g"), ("SQ", "q"), ("IF", 1, 0), ("SZ", "o"), ("GR",), ("IN", 1, 1), ("SZ", "d"),
    ("SF", "q"), ("GF",), ("SZ", "g"), ("SF", "u"), ("IF", 1, 1), ("SZ", "u"),
)


def dot_nn(a, b):
    return lax.dot_general(a, b, (((1,), (0,)), ((), ())), preferred_element_type=F32)


def dot_nt(a, b):
    return lax.dot_general(a, b, (((1,), (1,)), ((), ())), preferred_element_type=F32)


def dot_tn(a, b):
    return lax.dot_general(a, b, (((0,), (0,)), ((), ())), preferred_element_type=F32)


def at(i, n):
    return pl.ds(pl.multiple_of(i, n), n)


def layer_kernel(dims, names, *refs):
    r = dict(zip(names, refs))
    R, D, H, FF, C, NF, NT, MICRO = dims
    L = C * R
    NH = H // HEAD_DIM
    HP = 256
    KV = 2 * H
    Y = NF // 2
    SR = D // (NF * C)
    RT = 256
    CH = 128
    UNIT = 64
    NCH = R // CH
    f = lax.axis_index("fsdp")
    c = lax.axis_index("ctx")
    t = lax.axis_index("tp")
    core = lax.rem(f, 2)
    y = f // 2
    shard = f * C + c
    partner = {"fsdp": f + 1 - 2 * core}
    ssem, rsem = r["ssem"], r["rsem"]
    counter = [0]

    def slot():
        counter[0] += 1
        return counter[0] - 1

    def copy_to(src, dst, idx, dev, sidx=None):
        return pltpu.make_async_remote_copy(
            src_ref=src, dst_ref=dst, send_sem=ssem.at[idx if sidx is None else sidx], recv_sem=rsem.at[idx],
            device_id=dev, device_id_type=MESH)

    offsets = [(dy, dc) for dy in range(Y) for dc in range(C) if (dy, dc) != (0, 0)]

    def square(off):
        dy, dc = off
        return (2 * lax.rem(y + dy, Y) + core, lax.rem(c + dc, C))

    def square_from(off):
        dy, dc = off
        return (2 * lax.rem(y + Y - dy, Y) + core, lax.rem(c + C - dc, C))

    def dev_sq(off):
        pf, pc = square(off)
        return {"fsdp": pf, "ctx": pc}

    def z_to(k):
        return {"tp": lax.rem(t + k, NT)}

    group = [(df, dc) for df in range(NF) for dc in range(C) if (df, dc) != (0, 0)]

    def dev_group(off):
        return {"fsdp": lax.rem(f + off[0], NF), "ctx": lax.rem(c + off[1], C)}

    half = t // 2
    inner = (t == 1) | (t == 2)
    outer = (t == 0) | (t == 3)
    mate = {"tp": t + 1 - 2 * lax.rem(t, 2)}
    twin_t = lax.rem(t + 2, NT)
    twin = {"tp": twin_t}
    cross = {"tp": NT - 1 - t}
    HR = R // 2
    SUB = HR // CH
    hrows = at(half * HR, HR)

    def both(do_inner, do_outer):
        pl.when(inner)(do_inner)
        pl.when(outer)(do_outer)

    local = r["lsem"]

    def load(src, dst, n):
        cp = pltpu.make_async_copy(src, dst, local.at[n])
        cp.start()
        return cp

    own_rows = at(shard * SR, SR)
    wqkv, wo, woz, wg, wu, wd = r["wqkv"], r["wo"], r["woz"], r["wg"], r["wu"], r["wd"]
    load_first = [load(r[n + "_in"], r[n + "_own"], 3 + i) for i, n in enumerate(("gain_a", "gain_f", "wq", "wk", "wv"))]
    load_out = load(r["wo_in"], r["wo_own"], 8)
    load_ffn = [load(r[n + "_in"], r[n].at[0, own_rows], 9 + i) for i, n in enumerate(("wg", "wu", "wd"))]
    load_tok = load(r["tok_in"], r["tok"], 0)
    load_cot = [load(r["cot_in"].at[m, hrows], r["cot"].at[pl.ds(m * HR, HR)], 1 + m) for m in range(MICRO)]

    bar = pltpu.get_barrier_semaphore()
    for off in group:
        pl.semaphore_signal(bar, inc=1, device_id=dev_group(off), device_id_type=MESH)
    for k in range(1, NT):
        pl.semaphore_signal(bar, inc=1, device_id=z_to(k), device_id_type=MESH)

    def spot(width, shift):
        i = lax.broadcasted_iota(jnp.int32, (H, width), 0)
        j = lax.broadcasted_iota(jnp.int32, (H, width), 1)
        return (j == i + shift).astype(BF)

    W = HP + KV
    VOFF = HP - H
    gm = r["gmine"]
    cols = lax.broadcasted_iota(jnp.int32, (SR, D), 1)
    rows = lax.broadcasted_iota(jnp.int32, (SR, D), 0)
    place = (cols == rows + shard * SR).astype(BF)
    for cp in load_first:
        cp.wait()
    gm[...] = jnp.zeros_like(gm)
    gm[0:1, :] = dot_nn(r["gain_a_own"][...], place)
    gm[1:2, :] = dot_nn(r["gain_f_own"][...], place)
    wqkv[own_rows, :] = (dot_nn(r["wq_own"][...], spot(W, 0)) + dot_nn(r["wk_own"][...], spot(W, HP))
                         + dot_nn(r["wv_own"][...], spot(W, HP + H))).astype(BF)
    load_out.wait()
    woz[t] = dot_nn(r["wo_own"][...], spot(HP, 0)).astype(BF)
    for cp in load_ffn:
        cp.wait()
    pl.semaphore_wait(bar, len(group) + NT - 1)

    sends, weight_sends = [], []

    def send(src, dst, idx, dev, group=None):
        cp = copy_to(src, dst, idx, dev)
        cp.start()
        (sends if group is None else group).append(cp)
        return cp

    def rows_of(off):
        pf, pc = square_from(off)
        return at((pf * C + pc) * SR, SR)

    class Spread:
        def __init__(self, buf, view, far, group):
            self.buf, self.view, self.far, self.group = buf, view, far, group
            self.ix = {off: slot() for off in offsets}
            self.px = slot()
            self.rx = {off: slot() for off in offsets}

        def rows(self, off):
            return self.view(self.buf, rows_of(off))

        def start(self):
            w = self.view(self.buf, own_rows)
            for off in offsets:
                if self.far or 0 in off:
                    send(w, w, self.ix[off], dev_sq(off), self.group)
            send(w, w, self.px, partner, self.group)

        def relay_x(self):
            w = self.rows((0, 1))
            copy_to(w, w, self.ix[(0, 1)], partner).wait_recv()
            if not self.far:
                send(w, w, self.ix[(1, 1)], dev_sq((1, 0)), self.group)
            send(w, w, self.rx[(0, 1)], partner, self.group)

        def relay_y(self):
            for off in ((1, 0), (1, 1)):
                w = self.rows(off)
                copy_to(w, w, self.ix[off], partner).wait_recv()
                send(w, w, self.rx[off], partner, self.group)

        def finish(self):
            w = self.view(self.buf, own_rows)
            copy_to(w, w, self.px, partner).wait_recv()
            for off in offsets:
                copy_to(w, w, self.rx[off], partner).wait_recv()

    flat = lambda buf, rows: buf.at[rows]
    deep = lambda buf, rows: buf.at[:, rows]
    gall = r["gall"]
    gain_cp = [send(gm, gall.at[n], slot(), dev_group(off)) for n, off in enumerate(group)]
    qkv_sp = Spread(wqkv, flat, True, sends)
    qkv_sp.start()
    twin_ix = {}
    for k, buf in (("g", wg), ("u", wu), ("d", wd)):
        twin_ix[k] = slot()
        send(buf.at[0, own_rows], buf.at[1, own_rows], twin_ix[k], twin, weight_sends)
    spreads = {k + str(n): Spread(b.at[n], flat, False, weight_sends) for n in range(2) for k, b in (("g", wg), ("u", wu), ("d", wd))}
    spreads["o"] = Spread(wo, flat, False, sends)
    for k in "gud":
        spreads[k + "0"].start()
    wo_ix = [slot() for _ in range(1, NT)]
    for k, i in zip(range(1, NT), wo_ix):
        send(woz.at[t], woz.at[t], i, z_to(k))
    segr, segc = r["segr"].at[:, 0], r["segc"]
    gains, gacc, oT, oX = r["gains"], r["gacc"], r["oT"], r["oX"]
    tok, cot, n1 = r["tok"], r["cot"], r["n1"]

    def prepare():
        for m in range(MICRO):
            for b in range(L // 128):
                row = segr[m:m + 1, 128 * b:128 * b + 128].astype(F32)
                segc[m, 128 * b:128 * b + 128, :] = jnp.broadcast_to(row, (128, 128)).T.astype(jnp.int32)
        for cp in gain_cp:
            cp.wait_recv()
        gsum = gm[...]
        for n in range(len(group)):
            gsum = gsum + gall[n]
        gains[...] = gsum
        load_tok.wait()
        for m in range(MICRO):
            norm_one(m)
        gacc[...] = jnp.zeros_like(gacc)

    def norm_one(m):
        @pl.loop(0, R // CH)
        def _(i):
            xf = tok[m, at(i * CH, CH), :].astype(F32)
            rs = lax.rsqrt(jnp.mean(xf * xf, -1, keepdims=True) + EPS)
            n1[at(m * R + i * CH, CH), :] = (xf * rs * gains[0:1, :]).astype(BF)

    q, kv, kvT = r["q"], r["kv"], r["kvT"]
    scale = HEAD_DIM ** -0.5
    def qkv_ready():
        qkv_sp.relay_x()
        qkv_sp.relay_y()
        qkv_sp.finish()

    kv_ix = [slot() for _ in range(MICRO)]
    other = {"ctx": lax.rem(c + 1, C)}

    def project(m):
        @pl.loop(0, R // RT)
        def _(i):
            acc = dot_nn(n1[at(m * R + i * RT, RT), :], wqkv[...])
            q[m, at(i * RT, RT), :] = (acc[:, 0:HP] * scale).astype(BF)
            kv[m, at(c * R + i * RT, RT), :] = acc[:, HP:HP + KV].astype(BF)
        w = kv.at[m, at(c * R, R)]
        send(w, w, kv_ix[m], other)
        flip(m, c * R)

    def spread(w):
        if w == "o":
            for k, i in zip(range(1, NT), wo_ix):
                copy_to(woz.at[t], woz.at[t], i, z_to(k)).wait_recv()
            i = lax.broadcasted_iota(jnp.int32, (HP, D), 0)
            j = lax.broadcasted_iota(jnp.int32, (HP, D), 1)
            row = dot_nn(woz[0], (j == i).astype(BF))
            for k in range(1, NT):
                row = row + dot_nn(woz[k], (j == i + k * H).astype(BF))
            wo[own_rows, :] = row.astype(BF)
        else:
            v = {"g": wg, "u": wu, "d": wd}[w[0]].at[0, own_rows]
            copy_to(v, v, twin_ix[w[0]], twin).wait_recv()
        spreads[w].start()

    def weights_ready(n):
        for k in ["o"] if n == "o" else [w + str(n) for w in "gud"]:
            spreads[k].finish()

    onat, lse = r["onat"], r["lse"]
    lanes = lax.broadcasted_iota(jnp.int32, (RT, HP), 1)

    def head_mask(v, h, shift):
        lo = shift + h * HEAD_DIM
        return jnp.where((lanes >= lo) & (lanes < lo + HEAD_DIM), v, jnp.zeros_like(v))

    def flip(m, start):
        @pl.loop(0, R // RT)
        def _(i):
            kvT[m, :, at(start + i * RT, RT)] = kv[m, at(start + i * RT, RT), :].T

    def attend(m, i):
        kk = kv[m, :, 0:HP]
        sc = segc[m]
        sc = jnp.concatenate([sc] * (RT // 128), axis=1)
        sr = segr[m:m + 1, at(c * R + i * RT, RT)]
        qq = q[m, pl.ds(i * RT, RT), :]
        for h in range(NH):
            s = dot_nt(kk, head_mask(qq, h, 0))
            s = jnp.where(sc == sr, s, NEG)
            mx = jnp.max(s, axis=0, keepdims=True)
            e = jnp.exp(s - mx)
            tot = jnp.sum(e, axis=0, keepdims=True)
            p = (e * (1.0 / tot)).astype(BF)
            vT = kvT[m, H + h * HEAD_DIM:H + (h + 1) * HEAD_DIM, :]
            lo = VOFF + h * HEAD_DIM
            oT[m, lo:lo + HEAD_DIM, pl.ds(i * RT, RT)] = dot_nn(vT, p).astype(BF)
            lse[m, h, :, pl.ds(i * RT, RT)] = mx + jnp.log(tot)

    o_ix = [[slot() for _ in range(3)] for _ in range(MICRO)]

    def o_send(m, i, n):
        src = oT.at[m, pl.ds(VOFF, H), pl.ds(i * HR, HR)]
        return copy_to(src, oX.at[m, at(t * H, H)], o_ix[m][n], (mate, twin, cross)[n])

    def share_o(m, i):
        @pl.when(half == i)
        def _():
            o_send(m, i, 0).start()

        @pl.when(half != i)
        def _():
            o_send(m, i, 1).start()
            o_send(m, i, 2).start()

    def wait_o(m):
        for n in range(3):
            o_send(m, 0, n).wait_recv()

    def close_o(m):
        for n in range(3):
            o_send(m, 0, n).wait_send()

    def attend_tile(m, i):
        if i == 0:
            w = kv.at[m, at(c * R, R)]
            copy_to(w, w, kv_ix[m], other).wait_recv()
            flip(m, lax.rem(c + 1, C) * R)
        attend(m, i)
        share_o(m, i)

    y1, n2, big, dy = r["y1"], r["n2"], r["big"], r["dy"]
    d2s, d2r, fps, fpr = r["d2s"], r["d2r"], r["fps"], r["fpr"]
    d2_ix = [[slot() for _ in range(SUB)] for _ in range(MICRO)]
    fp_ix = [[slot() for _ in range(SUB)] for _ in range(MICRO)]

    def to_mate(src, dst, ix, m, j):
        rr = pl.ds(j * CH, CH)
        return copy_to(src.at[m, rr], dst.at[m, rr], ix[m][j], mate)

    def feed(m):
        oX[m, at(t * H, H), :] = oT[m, VOFF:HP, hrows]
        mr = pl.ds(m * HR, HR)
        onat[mr, :] = oX[m].T
        acc = tok[m, hrows, :].astype(F32)
        acc = acc + dot_nt(onat[mr, :], wo[...])
        y1[m] = acc
        rs = lax.rsqrt(jnp.mean(acc * acc, -1, keepdims=True) + EPS)
        n2[mr, :] = (acc * rs * gains[1:2, :]).astype(BF)

    def feed_slot(m, n):
        if (m, n) == fed[0]:
            for cp in load_cot:
                cp.wait()
        mr = pl.ds(m * HR, HR)
        n2v = n2[mr, :]
        g = dot_nn(n2v, wg[n])
        u = dot_nn(n2v, wu[n])
        th = jnp.tanh(GELU_K * (g + GELU_A * g * g * g))
        hf = 0.5 * (1.0 + th)
        gl = g * hf
        big[0, n, mr, :] = (gl * u).astype(BF)
        dh = dot_nn(cot[mr, :], wd[n])
        dgl = hf + 0.5 * g * (1.0 - th * th) * (GELU_K * (1.0 + 3.0 * GELU_A * g * g))
        dgv = (dh * u * dgl).astype(BF)
        duv = (dh * gl).astype(BF)
        big[1, n, mr, :] = dgv
        big[2, n, mr, :] = duv
        d2 = dot_nt(dgv, wg[n]) + dot_nt(duv, wu[n])
        if n == 0:
            dy[m] = d2
            return
        d2 = dy[m] + d2
        d2s[m] = d2.astype(BF)

        @pl.when(outer)
        def _():
            for j in range(SUB):
                to_mate(d2s, d2r, d2_ix, m, j).start()

        yn = y1[m]
        rs = lax.rsqrt(jnp.mean(yn * yn, -1, keepdims=True) + EPS)
        gacc[1:2, :] += jnp.sum(d2 * (yn * rs), axis=0, keepdims=True)
        fps[m] = (dot_nt(big[0, 0, mr, :], wd[0]) + dot_nt(big[0, 1, mr, :], wd[1])).astype(BF)

    def feed_out(m):
        @pl.when(outer)
        def _():
            for j in range(SUB):
                to_mate(fps, fpr, fp_ix, m, j).start()

    class Reduce:
        def __init__(self, k, pieces, put):
            self.own, self.half, self.recv, self.parts = r["own_" + k], r["st_" + k], r["rv_" + k], r["pt_" + k]
            self.pieces, self.put = pieces, put
            self.px = slot()
            self.ix = [slot() for _ in offsets]

        def pair_copy(self):
            return copy_to(self.half, self.recv, self.px, partner)

        def pair(self):
            tmp = r["tmp"]
            for left, right, c0, width in self.pieces:
                @pl.loop(0, D // RT)
                def _(i, left=left, right=right, c0=c0, width=width):
                    tmp[:, 0:width] = dot_tn(left[:, at(i * RT, RT)], right[...])

                    @pl.loop(0, RT // UNIT)
                    def _(p):
                        row = i * RT + p * UNIT
                        b = row // (C * SR)
                        to = at((b // 2) * C * SR + lax.rem(row, C * SR), UNIT)
                        part = tmp[at(p * UNIT, UNIT), 0:width]

                        @pl.when(lax.rem(b, 2) == core)
                        def _():
                            self.own[to, c0:c0 + width] = part

                        @pl.when(lax.rem(b, 2) != core)
                        def _():
                            self.half[to, c0:c0 + width] = part.astype(BF)
            self.pair_copy().start()

        def block(self, n):
            pf, pc = square(offsets[n])
            src = self.half.at[at(((pf // 2) * C + pc) * SR, SR)]
            return copy_to(src, self.parts.at[n], self.ix[n], dev_sq(offsets[n]))

        def square(self):
            self.pair_copy().wait()
            tot = self.own[...] + self.recv[...].astype(F32)
            self.own[...] = tot
            self.half[...] = tot.astype(BF)
            for n in range(len(offsets)):
                self.block(n).start()

        def finish(self):
            tot = self.own[at((y * C + c) * SR, SR), :]
            for n in range(len(offsets)):
                self.block(n).wait()
            for n in range(len(offsets)):
                tot = tot + self.parts[n].astype(F32)
            self.put(tot)

    zs_ix = {k: slot() for k in "gud"}

    def twin_sum(k):
        def put(tot):
            r["fin_" + k][...] = tot[:, 0:FF]
            r["zs_" + k][...] = tot[:, FF:2 * FF].astype(BF)
            send(r["zs_" + k], r["zr_" + k], zs_ix[k], twin)
        return put

    def split_qkv(tot):
        r["fin_qkv"][0] = tot[:, 0:H]
        r["fin_qkv"][1] = tot[:, HP:HP + H]
        r["fin_qkv"][2] = pltpu.roll(tot[:, W - HP:W], HP - VOFF, 1)[:, 0:H]
        for n, k in enumerate("qkv"):
            store(r["fin_qkv"].at[n], r["out_" + k])

    zo, zq = r["zo"], r["zq"]
    zo_ix, zo_sx = [slot(), slot()], slot()

    def zo_copies():
        out = []
        for dev, ix, sx in ((mate, zo_ix[0], None), (twin, zo_ix[1], None), (cross, zo_ix[1], zo_sx)):
            out.append(copy_to(zq.at[dev["tp"]], zo.at[half], ix, dev, sx))
        return out

    def out_sum(tot):
        for k in range(NT):
            base = k * H // 128 * 128
            part = tot[:, base:base + HP]
            zq[k] = (pltpu.roll(part, HP - (k * H - base), 1) if k * H > base else part).astype(BF)
        zo[half] = zq[t]
        for cp in zo_copies():
            cp.start()

    dqkv, ar = r["dqkv"], r["ar"]
    pieces = {
        "d": [(cot, big.at[0, n], n * FF, FF) for n in range(2)],
        "g": [(n2, big.at[1, n], n * FF, FF) for n in range(2)],
        "u": [(n2, big.at[2, n], n * FF, FF) for n in range(2)],
        "q": [(n1, dqkv.at[:, pl.ds(0, 512)], 0, 512), (n1, dqkv.at[:, pl.ds(512, W - 512)], 512, W - 512)],
        "o": [(ar, onat.at[:, pl.ds(0, 512)], 0, 512), (ar, onat.at[:, pl.ds(512, D - 512)], 512, D - 512)],
    }
    puts = {"d": twin_sum("d"), "g": twin_sum("g"), "u": twin_sum("u"), "q": split_qkv, "o": out_sum}
    reds = {k: Reduce(k, pieces[k], puts[k]) for k in "dguqo"}

    def reduce_step(k, what):
        if k == "o":
            pl.when(inner)(lambda: getattr(reds[k], what)())
        else:
            getattr(reds[k], what)()

    def last_sum(k):
        if k == "o":
            both(lambda: zo_copies()[1].wait_recv(), lambda: [cp.wait_recv() for cp in zo_copies()[:2]] and None)
            tot = zo[0].astype(F32) + zo[1].astype(F32)
            r["fin_o"][...] = tot[:, 0:H]
            store(r["fin_o"], r["out_o"])
        elif k != "q":
            copy_to(r["zs_" + k], r["zr_" + k], zs_ix[k], twin).wait_recv()
            r["fin_" + k][...] += r["zr_" + k][...].astype(F32)
            store(r["fin_" + k], r["out_" + k])

    doT, doS = r["doT"], r["doS"]
    do_ix = [[[slot(), slot()] for _ in range(SUB)] for _ in range(MICRO)]
    do_sx = [[slot() for _ in range(SUB)] for _ in range(MICRO)]

    def do_copies(m, j):
        out = []
        to = doT.at[m, pl.ds(VOFF, H), pl.ds(pl.multiple_of(half * HR + j * CH, CH), CH)]
        for dev, n, sx in ((mate, 0, None), (twin, 1, None), (cross, 1, do_sx[m][j])):
            src = doS.at[at(dev["tp"] * H, H), pl.ds(j * CH, CH)]
            out.append(copy_to(src, to, do_ix[m][j][n], dev, sx))
        return out

    def back_norm(m, j):
        @pl.when(inner)
        def _():
            to_mate(d2s, d2r, d2_ix, m, j).wait_recv()
            if m:
                for cp in do_copies(m - 1, j):
                    cp.wait_send()
            rr = pl.ds(j * CH, CH)
            gr = pl.ds(m * HR + j * CH, CH)
            yv = y1[m, rr, :]
            d2 = d2s[m, rr, :].astype(F32) + d2r[m, rr, :].astype(F32)
            tv = lax.rsqrt(jnp.mean(yv * yv, -1, keepdims=True) + EPS)
            e2 = gains[1:2, :] * d2
            dot = jnp.mean(yv * e2, -1, keepdims=True)
            dv = cot[gr, :].astype(F32) + tv * e2 - yv * (tv * tv * tv * dot)
            dy[m, rr, :] = dv
            av = dv.astype(BF)
            ar[gr, :] = av
            doS[:, rr] = dot_nn(av, wo[...]).astype(BF).T
            doT[m, VOFF:HP, pl.ds(pl.multiple_of(half * HR + j * CH, CH), CH)] = doS[at(t * H, H), rr]
            for cp in do_copies(m, j):
                cp.start()

    delta, dqT, dkv_in, dkv_own = r["delta"], r["dqT"], r["dkv_in"], r["dkv_own"]
    dkv_out = wg.at[:, pl.ds(0, R), pl.ds(0, KV)]
    lay = [(0, 0), (0, HP), (1, 0)]
    qm = [wd.at[a, pl.ds(0, R), pl.ds(b, HP)] for a, b in lay]
    dom = [wu.at[a, pl.ds(0, R), pl.ds(b, HP)] for a, b in lay]

    def back_start(m):
        if m == 0:
            for cp in weight_sends:
                cp.wait_send()
        for j in range(SUB):
            cps = do_copies(m, j)
            both(lambda: cps[1].wait_recv(), lambda: [cp.wait_recv() for cp in cps[:2]] and None)

        @pl.loop(0, R // RT)
        def _(i):
            rr = at(i * RT, RT)
            dov = doT[m, :, rr].T
            for h in range(NH):
                lo = VOFF + h * HEAD_DIM
                prod = doT[m, lo:lo + HEAD_DIM, rr].astype(F32) * oT[m, lo:lo + HEAD_DIM, rr].astype(F32)
                delta[h, :, rr] = jnp.sum(prod, axis=0, keepdims=True)
                dom[h][rr, :] = head_mask(dov, h, VOFF)
                qm[h][rr, :] = head_mask(q[m, rr, :], h, 0)

    def back_half(m, key0, first):
        @pl.loop(0, R // RT)
        def _(i):
            sc = segc[m, at(key0, R), :]
            sc = jnp.concatenate([sc] * (RT // 128), axis=1)
            sr = segr[m:m + 1, at(c * R + i * RT, RT)]
            cs = at(i * RT, RT)
            for h in range(NH):
                s = dot_nt(kv[m, at(key0, R), 0:HP], qm[h][cs, :])
                s = jnp.where(sc == sr, s, NEG)
                p = jnp.exp(s - lse[m, h, :, cs])
                dp = dot_nt(kv[m, at(key0, R), KV - HP:KV], dom[h][cs, :])
                big[h, 1, :, cs] = p.astype(BF)
                big[h, 0, :, cs] = (p * (dp - delta[h, :, cs])).astype(BF)

        dst = dkv_out if first else dkv_own

        @pl.loop(0, R // RT)
        def _(i):
            rr = at(i * RT, RT)
            dk = dot_nn(big[0, 0, rr, :], qm[0][...])
            dv = dot_nn(big[0, 1, rr, :], dom[0][...])
            for h in range(1, NH):
                dk = dk + dot_nn(big[h, 0, rr, :], qm[h][...])
                dv = dv + dot_nn(big[h, 1, rr, :], dom[h][...])
            dst[m, rr, 0:128] = dk[:, 0:128].astype(dst.dtype)
            dst[m, rr, 128:256] = (dk[:, 128:256] + dv[:, 0:128]).astype(dst.dtype)
            dst[m, rr, 256:384] = dv[:, 128:256].astype(dst.dtype)
        for h in range(NH):
            hs = pl.ds(h * HEAD_DIM, HEAD_DIM)
            part = dot_nn(kvT[m, hs, at(key0, R)], big[h, 0])
            if first:
                dqT[hs, :] = part
            else:
                dqT[hs, :] = dqT[hs, :] + part

    dkv_ix = [slot() for _ in range(MICRO)]

    def back_peer(m):
        back_half(m, lax.rem(c + 1, C) * R, True)
        send(dkv_out.at[m], dkv_in.at[m], dkv_ix[m], other)

    def back_own(m):
        back_half(m, c * R, False)
        dqkv[pl.ds(m * R, R), 0:HP] = jnp.zeros((R, HP), BF)
        dqkv[pl.ds(m * R, R), 0:H] = (dqT[...] * scale).T.astype(BF)

    snd, rc1, rc2, igb = r["snd"], r["rc1"], r["rc2"], r["igb"]
    in_ix = [[[slot() for _ in range(SUB)] for _ in range(2)] for _ in range(MICRO)]
    sw_ix = [[slot() for _ in range(SUB)] for _ in range(MICRO)]

    def piece(own, j):
        return pl.ds(pl.multiple_of((half if own else 1 - half) * HR + j * CH, CH), CH)

    def inward(m, own, j):
        rr = piece(own, j)
        return copy_to(snd.at[m, rr], rc1.at[m, rr], in_ix[m][own][j], mate)

    def swap(m, j):
        return copy_to(snd.at[m, piece(0, j)], rc2.at[m, pl.ds(j * CH, CH)], sw_ix[m][j], cross)

    def join(m):
        copy_to(dkv_out.at[m], dkv_in.at[m], dkv_ix[m], other).wait_recv()
        for own in range(2):
            base = (half if own else 1 - half) * HR
            rr = at(base, HR)
            gr = pl.ds(pl.multiple_of(m * R + base, HR), HR)
            dqkv[gr, HP:HP + KV] = (dkv_own[m, rr, :] + dkv_in[m, rr, :].astype(F32)).astype(BF)
            d1 = dot_nt(dqkv[gr, :], wqkv[...])
            snd[m, rr, :] = d1.astype(BF)

            @pl.when(outer)
            def _(own=own):
                for j in range(SUB):
                    inward(m, own, j).start()

            xv = tok[m, rr, :].astype(F32)
            rs = lax.rsqrt(jnp.mean(xv * xv, -1, keepdims=True) + EPS)
            gacc[0:1, :] += jnp.sum(d1 * (xv * rs), axis=0, keepdims=True)

    def cross_over(m, j):
        @pl.when(inner)
        def _():
            inward(m, 0, j).wait_recv()
            rr = piece(0, j)
            snd[m, rr, :] = (snd[m, rr, :].astype(F32) + rc1[m, rr, :].astype(F32)).astype(BF)
            swap(m, j).start()

    class Result:
        def __init__(self, buf, name):
            self.buf, self.name = buf, name
            self.ix = [[[slot() for _ in range(3)] for _ in range(SUB)] for _ in range(MICRO)]

        def copy(self, m, j, n):
            at_ = self.buf.at[m, piece(n != 2, j)]
            return copy_to(at_, at_, self.ix[m][j][n], cross if n == 1 else mate)

        def arrived(self, m, j, n):
            at_ = self.buf.at[m, piece(0, j)]
            copy_to(at_, at_, self.ix[m][j][n], mate).wait_recv()

        def store(self, m, j, own):
            rr = piece(own, j)
            store(self.buf.at[m, rr], r[self.name].at[m, 0, rr])

        def near(self, m, j, make):
            def one():
                make(m, j)
                self.copy(m, j, 1).start()
                self.copy(m, j, 0).start()
            both(one, lambda: self.arrived(m, j, 0))
            self.store(m, j, 1)

        def far(self, m, j):
            def one():
                self.arrived(m, j, 1)
                self.copy(m, j, 2).start()
            both(one, lambda: self.arrived(m, j, 2))
            self.store(m, j, 0)

        def close(self, m, j):
            @pl.when(inner)
            def _():
                for n in range(3):
                    self.copy(m, j, n).wait_send()

    stores = []

    def store(src, dst):
        cp = pltpu.make_async_copy(src, dst, local.at[12 + len(stores)])
        cp.start()
        stores.append(cp)

    def make_output(m, j):
        to_mate(fps, fpr, fp_ix, m, j).wait_recv()
        rr = pl.ds(j * CH, CH)
        tot = y1[m, rr, :] + (fps[m, rr, :].astype(F32) + fpr[m, rr, :].astype(F32))
        r["outv"][m, piece(1, j), :] = tot.astype(BF)

    def make_input_grad(m, j):
        inward(m, 1, j).wait_recv()
        swap(m, j).wait_recv()
        rr = pl.ds(j * CH, CH)
        here = piece(1, j)
        xv = tok[m, here, :].astype(F32)
        d1 = snd[m, here, :].astype(F32) + rc1[m, here, :].astype(F32) + rc2[m, rr, :].astype(F32)
        tv = lax.rsqrt(jnp.mean(xv * xv, -1, keepdims=True) + EPS)
        e1 = gains[0:1, :] * d1
        dot = jnp.mean(xv * e1, -1, keepdims=True)
        igb[m, here, :] = (dy[m, rr, :] + tv * e1 - xv * (tv * tv * tv * dot)).astype(BF)

    out_res, ig_res = Result(r["outv"], "out"), Result(igb, "ig")

    gz, gz_ix = r["gz"], [slot() for _ in range(NT)]
    gin, gpart = r["gin"], r["gpart"]
    gain_ix = [slot() for _ in group]

    def gain_z():
        for k in range(1, NT):
            send(gacc, gz.at[k], gz_ix[k], z_to(k))

    def gain_group():
        for k in range(1, NT):
            copy_to(gacc, gz.at[k], gz_ix[k], z_to(k)).wait_recv()
        tot = gacc[...]
        for k in range(1, NT):
            tot = tot + gz[k]
        gpart[...] = tot
        for n, off in enumerate(group):
            send(gpart, gin.at[n], gain_ix[n], dev_group(off))

    def gain_final():
        for n, off in enumerate(group):
            copy_to(gpart, gin.at[n], gain_ix[n], dev_group(off)).wait_recv()
        tot = gpart[...]
        for n in range(len(group)):
            tot = tot + gin[n]
        tot = lax.dot_general(
            tot, place.astype(F32), (((1,), (1,)), ((), ())), precision=lax.Precision.HIGHEST,
            preferred_element_type=F32)
        r["fin_gain"][0] = tot[0:1, :]
        r["fin_gain"][1] = tot[1:2, :]
        store(r["fin_gain"].at[0], r["out_ga"])
        store(r["fin_gain"].at[1], r["out_gf"])

    fed = [step[1:] for step in ORDER if step[0] == "FS"]
    acts = {
        "prep": prepare, "qR": qkv_ready, "wF": weights_ready, "P": project, "wS": spread,
        "wX": lambda w: spreads[w].relay_x(), "wY": lambda w: spreads[w].relay_y(), "AT": attend_tile,
        "O": wait_o, "F1": feed, "FS": feed_slot, "FP": feed_out, "G": lambda k: reduce_step(k, "pair"), "SQ": lambda k: reduce_step(k, "square"),
        "SF": lambda k: reduce_step(k, "finish"), "SZ": last_sum, "BN": back_norm, "BS": back_start,
        "PE": back_peer, "OW": back_own, "J": join, "X": cross_over,
        "ON": lambda m, j: out_res.near(m, j, make_output), "OF": out_res.far,
        "IN": lambda m, j: ig_res.near(m, j, make_input_grad), "IF": ig_res.far,
        "GZ": gain_z, "GR": gain_group, "GF": gain_final,
    }
    for step in ORDER:
        acts[step[0]](*step[1:])
    for cp in stores:
        cp.wait()
    for cp in sends:
        cp.wait_send()
    for m in range(MICRO):
        close_o(m)
        for j in range(SUB):
            out_res.close(m, j)
            ig_res.close(m, j)

            def inner_done(m=m, j=j):
                if m == MICRO - 1:
                    for cp in do_copies(m, j):
                        cp.wait_send()
                swap(m, j).wait_send()

            def outer_done(m=m, j=j):
                to_mate(d2s, d2r, d2_ix, m, j).wait_send()
                to_mate(fps, fpr, fp_ix, m, j).wait_send()
                inward(m, 0, j).wait_send()
                inward(m, 1, j).wait_send()

            both(inner_done, outer_done)

    @pl.when(inner)
    def _():
        for cp in zo_copies():
            cp.wait_send()

    assert counter[0] <= ssem.shape[0]


def fused_shards(dims, tokens, segments, cotangent, query_weight, key_weight, value_weight, out_weight,
                 gate_weight, up_weight, down_weight, attn_gain, ffn_gain):
    R, D, H, FF, C, NF, NT, MICRO = dims
    L = C * R
    SR = D // (NF * C)
    NH = H // HEAD_DIM
    HP, KV, Y = 256, 2 * H, NF // 2
    HALF = Y * C * SR
    NO = Y * C - 1
    NG = NF * C - 1
    W = HP + KV
    ins = [
        ("tok_in", tokens.reshape(MICRO, R, D)),
        ("segr", segments),
        ("cot_in", cotangent.reshape(MICRO, R, D)),
        ("wq_in", query_weight),
        ("wk_in", key_weight),
        ("wv_in", value_weight),
        ("wo_in", out_weight),
        ("wg_in", gate_weight),
        ("wu_in", up_weight),
        ("wd_in", down_weight),
        ("gain_a_in", attn_gain[None]),
        ("gain_f_in", ffn_gain[None]),
    ]
    outs = [
        ("out", (MICRO, 1, R, D), BF),
        ("ig", (MICRO, 1, R, D), BF),
        ("out_q", (SR, H), F32),
        ("out_k", (SR, H), F32),
        ("out_v", (SR, H), F32),
        ("out_o", (SR, H), F32),
        ("out_g", (SR, FF), F32),
        ("out_u", (SR, FF), F32),
        ("out_d", (SR, FF), F32),
        ("out_ga", (1, SR), F32),
        ("out_gf", (1, SR), F32),
    ]
    v = pltpu.VMEM
    HR = R // 2
    scratch = [
        ("tok", v((MICRO, R, D), BF)), ("cot", v((MICRO * HR, D), BF)), ("dy", v((MICRO, HR, D), F32)),
        ("outv", v((MICRO, R, D), BF)), ("igb", v((MICRO, R, D), BF)),
        ("gz", v((NT, 2, D), F32)), ("gpart", v((2, D), F32)),
        ("lsem", pltpu.SemaphoreType.DMA((48,))),
        ("gmine", v((2, D), F32)), ("gall", v((NG, 2, D), F32)), ("gains", v((2, D), F32)),
        ("gacc", v((2, D), F32)), ("gin", v((NG, 2, D), F32)),
        ("wqkv", v((D, W), BF)), ("wo", v((D, D), BF)), ("woz", v((NT, SR, HP), BF)),
        ("wg", v((2, D, FF), BF)), ("wu", v((2, D, FF), BF)), ("wd", v((2, D, FF), BF)),
        ("segc", v((MICRO, L, 128), jnp.int32)),
        ("n1", v((MICRO * R, D), BF)), ("q", v((MICRO, R, HP), BF)),
        ("kv", v((MICRO, L, KV), BF)), ("kvT", v((MICRO, KV, L), BF)),
        ("oT", v((MICRO, HP, R), BF)), ("oX", v((MICRO, D, HR), BF)), ("onat", v((MICRO * HR, D), BF)),
        ("lse", v((MICRO, NH, 1, R), F32)),
        ("d2s", v((MICRO, HR, D), BF)), ("d2r", v((MICRO, HR, D), BF)),
        ("fps", v((MICRO, HR, D), BF)), ("fpr", v((MICRO, HR, D), BF)),
        ("snd", v((MICRO, R, D), BF)), ("rc1", v((MICRO, R, D), BF)), ("rc2", v((MICRO, HR, D), BF)),
        ("y1", v((MICRO, HR, D), F32)), ("n2", v((MICRO * HR, D), BF)), ("ar", v((MICRO * HR, D), BF)),
        ("big", v((3, 2, R, FF), BF)),
        ("doT", v((MICRO, HP, R), BF)), ("doS", v((D, HR), BF)),
        ("delta", v((NH, 1, R), F32)), ("dqT", v((H, R), F32)), ("dqkv", v((MICRO * R, W), BF)),
        ("dkv_own", v((MICRO, R, KV), F32)), ("dkv_in", v((MICRO, R, KV), BF)),
        ("gain_a_own", v((1, SR), BF)), ("gain_f_own", v((1, SR), BF)), ("fin_gain", v((2, 1, SR), F32)),
        ("wq_own", v((SR, H), BF)), ("wk_own", v((SR, H), BF)), ("wv_own", v((SR, H), BF)), ("wo_own", v((SR, H), BF)),
        ("fin_g", v((SR, FF), F32)), ("fin_u", v((SR, FF), F32)), ("fin_d", v((SR, FF), F32)),
        ("fin_qkv", v((3, SR, H), F32)), ("fin_o", v((SR, H), F32)),
        ("tmp", v((256, 512), F32)), ("zo", v((2, SR, HP), BF)), ("zq", v((NT, SR, HP), BF)),
    ]
    for k, cols in (("q", W), ("o", D), ("g", 2 * FF), ("u", 2 * FF), ("d", 2 * FF)):
        scratch += [("own_" + k, v((HALF, cols), F32)), ("rv_" + k, v((HALF, cols), BF)),
                    ("st_" + k, v((HALF, cols), BF)), ("pt_" + k, v((NO, SR, cols), BF))]
    for k in "gud":
        scratch += [("zs_" + k, v((SR, FF), BF)), ("zr_" + k, v((SR, FF), BF))]
    nsem = 320
    scratch += [("ssem", pltpu.SemaphoreType.DMA((nsem,))), ("rsem", pltpu.SemaphoreType.DMA((nsem,)))]
    names = [n for n, _ in ins] + [n for n, _, _ in outs] + [n for n, _ in scratch]
    def spec(name):
        return pl.BlockSpec(memory_space=pltpu.VMEM if name == "segr" else pl.ANY)

    res = pl.pallas_call(
        functools.partial(layer_kernel, dims, names),
        out_shape=[jax.ShapeDtypeStruct(s, d) for _, s, d in outs],
        in_specs=[spec(n) for n, _ in ins],
        out_specs=[spec(n) for n, _, _ in outs],
        scratch_shapes=[s for _, s in scratch],
        compiler_params=pltpu.CompilerParams(
            collective_id=0, has_side_effects=True, vmem_limit_bytes=67043328),
    )(*[a for _, a in ins])
    res = settle(res)
    return tuple(res[:9]) + (res[9].reshape(SR), res[10].reshape(SR))


def settle(arrays):
    pieces = []
    for n, a in enumerate(arrays):
        if a.ndim == 4:
            pieces += [(n, (m, 0, pl.ds(k * 256, 256))) for m in range(a.shape[0]) for k in range(a.shape[2] // 256)]
        else:
            pieces.append((n, None))

    kinds = [F32] * len(arrays)
    kinds[0] = arrays[0].dtype
    wide = [n for n, a in enumerate(arrays) if a.dtype != kinds[n]]

    def kernel(*refs):
        k = len(arrays)
        src, dst, buf, sem = refs[:k], refs[k:2 * k], refs[2 * k:3 * k], refs[3 * k:]
        last = list(buf)
        for i, n in enumerate(wide):
            last[n] = sem[2 + i]
        pick = lambda ref, at: ref if at is None else ref.at[at]
        come = [pltpu.make_async_copy(pick(src[n], at), pick(buf[n], at), sem[0].at[i]) for i, (n, at) in enumerate(pieces)]
        go = [pltpu.make_async_copy(pick(last[n], at), pick(dst[n], at), sem[1].at[i]) for i, (n, at) in enumerate(pieces)]
        for cp in come:
            cp.start()
        for a, b, (n, at) in zip(come, go, pieces):
            a.wait()
            if n in wide:
                last[n][at] = buf[n][at].astype(F32)
            b.start()
        for cp in go:
            cp.wait()

    hbm = pl.BlockSpec(memory_space=pl.ANY)
    return pl.pallas_call(
        kernel,
        out_shape=[jax.ShapeDtypeStruct(a.shape, d) for a, d in zip(arrays, kinds)],
        in_specs=[hbm] * len(arrays),
        out_specs=[hbm] * len(arrays),
        scratch_shapes=[pltpu.VMEM(a.shape, a.dtype) for a in arrays] + [pltpu.SemaphoreType.DMA((len(pieces),))] * 2
        + [pltpu.VMEM(arrays[n].shape, F32) for n in wide],
    )(*arrays)


def fits(dims, seqs):
    R, D, H, FF, C, NF, NT, MICRO = dims
    blocks = D % (16 * NF * C) == 0 and D % 256 == 0
    return (C, NT, NF, H, MICRO, seqs, R, FF) == (2, 4, 4, 192, 2, 1, 512, 512) and D <= 768 and blocks


SPECS = (
    P(None, "fsdp", "ctx", None),
    P(None, "fsdp", None),
    P(None, "fsdp", "ctx", None),
) + (P(("fsdp", "ctx"), "tp"),) * 7 + (P(("fsdp", "ctx")),) * 2
OUT_SPECS = (P(None, "fsdp", "ctx", None),) * 2 + (P(("fsdp", "ctx"), "tp"),) * 7 + (P(("fsdp", "ctx")),) * 2


def solution(mesh):
    nf, nc, nt = mesh.shape["fsdp"], mesh.shape["ctx"], mesh.shape["tp"]

    def chosen(*args):
        tokens, weight, ffw = args[0], args[3], args[7]
        micro, seqs, rows, width = tokens.shape
        dims = (rows, width, weight.shape[1], ffw.shape[1], nc, nf, nt, micro)
        return fused_shards(dims, *args) if fits(dims, seqs) else shards(*args)

    return jax.shard_map(chosen, mesh=mesh, in_specs=SPECS, out_specs=OUT_SPECS, check_vma=False)
```

```python
import functools

import jax
import jax.numpy as jnp
from jax import lax
from jax.experimental import pallas as pl
from jax.experimental.pallas import tpu as pltpu
from jax.sharding import PartitionSpec as P

HEAD_DIM = 64


EPS = 1e-06


def gather_weights(
    query_weight,
    key_weight,
    value_weight,
    out_weight,
    gate_weight,
    up_weight,
    down_weight,
    attn_gain,
    ffn_gain,
):
    return (
        lax.all_gather(query_weight, ("fsdp", "ctx"), axis=0, tiled=True),
        lax.all_gather(key_weight, ("fsdp", "ctx"), axis=0, tiled=True),
        lax.all_gather(value_weight, ("fsdp", "ctx"), axis=0, tiled=True),
        lax.all_gather(out_weight, ("fsdp", "ctx"), axis=0, tiled=True),
        lax.all_gather(gate_weight, ("fsdp", "ctx"), axis=0, tiled=True),
        lax.all_gather(up_weight, ("fsdp", "ctx"), axis=0, tiled=True),
        lax.all_gather(down_weight, ("fsdp", "ctx"), axis=0, tiled=True),
        lax.all_gather(attn_gain, ("fsdp", "ctx"), axis=0, tiled=True),
        lax.all_gather(ffn_gain, ("fsdp", "ctx"), axis=0, tiled=True),
    )


def tensor_sum(partial_value):
    return lax.psum(partial_value, "tp")


def normalize(values, gain_vec):
    return values * lax.rsqrt(jnp.mean(values * values, -1, keepdims=True) + EPS) * gain_vec


def gelu_mix(gate_act, up_act):
    return jax.nn.gelu(gate_act, approximate=True) * up_act


def contract_last(left_op, right_op):
    return lax.dot_general(
        left_op, right_op, (((1,), (1,)), ((), ())), preferred_element_type=jnp.float32
    )


def contract_first(left_op, right_op):
    return lax.dot_general(
        left_op, right_op, (((0,), (0,)), ((), ())), preferred_element_type=jnp.float32
    )


def masked_scores(queries, key_whole, query_seg, seg_all, head_count):
    local_rows = queries.shape[0]
    query_heads = queries.reshape(local_rows, head_count, HEAD_DIM)
    key_heads = key_whole.reshape(key_whole.shape[0], head_count, HEAD_DIM)
    products = jnp.einsum(
        "qhd,khd->hqk", query_heads, key_heads, preferred_element_type=jnp.float32
    ) * HEAD_DIM ** (-0.5)
    same_doc = query_seg[:, None] == seg_all[None, :]
    return jnp.where(same_doc[None], products, -1e30)


def forward_pass(inputs, seg_all, gathered, ctx_pos):
    w_query, w_key, w_value, w_out, w_gate, w_up, w_down, gain_attn, gain_ffn = gathered
    head_count = w_query.shape[1] // HEAD_DIM
    local_rows = inputs.shape[0]
    query_seg = lax.dynamic_slice_in_dim(seg_all, ctx_pos * local_rows, local_rows)
    inputs_f = inputs.astype(jnp.float32)
    normed_one = normalize(inputs_f, gain_attn.astype(jnp.float32)).astype(jnp.bfloat16)
    queries = jnp.dot(normed_one, w_query, preferred_element_type=jnp.float32).astype(jnp.bfloat16)
    key_local = jnp.dot(normed_one, w_key, preferred_element_type=jnp.float32).astype(jnp.bfloat16)
    value_local = jnp.dot(normed_one, w_value, preferred_element_type=jnp.float32).astype(
        jnp.bfloat16
    )
    key_whole, value_whole = (
        lax.all_gather(key_local, "ctx", axis=0, tiled=True),
        lax.all_gather(value_local, "ctx", axis=0, tiled=True),
    )
    scores = masked_scores(queries, key_whole, query_seg, seg_all, head_count)
    row_max = jnp.max(scores, -1, keepdims=True)
    row_total = jnp.sum(jnp.exp(scores - row_max), -1, keepdims=True)
    log_total = row_max + jnp.log(row_total)
    probs_low = jnp.exp(scores - log_total).astype(jnp.bfloat16)
    value_heads = value_whole.reshape(value_whole.shape[0], head_count, HEAD_DIM)
    attn_mixed = jnp.einsum(
        "hqk,khd->qhd", probs_low, value_heads, preferred_element_type=jnp.float32
    )
    attn_mixed = attn_mixed.reshape(local_rows, head_count * HEAD_DIM).astype(jnp.bfloat16)
    attn_partial = contract_last(attn_mixed, w_out)
    residual = inputs_f + tensor_sum(attn_partial)
    normed_two = normalize(residual, gain_ffn.astype(jnp.float32)).astype(jnp.bfloat16)
    gate_act = jnp.dot(normed_two, w_gate, preferred_element_type=jnp.float32)
    up_act = jnp.dot(normed_two, w_up, preferred_element_type=jnp.float32)
    hidden = gelu_mix(gate_act, up_act).astype(jnp.bfloat16)
    ffn_partial = contract_last(hidden, w_down)
    result = (residual + tensor_sum(ffn_partial)).astype(jnp.bfloat16)
    stored = (
        inputs_f,
        normed_one,
        queries,
        key_whole,
        value_whole,
        log_total,
        attn_mixed,
        residual,
        normed_two,
        gate_act,
        up_act,
        hidden,
        query_seg,
    )
    return (result, stored)


def backward_pass(cot_rows, stored, gathered, seg_all, ctx_pos):
    w_query, w_key, w_value, w_out, w_gate, w_up, w_down, gain_attn, gain_ffn = gathered
    (
        inputs_f,
        normed_one,
        queries,
        key_whole,
        value_whole,
        log_total,
        attn_mixed,
        residual,
        normed_two,
        gate_act,
        up_act,
        hidden,
        query_seg,
    ) = stored
    head_count = w_query.shape[1] // HEAD_DIM
    local_rows = queries.shape[0]
    seq_rows = key_whole.shape[0]
    scale = HEAD_DIM ** (-0.5)
    dout = cot_rows.astype(jnp.float32)
    dout_low = dout.astype(jnp.bfloat16)
    grad_down = contract_first(dout_low, hidden)
    dhidden = jnp.dot(dout_low, w_down, preferred_element_type=jnp.float32)
    mixed_unused, mix_back = jax.vjp(gelu_mix, gate_act, up_act)
    dgate, dup = mix_back(dhidden)
    dgate_low = dgate.astype(jnp.bfloat16)
    dup_low = dup.astype(jnp.bfloat16)
    grad_gate = contract_first(normed_two, dgate_low)
    grad_up = contract_first(normed_two, dup_low)
    dn2_partial = contract_last(dgate_low, w_gate) + contract_last(dup_low, w_up)
    norm_unused, norm_back = jax.vjp(normalize, residual, gain_ffn.astype(jnp.float32))
    dresid_norm, grad_gain_ffn = norm_back(tensor_sum(dn2_partial))
    dresidual = dout + dresid_norm
    dres_low = dresidual.astype(jnp.bfloat16)
    grad_out = contract_first(dres_low, attn_mixed)
    dmixed = jnp.dot(dres_low, w_out, preferred_element_type=jnp.float32).astype(jnp.bfloat16)
    dmixed_heads = dmixed.reshape(local_rows, head_count, HEAD_DIM)
    scores = masked_scores(queries, key_whole, query_seg, seg_all, head_count)
    prob_full = jnp.exp(scores - log_total)
    key_heads = key_whole.reshape(seq_rows, head_count, HEAD_DIM)
    value_heads = value_whole.reshape(seq_rows, head_count, HEAD_DIM)
    dprobs = jnp.einsum(
        "qhd,khd->hqk", dmixed_heads, value_heads, preferred_element_type=jnp.float32
    )
    row_delta = jnp.sum(prob_full * dprobs, -1, keepdims=True)
    dscores = (prob_full * (dprobs - row_delta)).astype(jnp.bfloat16)
    dquery = (
        jnp.einsum("hqk,khd->qhd", dscores, key_heads, preferred_element_type=jnp.float32) * scale
    )
    query_all, dmixed_all = (
        lax.all_gather(queries, "ctx", axis=0, tiled=True),
        lax.all_gather(dmixed, "ctx", axis=0, tiled=True),
    )
    log_all, delta_all = (
        lax.all_gather(log_total, "ctx", axis=1, tiled=True),
        lax.all_gather(row_delta, "ctx", axis=1, tiled=True),
    )
    start = ctx_pos * local_rows
    key_own = lax.dynamic_slice_in_dim(key_whole, start, local_rows)
    value_own = lax.dynamic_slice_in_dim(value_whole, start, local_rows).reshape(
        local_rows, head_count, HEAD_DIM
    )
    scores_own = masked_scores(query_all, key_own, seg_all, query_seg, head_count)
    prob_own = jnp.exp(scores_own - log_all)
    dmixed_all_heads = dmixed_all.reshape(seq_rows, head_count, HEAD_DIM)
    query_all_heads = query_all.reshape(seq_rows, head_count, HEAD_DIM)
    dprobs_own = jnp.einsum(
        "qhd,khd->hqk", dmixed_all_heads, value_own, preferred_element_type=jnp.float32
    )
    dscores_own = (prob_own * (dprobs_own - delta_all)).astype(jnp.bfloat16)
    dkey_local = (
        jnp.einsum("hqk,qhd->khd", dscores_own, query_all_heads, preferred_element_type=jnp.float32)
        * scale
    ).reshape(local_rows, head_count * HEAD_DIM)
    dvalue_local = jnp.einsum(
        "hqk,qhd->khd",
        prob_own.astype(jnp.bfloat16),
        dmixed_all_heads,
        preferred_element_type=jnp.float32,
    ).reshape(local_rows, head_count * HEAD_DIM)
    dquery_low = dquery.reshape(local_rows, head_count * HEAD_DIM).astype(jnp.bfloat16)
    dkey_low = dkey_local.astype(jnp.bfloat16)
    dvalue_low = dvalue_local.astype(jnp.bfloat16)
    grad_query = contract_first(normed_one, dquery_low)
    grad_key = contract_first(normed_one, dkey_low)
    grad_value = contract_first(normed_one, dvalue_low)
    dn1_partial = (
        contract_last(dquery_low, w_query)
        + contract_last(dkey_low, w_key)
        + contract_last(dvalue_low, w_value)
    )
    norm_unused_two, norm_back_two = jax.vjp(normalize, inputs_f, gain_attn.astype(jnp.float32))
    dinput_norm, grad_gain_attn = norm_back_two(tensor_sum(dn1_partial))
    input_grad = dresidual + dinput_norm
    grad_terms = (
        grad_query,
        grad_key,
        grad_value,
        grad_out,
        grad_gate,
        grad_up,
        grad_down,
        grad_gain_attn,
        grad_gain_ffn,
    )
    return (input_grad, grad_terms)


def shards(
    tokens,
    segments,
    cotangent,
    query_weight,
    key_weight,
    value_weight,
    out_weight,
    gate_weight,
    up_weight,
    down_weight,
    attn_gain,
    ffn_gain,
):
    ctx_pos = lax.axis_index("ctx")
    results = []
    input_grads = []
    total_grads = None
    for micro_step in range(tokens.shape[0]):
        seg_all = segments[micro_step, 0]
        gathered = gather_weights(
            query_weight,
            key_weight,
            value_weight,
            out_weight,
            gate_weight,
            up_weight,
            down_weight,
            attn_gain,
            ffn_gain,
        )
        result, stored = forward_pass(tokens[micro_step, 0], seg_all, gathered, ctx_pos)
        gathered = gather_weights(
            query_weight,
            key_weight,
            value_weight,
            out_weight,
            gate_weight,
            up_weight,
            down_weight,
            attn_gain,
            ffn_gain,
        )
        input_grad, grad_terms = backward_pass(
            cotangent[micro_step, 0], stored, gathered, seg_all, ctx_pos
        )
        results.append(result)
        input_grads.append(input_grad)
        total_grads = (
            grad_terms if total_grads is None else jax.tree.map(jnp.add, total_grads, grad_terms)
        )
    gain_attn_total = total_grads[7]
    gain_ffn_total = total_grads[8]
    owned = (
        lax.psum_scatter(total_grads[0], ("fsdp", "ctx"), scatter_dimension=0, tiled=True),
        lax.psum_scatter(total_grads[1], ("fsdp", "ctx"), scatter_dimension=0, tiled=True),
        lax.psum_scatter(total_grads[2], ("fsdp", "ctx"), scatter_dimension=0, tiled=True),
        lax.psum_scatter(total_grads[3], ("fsdp", "ctx"), scatter_dimension=0, tiled=True),
        lax.psum_scatter(total_grads[4], ("fsdp", "ctx"), scatter_dimension=0, tiled=True),
        lax.psum_scatter(total_grads[5], ("fsdp", "ctx"), scatter_dimension=0, tiled=True),
        lax.psum_scatter(total_grads[6], ("fsdp", "ctx"), scatter_dimension=0, tiled=True),
        lax.psum_scatter(gain_attn_total, ("fsdp", "ctx"), scatter_dimension=0, tiled=True),
        lax.psum_scatter(gain_ffn_total, ("fsdp", "ctx"), scatter_dimension=0, tiled=True),
    )
    output = jnp.stack(results)[:, None]
    input_grad_all = jnp.stack(input_grads)[:, None]
    return (
        output,
        input_grad_all,
        owned[0],
        owned[1],
        owned[2],
        owned[3],
        owned[4],
        owned[5],
        owned[6],
        owned[7],
        owned[8],
    )


NEG = -1e30
MESH = pl.DeviceIdType.MESH
BF = jnp.bfloat16
F32 = jnp.float32
GELU_K = 0.7978845608028654
GELU_A = 0.044715
ORDER = (
    ("prep",), ("qR",), ("P", 0), ("wS", "g1"), ("P", 1), ("wX", "g0"), ("wY", "g0"), ("wX", "d0"), ("wS", "o"),
    ("wS", "u1"), ("wX", "g1"), ("wS", "d1"), ("AT", 0, 0), ("AT", 0, 1), ("wX", "u0"), ("AT", 1, 0), ("wX", "o"),
    ("wY", "d0"), ("wY", "g1"), ("wY", "u0"), ("AT", 1, 1), ("wX", "u1"), ("wF", 0), ("wX", "d1"), ("O", 0),
    ("wY", "o"), ("wY", "u1"), ("wF", "o"), ("F1", 0), ("wY", "d1"), ("FS", 0, 0), ("wF", 1), ("FS", 0, 1), ("FP", 0),
    ("O", 1), ("F1", 1), ("FS", 1, 0), ("FS", 1, 1), ("G", "d"), ("BN", 0, 0), ("BN", 0, 1), ("FP", 1), ("SQ", "d"),
    ("G", "g"), ("ON", 0, 0), ("BS", 0), ("G", "u"), ("ON", 0, 1), ("PE", 0), ("OF", 0, 0), ("OF", 0, 1), ("SF", "d"),
    ("BN", 1, 0), ("BN", 1, 1), ("OW", 0), ("J", 0), ("BS", 1), ("ON", 1, 0), ("PE", 1), ("G", "o"), ("ON", 1, 1),
    ("SQ", "o"), ("OF", 1, 0), ("X", 0, 0), ("OW", 1), ("OF", 1, 1), ("X", 0, 1), ("J", 1), ("IN", 0, 0), ("SF", "o"),
    ("SQ", "g"), ("IF", 0, 0), ("IN", 0, 1), ("G", "q"), ("X", 1, 0), ("SQ", "u"), ("IF", 0, 1), ("X", 1, 1), ("GZ",),
    ("IN", 1, 0), ("SF", "g"), ("SQ", "q"), ("IF", 1, 0), ("SZ", "o"), ("GR",), ("IN", 1, 1), ("SZ", "d"),
    ("SF", "q"), ("GF",), ("SZ", "g"), ("SF", "u"), ("IF", 1, 1), ("SZ", "u"),
)


def dot_nn(a, b):
    return lax.dot_general(a, b, (((1,), (0,)), ((), ())), preferred_element_type=F32)


def dot_nt(a, b):
    return lax.dot_general(a, b, (((1,), (1,)), ((), ())), preferred_element_type=F32)


def dot_tn(a, b):
    return lax.dot_general(a, b, (((0,), (0,)), ((), ())), preferred_element_type=F32)


def at(i, n):
    return pl.ds(pl.multiple_of(i, n), n)


def layer_kernel(dims, names, *refs):
    r = dict(zip(names, refs))
    R, D, H, FF, C, NF, NT, MICRO = dims
    L = C * R
    NH = H // HEAD_DIM
    HP = 256
    KV = 2 * H
    Y = NF // 2
    SR = D // (NF * C)
    RT = 256
    CH = 128
    UNIT = 64
    NCH = R // CH
    f = lax.axis_index("fsdp")
    c = lax.axis_index("ctx")
    t = lax.axis_index("tp")
    core = lax.rem(f, 2)
    y = f // 2
    shard = f * C + c
    partner = {"fsdp": f + 1 - 2 * core}
    ssem, rsem = r["ssem"], r["rsem"]
    counter = [0]

    def slot():
        counter[0] += 1
        return counter[0] - 1

    def copy_to(src, dst, idx, dev, sidx=None):
        return pltpu.make_async_remote_copy(
            src_ref=src, dst_ref=dst, send_sem=ssem.at[idx if sidx is None else sidx], recv_sem=rsem.at[idx],
            device_id=dev, device_id_type=MESH)

    offsets = [(dy, dc) for dy in range(Y) for dc in range(C) if (dy, dc) != (0, 0)]

    def square(off):
        dy, dc = off
        return (2 * lax.rem(y + dy, Y) + core, lax.rem(c + dc, C))

    def square_from(off):
        dy, dc = off
        return (2 * lax.rem(y + Y - dy, Y) + core, lax.rem(c + C - dc, C))

    def dev_sq(off):
        pf, pc = square(off)
        return {"fsdp": pf, "ctx": pc}

    def z_to(k):
        return {"tp": lax.rem(t + k, NT)}

    group = [(df, dc) for df in range(NF) for dc in range(C) if (df, dc) != (0, 0)]

    def dev_group(off):
        return {"fsdp": lax.rem(f + off[0], NF), "ctx": lax.rem(c + off[1], C)}

    half = t // 2
    inner = (t == 1) | (t == 2)
    outer = (t == 0) | (t == 3)
    mate = {"tp": t + 1 - 2 * lax.rem(t, 2)}
    twin_t = lax.rem(t + 2, NT)
    twin = {"tp": twin_t}
    cross = {"tp": NT - 1 - t}
    HR = R // 2
    SUB = HR // CH
    hrows = at(half * HR, HR)

    def both(do_inner, do_outer):
        pl.when(inner)(do_inner)
        pl.when(outer)(do_outer)

    local = r["lsem"]

    def load(src, dst, n):
        cp = pltpu.make_async_copy(src, dst, local.at[n])
        cp.start()
        return cp

    own_rows = at(shard * SR, SR)
    wqkv, wo, woz, wg, wu, wd = r["wqkv"], r["wo"], r["woz"], r["wg"], r["wu"], r["wd"]
    load_first = [load(r[n + "_in"], r[n + "_own"], 3 + i) for i, n in enumerate(("gain_a", "gain_f", "wq", "wk", "wv"))]
    load_out = load(r["wo_in"], r["wo_own"], 8)
    load_ffn = [load(r[n + "_in"], r[n].at[0, own_rows], 9 + i) for i, n in enumerate(("wg", "wu", "wd"))]
    load_tok = load(r["tok_in"], r["tok"], 0)
    load_cot = [load(r["cot_in"].at[m, hrows], r["cot"].at[pl.ds(m * HR, HR)], 1 + m) for m in range(MICRO)]

    bar = pltpu.get_barrier_semaphore()
    for off in group:
        pl.semaphore_signal(bar, inc=1, device_id=dev_group(off), device_id_type=MESH)
    for k in range(1, NT):
        pl.semaphore_signal(bar, inc=1, device_id=z_to(k), device_id_type=MESH)

    def spot(width, shift):
        i = lax.broadcasted_iota(jnp.int32, (H, width), 0)
        j = lax.broadcasted_iota(jnp.int32, (H, width), 1)
        return (j == i + shift).astype(BF)

    W = HP + KV
    VOFF = HP - H
    gm = r["gmine"]
    cols = lax.broadcasted_iota(jnp.int32, (SR, D), 1)
    rows = lax.broadcasted_iota(jnp.int32, (SR, D), 0)
    place = (cols == rows + shard * SR).astype(BF)
    for cp in load_first:
        cp.wait()
    gm[...] = jnp.zeros_like(gm)
    gm[0:1, :] = dot_nn(r["gain_a_own"][...], place)
    gm[1:2, :] = dot_nn(r["gain_f_own"][...], place)
    wqkv[own_rows, :] = (dot_nn(r["wq_own"][...], spot(W, 0)) + dot_nn(r["wk_own"][...], spot(W, HP))
                         + dot_nn(r["wv_own"][...], spot(W, HP + H))).astype(BF)
    load_out.wait()
    woz[t] = dot_nn(r["wo_own"][...], spot(HP, 0)).astype(BF)
    for cp in load_ffn:
        cp.wait()
    pl.semaphore_wait(bar, len(group) + NT - 1)

    sends, weight_sends = [], []

    def send(src, dst, idx, dev, group=None):
        cp = copy_to(src, dst, idx, dev)
        cp.start()
        (sends if group is None else group).append(cp)
        return cp

    def rows_of(off):
        pf, pc = square_from(off)
        return at((pf * C + pc) * SR, SR)

    class Spread:
        def __init__(self, buf, view, far, group):
            self.buf, self.view, self.far, self.group = buf, view, far, group
            self.ix = {off: slot() for off in offsets}
            self.px = slot()
            self.rx = {off: slot() for off in offsets}

        def rows(self, off):
            return self.view(self.buf, rows_of(off))

        def start(self):
            w = self.view(self.buf, own_rows)
            for off in offsets:
                if self.far or 0 in off:
                    send(w, w, self.ix[off], dev_sq(off), self.group)
            send(w, w, self.px, partner, self.group)

        def relay_x(self):
            w = self.rows((0, 1))
            copy_to(w, w, self.ix[(0, 1)], partner).wait_recv()
            if not self.far:
                send(w, w, self.ix[(1, 1)], dev_sq((1, 0)), self.group)
            send(w, w, self.rx[(0, 1)], partner, self.group)

        def relay_y(self):
            for off in ((1, 0), (1, 1)):
                w = self.rows(off)
                copy_to(w, w, self.ix[off], partner).wait_recv()
                send(w, w, self.rx[off], partner, self.group)

        def finish(self):
            w = self.view(self.buf, own_rows)
            copy_to(w, w, self.px, partner).wait_recv()
            for off in offsets:
                copy_to(w, w, self.rx[off], partner).wait_recv()

    flat = lambda buf, rows: buf.at[rows]
    deep = lambda buf, rows: buf.at[:, rows]
    gall = r["gall"]
    gain_cp = [send(gm, gall.at[n], slot(), dev_group(off)) for n, off in enumerate(group)]
    qkv_sp = Spread(wqkv, flat, True, sends)
    qkv_sp.start()
    twin_ix = {}
    for k, buf in (("g", wg), ("u", wu), ("d", wd)):
        twin_ix[k] = slot()
        send(buf.at[0, own_rows], buf.at[1, own_rows], twin_ix[k], twin, weight_sends)
    spreads = {k + str(n): Spread(b.at[n], flat, False, weight_sends) for n in range(2) for k, b in (("g", wg), ("u", wu), ("d", wd))}
    spreads["o"] = Spread(wo, flat, False, sends)
    for k in "gud":
        spreads[k + "0"].start()
    wo_ix = [slot() for _ in range(1, NT)]
    for k, i in zip(range(1, NT), wo_ix):
        send(woz.at[t], woz.at[t], i, z_to(k))
    segr, segc = r["segr"].at[:, 0], r["segc"]
    gains, gacc, oT, oX = r["gains"], r["gacc"], r["oT"], r["oX"]
    tok, cot, n1 = r["tok"], r["cot"], r["n1"]

    def prepare():
        for m in range(MICRO):
            for b in range(L // 128):
                row = segr[m:m + 1, 128 * b:128 * b + 128].astype(F32)
                segc[m, 128 * b:128 * b + 128, :] = jnp.broadcast_to(row, (128, 128)).T.astype(jnp.int32)
        for cp in gain_cp:
            cp.wait_recv()
        gsum = gm[...]
        for n in range(len(group)):
            gsum = gsum + gall[n]
        gains[...] = gsum
        load_tok.wait()
        for m in range(MICRO):
            norm_one(m)
        gacc[...] = jnp.zeros_like(gacc)

    def norm_one(m):
        @pl.loop(0, R // CH)
        def _(i):
            xf = tok[m, at(i * CH, CH), :].astype(F32)
            rs = lax.rsqrt(jnp.mean(xf * xf, -1, keepdims=True) + EPS)
            n1[at(m * R + i * CH, CH), :] = (xf * rs * gains[0:1, :]).astype(BF)

    q, kv, kvT = r["q"], r["kv"], r["kvT"]
    scale = HEAD_DIM ** -0.5
    def qkv_ready():
        qkv_sp.relay_x()
        qkv_sp.relay_y()
        qkv_sp.finish()

    kv_ix = [slot() for _ in range(MICRO)]
    other = {"ctx": lax.rem(c + 1, C)}

    def project(m):
        @pl.loop(0, R // RT)
        def _(i):
            acc = dot_nn(n1[at(m * R + i * RT, RT), :], wqkv[...])
            q[m, at(i * RT, RT), :] = (acc[:, 0:HP] * scale).astype(BF)
            kv[m, at(c * R + i * RT, RT), :] = acc[:, HP:HP + KV].astype(BF)
        w = kv.at[m, at(c * R, R)]
        send(w, w, kv_ix[m], other)
        flip(m, c * R)

    def spread(w):
        if w == "o":
            for k, i in zip(range(1, NT), wo_ix):
                copy_to(woz.at[t], woz.at[t], i, z_to(k)).wait_recv()
            i = lax.broadcasted_iota(jnp.int32, (HP, D), 0)
            j = lax.broadcasted_iota(jnp.int32, (HP, D), 1)
            row = dot_nn(woz[0], (j == i).astype(BF))
            for k in range(1, NT):
                row = row + dot_nn(woz[k], (j == i + k * H).astype(BF))
            wo[own_rows, :] = row.astype(BF)
        else:
            v = {"g": wg, "u": wu, "d": wd}[w[0]].at[0, own_rows]
            copy_to(v, v, twin_ix[w[0]], twin).wait_recv()
        spreads[w].start()

    def weights_ready(n):
        for k in ["o"] if n == "o" else [w + str(n) for w in "gud"]:
            spreads[k].finish()

    onat, lse = r["onat"], r["lse"]
    lanes = lax.broadcasted_iota(jnp.int32, (RT, HP), 1)

    def head_mask(v, h, shift):
        lo = shift + h * HEAD_DIM
        return jnp.where((lanes >= lo) & (lanes < lo + HEAD_DIM), v, jnp.zeros_like(v))

    def flip(m, start):
        @pl.loop(0, R // RT)
        def _(i):
            kvT[m, :, at(start + i * RT, RT)] = kv[m, at(start + i * RT, RT), :].T

    def attend(m, i):
        kk = kv[m, :, 0:HP]
        sc = segc[m]
        sc = jnp.concatenate([sc] * (RT // 128), axis=1)
        sr = segr[m:m + 1, at(c * R + i * RT, RT)]
        qq = q[m, pl.ds(i * RT, RT), :]
        for h in range(NH):
            s = dot_nt(kk, head_mask(qq, h, 0))
            s = jnp.where(sc == sr, s, NEG)
            mx = jnp.max(s, axis=0, keepdims=True)
            e = jnp.exp(s - mx)
            tot = jnp.sum(e, axis=0, keepdims=True)
            p = (e * (1.0 / tot)).astype(BF)
            vT = kvT[m, H + h * HEAD_DIM:H + (h + 1) * HEAD_DIM, :]
            lo = VOFF + h * HEAD_DIM
            oT[m, lo:lo + HEAD_DIM, pl.ds(i * RT, RT)] = dot_nn(vT, p).astype(BF)
            lse[m, h, :, pl.ds(i * RT, RT)] = mx + jnp.log(tot)

    o_ix = [[slot() for _ in range(3)] for _ in range(MICRO)]

    def o_send(m, i, n):
        src = oT.at[m, pl.ds(VOFF, H), pl.ds(i * HR, HR)]
        return copy_to(src, oX.at[m, at(t * H, H)], o_ix[m][n], (mate, twin, cross)[n])

    def share_o(m, i):
        @pl.when(half == i)
        def _():
            o_send(m, i, 0).start()

        @pl.when(half != i)
        def _():
            o_send(m, i, 1).start()
            o_send(m, i, 2).start()

    def wait_o(m):
        for n in range(3):
            o_send(m, 0, n).wait_recv()

    def close_o(m):
        for n in range(3):
            o_send(m, 0, n).wait_send()

    def attend_tile(m, i):
        if i == 0:
            w = kv.at[m, at(c * R, R)]
            copy_to(w, w, kv_ix[m], other).wait_recv()
            flip(m, lax.rem(c + 1, C) * R)
        attend(m, i)
        share_o(m, i)

    y1, n2, big, dy = r["y1"], r["n2"], r["big"], r["dy"]
    d2s, d2r, fps, fpr = r["d2s"], r["d2r"], r["fps"], r["fpr"]
    d2_ix = [[slot() for _ in range(SUB)] for _ in range(MICRO)]
    fp_ix = [[slot() for _ in range(SUB)] for _ in range(MICRO)]

    def to_mate(src, dst, ix, m, j):
        rr = pl.ds(j * CH, CH)
        return copy_to(src.at[m, rr], dst.at[m, rr], ix[m][j], mate)

    def feed(m):
        oX[m, at(t * H, H), :] = oT[m, VOFF:HP, hrows]
        mr = pl.ds(m * HR, HR)
        onat[mr, :] = oX[m].T
        acc = tok[m, hrows, :].astype(F32)
        acc = acc + dot_nt(onat[mr, :], wo[...])
        y1[m] = acc
        rs = lax.rsqrt(jnp.mean(acc * acc, -1, keepdims=True) + EPS)
        n2[mr, :] = (acc * rs * gains[1:2, :]).astype(BF)

    def feed_slot(m, n):
        if (m, n) == fed[0]:
            for cp in load_cot:
                cp.wait()
        mr = pl.ds(m * HR, HR)
        n2v = n2[mr, :]
        g = dot_nn(n2v, wg[n])
        u = dot_nn(n2v, wu[n])
        th = jnp.tanh(GELU_K * (g + GELU_A * g * g * g))
        hf = 0.5 * (1.0 + th)
        gl = g * hf
        big[0, n, mr, :] = (gl * u).astype(BF)
        dh = dot_nn(cot[mr, :], wd[n])
        dgl = hf + 0.5 * g * (1.0 - th * th) * (GELU_K * (1.0 + 3.0 * GELU_A * g * g))
        dgv = (dh * u * dgl).astype(BF)
        duv = (dh * gl).astype(BF)
        big[1, n, mr, :] = dgv
        big[2, n, mr, :] = duv
        d2 = dot_nt(dgv, wg[n]) + dot_nt(duv, wu[n])
        if n == 0:
            dy[m] = d2
            return
        d2 = dy[m] + d2
        d2s[m] = d2.astype(BF)

        @pl.when(outer)
        def _():
            for j in range(SUB):
                to_mate(d2s, d2r, d2_ix, m, j).start()

        yn = y1[m]
        rs = lax.rsqrt(jnp.mean(yn * yn, -1, keepdims=True) + EPS)
        gacc[1:2, :] += jnp.sum(d2 * (yn * rs), axis=0, keepdims=True)
        fps[m] = (dot_nt(big[0, 0, mr, :], wd[0]) + dot_nt(big[0, 1, mr, :], wd[1])).astype(BF)

    def feed_out(m):
        @pl.when(outer)
        def _():
            for j in range(SUB):
                to_mate(fps, fpr, fp_ix, m, j).start()

    class Reduce:
        def __init__(self, k, pieces, put):
            self.own, self.half, self.recv, self.parts = r["own_" + k], r["st_" + k], r["rv_" + k], r["pt_" + k]
            self.pieces, self.put = pieces, put
            self.px = slot()
            self.ix = [slot() for _ in offsets]

        def pair_copy(self):
            return copy_to(self.half, self.recv, self.px, partner)

        def pair(self):
            tmp = r["tmp"]
            for left, right, c0, width in self.pieces:
                @pl.loop(0, D // RT)
                def _(i, left=left, right=right, c0=c0, width=width):
                    tmp[:, 0:width] = dot_tn(left[:, at(i * RT, RT)], right[...])

                    @pl.loop(0, RT // UNIT)
                    def _(p):
                        row = i * RT + p * UNIT
                        b = row // (C * SR)
                        to = at((b // 2) * C * SR + lax.rem(row, C * SR), UNIT)
                        part = tmp[at(p * UNIT, UNIT), 0:width]

                        @pl.when(lax.rem(b, 2) == core)
                        def _():
                            self.own[to, c0:c0 + width] = part

                        @pl.when(lax.rem(b, 2) != core)
                        def _():
                            self.half[to, c0:c0 + width] = part.astype(BF)
            self.pair_copy().start()

        def block(self, n):
            pf, pc = square(offsets[n])
            src = self.half.at[at(((pf // 2) * C + pc) * SR, SR)]
            return copy_to(src, self.parts.at[n], self.ix[n], dev_sq(offsets[n]))

        def square(self):
            self.pair_copy().wait()
            tot = self.own[...] + self.recv[...].astype(F32)
            self.own[...] = tot
            self.half[...] = tot.astype(BF)
            for n in range(len(offsets)):
                self.block(n).start()

        def finish(self):
            tot = self.own[at((y * C + c) * SR, SR), :]
            for n in range(len(offsets)):
                self.block(n).wait()
            for n in range(len(offsets)):
                tot = tot + self.parts[n].astype(F32)
            self.put(tot)

    zs_ix = {k: slot() for k in "gud"}

    def twin_sum(k):
        def put(tot):
            r["fin_" + k][...] = tot[:, 0:FF]
            r["zs_" + k][...] = tot[:, FF:2 * FF].astype(BF)
            send(r["zs_" + k], r["zr_" + k], zs_ix[k], twin)
        return put

    def split_qkv(tot):
        r["fin_qkv"][0] = tot[:, 0:H]
        r["fin_qkv"][1] = tot[:, HP:HP + H]
        r["fin_qkv"][2] = pltpu.roll(tot[:, W - HP:W], HP - VOFF, 1)[:, 0:H]
        for n, k in enumerate("qkv"):
            store(r["fin_qkv"].at[n], r["out_" + k])

    zo, zq = r["zo"], r["zq"]
    zo_ix, zo_sx = [slot(), slot()], slot()

    def zo_copies():
        out = []
        for dev, ix, sx in ((mate, zo_ix[0], None), (twin, zo_ix[1], None), (cross, zo_ix[1], zo_sx)):
            out.append(copy_to(zq.at[dev["tp"]], zo.at[half], ix, dev, sx))
        return out

    def out_sum(tot):
        for k in range(NT):
            base = k * H // 128 * 128
            part = tot[:, base:base + HP]
            zq[k] = (pltpu.roll(part, HP - (k * H - base), 1) if k * H > base else part).astype(BF)
        zo[half] = zq[t]
        for cp in zo_copies():
            cp.start()

    dqkv, ar = r["dqkv"], r["ar"]
    pieces = {
        "d": [(cot, big.at[0, n], n * FF, FF) for n in range(2)],
        "g": [(n2, big.at[1, n], n * FF, FF) for n in range(2)],
        "u": [(n2, big.at[2, n], n * FF, FF) for n in range(2)],
        "q": [(n1, dqkv.at[:, pl.ds(0, 512)], 0, 512), (n1, dqkv.at[:, pl.ds(512, W - 512)], 512, W - 512)],
        "o": [(ar, onat.at[:, pl.ds(0, 512)], 0, 512), (ar, onat.at[:, pl.ds(512, D - 512)], 512, D - 512)],
    }
    puts = {"d": twin_sum("d"), "g": twin_sum("g"), "u": twin_sum("u"), "q": split_qkv, "o": out_sum}
    reds = {k: Reduce(k, pieces[k], puts[k]) for k in "dguqo"}

    def reduce_step(k, what):
        if k == "o":
            pl.when(inner)(lambda: getattr(reds[k], what)())
        else:
            getattr(reds[k], what)()

    def last_sum(k):
        if k == "o":
            both(lambda: zo_copies()[1].wait_recv(), lambda: [cp.wait_recv() for cp in zo_copies()[:2]] and None)
            tot = zo[0].astype(F32) + zo[1].astype(F32)
            r["fin_o"][...] = tot[:, 0:H]
            store(r["fin_o"], r["out_o"])
        elif k != "q":
            copy_to(r["zs_" + k], r["zr_" + k], zs_ix[k], twin).wait_recv()
            r["fin_" + k][...] += r["zr_" + k][...].astype(F32)
            store(r["fin_" + k], r["out_" + k])

    doT, doS = r["doT"], r["doS"]
    do_ix = [[[slot(), slot()] for _ in range(SUB)] for _ in range(MICRO)]
    do_sx = [[slot() for _ in range(SUB)] for _ in range(MICRO)]

    def do_copies(m, j):
        out = []
        to = doT.at[m, pl.ds(VOFF, H), pl.ds(pl.multiple_of(half * HR + j * CH, CH), CH)]
        for dev, n, sx in ((mate, 0, None), (twin, 1, None), (cross, 1, do_sx[m][j])):
            src = doS.at[at(dev["tp"] * H, H), pl.ds(j * CH, CH)]
            out.append(copy_to(src, to, do_ix[m][j][n], dev, sx))
        return out

    def back_norm(m, j):
        @pl.when(inner)
        def _():
            to_mate(d2s, d2r, d2_ix, m, j).wait_recv()
            if m:
                for cp in do_copies(m - 1, j):
                    cp.wait_send()
            rr = pl.ds(j * CH, CH)
            gr = pl.ds(m * HR + j * CH, CH)
            yv = y1[m, rr, :]
            d2 = d2s[m, rr, :].astype(F32) + d2r[m, rr, :].astype(F32)
            tv = lax.rsqrt(jnp.mean(yv * yv, -1, keepdims=True) + EPS)
            e2 = gains[1:2, :] * d2
            dot = jnp.mean(yv * e2, -1, keepdims=True)
            dv = cot[gr, :].astype(F32) + tv * e2 - yv * (tv * tv * tv * dot)
            dy[m, rr, :] = dv
            av = dv.astype(BF)
            ar[gr, :] = av
            doS[:, rr] = dot_nn(av, wo[...]).astype(BF).T
            doT[m, VOFF:HP, pl.ds(pl.multiple_of(half * HR + j * CH, CH), CH)] = doS[at(t * H, H), rr]
            for cp in do_copies(m, j):
                cp.start()

    delta, dqT, dkv_in, dkv_own = r["delta"], r["dqT"], r["dkv_in"], r["dkv_own"]
    dkv_out = wg.at[:, pl.ds(0, R), pl.ds(0, KV)]
    lay = [(0, 0), (0, HP), (1, 0)]
    qm = [wd.at[a, pl.ds(0, R), pl.ds(b, HP)] for a, b in lay]
    dom = [wu.at[a, pl.ds(0, R), pl.ds(b, HP)] for a, b in lay]

    def back_start(m):
        if m == 0:
            for cp in weight_sends:
                cp.wait_send()
        for j in range(SUB):
            cps = do_copies(m, j)
            both(lambda: cps[1].wait_recv(), lambda: [cp.wait_recv() for cp in cps[:2]] and None)

        @pl.loop(0, R // RT)
        def _(i):
            rr = at(i * RT, RT)
            dov = doT[m, :, rr].T
            for h in range(NH):
                lo = VOFF + h * HEAD_DIM
                prod = doT[m, lo:lo + HEAD_DIM, rr].astype(F32) * oT[m, lo:lo + HEAD_DIM, rr].astype(F32)
                delta[h, :, rr] = jnp.sum(prod, axis=0, keepdims=True)
                dom[h][rr, :] = head_mask(dov, h, VOFF)
                qm[h][rr, :] = head_mask(q[m, rr, :], h, 0)

    def back_half(m, key0, first):
        @pl.loop(0, R // RT)
        def _(i):
            sc = segc[m, at(key0, R), :]
            sc = jnp.concatenate([sc] * (RT // 128), axis=1)
            sr = segr[m:m + 1, at(c * R + i * RT, RT)]
            cs = at(i * RT, RT)
            for h in range(NH):
                s = dot_nt(kv[m, at(key0, R), 0:HP], qm[h][cs, :])
                s = jnp.where(sc == sr, s, NEG)
                p = jnp.exp(s - lse[m, h, :, cs])
                dp = dot_nt(kv[m, at(key0, R), KV - HP:KV], dom[h][cs, :])
                big[h, 1, :, cs] = p.astype(BF)
                big[h, 0, :, cs] = (p * (dp - delta[h, :, cs])).astype(BF)

        dst = dkv_out if first else dkv_own

        @pl.loop(0, R // RT)
        def _(i):
            rr = at(i * RT, RT)
            dk = dot_nn(big[0, 0, rr, :], qm[0][...])
            dv = dot_nn(big[0, 1, rr, :], dom[0][...])
            for h in range(1, NH):
                dk = dk + dot_nn(big[h, 0, rr, :], qm[h][...])
                dv = dv + dot_nn(big[h, 1, rr, :], dom[h][...])
            dst[m, rr, 0:128] = dk[:, 0:128].astype(dst.dtype)
            dst[m, rr, 128:256] = (dk[:, 128:256] + dv[:, 0:128]).astype(dst.dtype)
            dst[m, rr, 256:384] = dv[:, 128:256].astype(dst.dtype)
        for h in range(NH):
            hs = pl.ds(h * HEAD_DIM, HEAD_DIM)
            part = dot_nn(kvT[m, hs, at(key0, R)], big[h, 0])
            if first:
                dqT[hs, :] = part
            else:
                dqT[hs, :] = dqT[hs, :] + part

    dkv_ix = [slot() for _ in range(MICRO)]

    def back_peer(m):
        back_half(m, lax.rem(c + 1, C) * R, True)
        send(dkv_out.at[m], dkv_in.at[m], dkv_ix[m], other)

    def back_own(m):
        back_half(m, c * R, False)
        dqkv[pl.ds(m * R, R), 0:HP] = jnp.zeros((R, HP), BF)
        dqkv[pl.ds(m * R, R), 0:H] = (dqT[...] * scale).T.astype(BF)

    snd, rc1, rc2, igb = r["snd"], r["rc1"], r["rc2"], r["igb"]
    in_ix = [[[slot() for _ in range(SUB)] for _ in range(2)] for _ in range(MICRO)]
    sw_ix = [[slot() for _ in range(SUB)] for _ in range(MICRO)]

    def piece(own, j):
        return pl.ds(pl.multiple_of((half if own else 1 - half) * HR + j * CH, CH), CH)

    def inward(m, own, j):
        rr = piece(own, j)
        return copy_to(snd.at[m, rr], rc1.at[m, rr], in_ix[m][own][j], mate)

    def swap(m, j):
        return copy_to(snd.at[m, piece(0, j)], rc2.at[m, pl.ds(j * CH, CH)], sw_ix[m][j], cross)

    def join(m):
        copy_to(dkv_out.at[m], dkv_in.at[m], dkv_ix[m], other).wait_recv()
        for own in range(2):
            base = (half if own else 1 - half) * HR
            rr = at(base, HR)
            gr = pl.ds(pl.multiple_of(m * R + base, HR), HR)
            dqkv[gr, HP:HP + KV] = (dkv_own[m, rr, :] + dkv_in[m, rr, :].astype(F32)).astype(BF)
            d1 = dot_nt(dqkv[gr, :], wqkv[...])
            snd[m, rr, :] = d1.astype(BF)

            @pl.when(outer)
            def _(own=own):
                for j in range(SUB):
                    inward(m, own, j).start()

            xv = tok[m, rr, :].astype(F32)
            rs = lax.rsqrt(jnp.mean(xv * xv, -1, keepdims=True) + EPS)
            gacc[0:1, :] += jnp.sum(d1 * (xv * rs), axis=0, keepdims=True)

    def cross_over(m, j):
        @pl.when(inner)
        def _():
            inward(m, 0, j).wait_recv()
            rr = piece(0, j)
            snd[m, rr, :] = (snd[m, rr, :].astype(F32) + rc1[m, rr, :].astype(F32)).astype(BF)
            swap(m, j).start()

    class Result:
        def __init__(self, buf, name):
            self.buf, self.name = buf, name
            self.ix = [[[slot() for _ in range(3)] for _ in range(SUB)] for _ in range(MICRO)]

        def copy(self, m, j, n):
            at_ = self.buf.at[m, piece(n != 2, j)]
            return copy_to(at_, at_, self.ix[m][j][n], cross if n == 1 else mate)

        def arrived(self, m, j, n):
            at_ = self.buf.at[m, piece(0, j)]
            copy_to(at_, at_, self.ix[m][j][n], mate).wait_recv()

        def store(self, m, j, own):
            rr = piece(own, j)
            store(self.buf.at[m, rr], r[self.name].at[m, 0, rr])

        def near(self, m, j, make):
            def one():
                make(m, j)
                self.copy(m, j, 1).start()
                self.copy(m, j, 0).start()
            both(one, lambda: self.arrived(m, j, 0))
            self.store(m, j, 1)

        def far(self, m, j):
            def one():
                self.arrived(m, j, 1)
                self.copy(m, j, 2).start()
            both(one, lambda: self.arrived(m, j, 2))
            self.store(m, j, 0)

        def close(self, m, j):
            @pl.when(inner)
            def _():
                for n in range(3):
                    self.copy(m, j, n).wait_send()

    stores = []

    def store(src, dst):
        cp = pltpu.make_async_copy(src, dst, local.at[12 + len(stores)])
        cp.start()
        stores.append(cp)

    def make_output(m, j):
        to_mate(fps, fpr, fp_ix, m, j).wait_recv()
        rr = pl.ds(j * CH, CH)
        tot = y1[m, rr, :] + (fps[m, rr, :].astype(F32) + fpr[m, rr, :].astype(F32))
        r["outv"][m, piece(1, j), :] = tot.astype(BF)

    def make_input_grad(m, j):
        inward(m, 1, j).wait_recv()
        swap(m, j).wait_recv()
        rr = pl.ds(j * CH, CH)
        here = piece(1, j)
        xv = tok[m, here, :].astype(F32)
        d1 = snd[m, here, :].astype(F32) + rc1[m, here, :].astype(F32) + rc2[m, rr, :].astype(F32)
        tv = lax.rsqrt(jnp.mean(xv * xv, -1, keepdims=True) + EPS)
        e1 = gains[0:1, :] * d1
        dot = jnp.mean(xv * e1, -1, keepdims=True)
        igb[m, here, :] = (dy[m, rr, :] + tv * e1 - xv * (tv * tv * tv * dot)).astype(BF)

    out_res, ig_res = Result(r["outv"], "out"), Result(igb, "ig")

    gz, gz_ix = r["gz"], [slot() for _ in range(NT)]
    gin, gpart = r["gin"], r["gpart"]
    gain_ix = [slot() for _ in group]

    def gain_z():
        for k in range(1, NT):
            send(gacc, gz.at[k], gz_ix[k], z_to(k))

    def gain_group():
        for k in range(1, NT):
            copy_to(gacc, gz.at[k], gz_ix[k], z_to(k)).wait_recv()
        tot = gacc[...]
        for k in range(1, NT):
            tot = tot + gz[k]
        gpart[...] = tot
        for n, off in enumerate(group):
            send(gpart, gin.at[n], gain_ix[n], dev_group(off))

    def gain_final():
        for n, off in enumerate(group):
            copy_to(gpart, gin.at[n], gain_ix[n], dev_group(off)).wait_recv()
        tot = gpart[...]
        for n in range(len(group)):
            tot = tot + gin[n]
        tot = lax.dot_general(
            tot, place.astype(F32), (((1,), (1,)), ((), ())), precision=lax.Precision.HIGHEST,
            preferred_element_type=F32)
        r["fin_gain"][0] = tot[0:1, :]
        r["fin_gain"][1] = tot[1:2, :]
        store(r["fin_gain"].at[0], r["out_ga"])
        store(r["fin_gain"].at[1], r["out_gf"])

    fed = [step[1:] for step in ORDER if step[0] == "FS"]
    acts = {
        "prep": prepare, "qR": qkv_ready, "wF": weights_ready, "P": project, "wS": spread,
        "wX": lambda w: spreads[w].relay_x(), "wY": lambda w: spreads[w].relay_y(), "AT": attend_tile,
        "O": wait_o, "F1": feed, "FS": feed_slot, "FP": feed_out, "G": lambda k: reduce_step(k, "pair"), "SQ": lambda k: reduce_step(k, "square"),
        "SF": lambda k: reduce_step(k, "finish"), "SZ": last_sum, "BN": back_norm, "BS": back_start,
        "PE": back_peer, "OW": back_own, "J": join, "X": cross_over,
        "ON": lambda m, j: out_res.near(m, j, make_output), "OF": out_res.far,
        "IN": lambda m, j: ig_res.near(m, j, make_input_grad), "IF": ig_res.far,
        "GZ": gain_z, "GR": gain_group, "GF": gain_final,
    }
    for step in ORDER:
        acts[step[0]](*step[1:])
    for cp in stores:
        cp.wait()
    for cp in sends:
        cp.wait_send()
    for m in range(MICRO):
        close_o(m)
        for j in range(SUB):
            out_res.close(m, j)
            ig_res.close(m, j)

            def inner_done(m=m, j=j):
                if m == MICRO - 1:
                    for cp in do_copies(m, j):
                        cp.wait_send()
                swap(m, j).wait_send()

            def outer_done(m=m, j=j):
                to_mate(d2s, d2r, d2_ix, m, j).wait_send()
                to_mate(fps, fpr, fp_ix, m, j).wait_send()
                inward(m, 0, j).wait_send()
                inward(m, 1, j).wait_send()

            both(inner_done, outer_done)

    @pl.when(inner)
    def _():
        for cp in zo_copies():
            cp.wait_send()

    assert counter[0] <= ssem.shape[0]


def fused_shards(dims, tokens, segments, cotangent, query_weight, key_weight, value_weight, out_weight,
                 gate_weight, up_weight, down_weight, attn_gain, ffn_gain):
    R, D, H, FF, C, NF, NT, MICRO = dims
    L = C * R
    SR = D // (NF * C)
    NH = H // HEAD_DIM
    HP, KV, Y = 256, 2 * H, NF // 2
    HALF = Y * C * SR
    NO = Y * C - 1
    NG = NF * C - 1
    W = HP + KV
    ins = [
        ("tok_in", tokens.reshape(MICRO, R, D)),
        ("segr", segments),
        ("cot_in", cotangent.reshape(MICRO, R, D)),
        ("wq_in", query_weight),
        ("wk_in", key_weight),
        ("wv_in", value_weight),
        ("wo_in", out_weight),
        ("wg_in", gate_weight),
        ("wu_in", up_weight),
        ("wd_in", down_weight),
        ("gain_a_in", attn_gain[None]),
        ("gain_f_in", ffn_gain[None]),
    ]
    outs = [
        ("out", (MICRO, 1, R, D), BF),
        ("ig", (MICRO, 1, R, D), BF),
        ("out_q", (SR, H), F32),
        ("out_k", (SR, H), F32),
        ("out_v", (SR, H), F32),
        ("out_o", (SR, H), F32),
        ("out_g", (SR, FF), F32),
        ("out_u", (SR, FF), F32),
        ("out_d", (SR, FF), F32),
        ("out_ga", (1, SR), F32),
        ("out_gf", (1, SR), F32),
    ]
    v = pltpu.VMEM
    HR = R // 2
    scratch = [
        ("tok", v((MICRO, R, D), BF)), ("cot", v((MICRO * HR, D), BF)), ("dy", v((MICRO, HR, D), F32)),
        ("outv", v((MICRO, R, D), BF)), ("igb", v((MICRO, R, D), BF)),
        ("gz", v((NT, 2, D), F32)), ("gpart", v((2, D), F32)),
        ("lsem", pltpu.SemaphoreType.DMA((48,))),
        ("gmine", v((2, D), F32)), ("gall", v((NG, 2, D), F32)), ("gains", v((2, D), F32)),
        ("gacc", v((2, D), F32)), ("gin", v((NG, 2, D), F32)),
        ("wqkv", v((D, W), BF)), ("wo", v((D, D), BF)), ("woz", v((NT, SR, HP), BF)),
        ("wg", v((2, D, FF), BF)), ("wu", v((2, D, FF), BF)), ("wd", v((2, D, FF), BF)),
        ("segc", v((MICRO, L, 128), jnp.int32)),
        ("n1", v((MICRO * R, D), BF)), ("q", v((MICRO, R, HP), BF)),
        ("kv", v((MICRO, L, KV), BF)), ("kvT", v((MICRO, KV, L), BF)),
        ("oT", v((MICRO, HP, R), BF)), ("oX", v((MICRO, D, HR), BF)), ("onat", v((MICRO * HR, D), BF)),
        ("lse", v((MICRO, NH, 1, R), F32)),
        ("d2s", v((MICRO, HR, D), BF)), ("d2r", v((MICRO, HR, D), BF)),
        ("fps", v((MICRO, HR, D), BF)), ("fpr", v((MICRO, HR, D), BF)),
        ("snd", v((MICRO, R, D), BF)), ("rc1", v((MICRO, R, D), BF)), ("rc2", v((MICRO, HR, D), BF)),
        ("y1", v((MICRO, HR, D), F32)), ("n2", v((MICRO * HR, D), BF)), ("ar", v((MICRO * HR, D), BF)),
        ("big", v((3, 2, R, FF), BF)),
        ("doT", v((MICRO, HP, R), BF)), ("doS", v((D, HR), BF)),
        ("delta", v((NH, 1, R), F32)), ("dqT", v((H, R), F32)), ("dqkv", v((MICRO * R, W), BF)),
        ("dkv_own", v((MICRO, R, KV), F32)), ("dkv_in", v((MICRO, R, KV), BF)),
        ("gain_a_own", v((1, SR), BF)), ("gain_f_own", v((1, SR), BF)), ("fin_gain", v((2, 1, SR), F32)),
        ("wq_own", v((SR, H), BF)), ("wk_own", v((SR, H), BF)), ("wv_own", v((SR, H), BF)), ("wo_own", v((SR, H), BF)),
        ("fin_g", v((SR, FF), F32)), ("fin_u", v((SR, FF), F32)), ("fin_d", v((SR, FF), F32)),
        ("fin_qkv", v((3, SR, H), F32)), ("fin_o", v((SR, H), F32)),
        ("tmp", v((256, 512), F32)), ("zo", v((2, SR, HP), BF)), ("zq", v((NT, SR, HP), BF)),
    ]
    for k, cols in (("q", W), ("o", D), ("g", 2 * FF), ("u", 2 * FF), ("d", 2 * FF)):
        scratch += [("own_" + k, v((HALF, cols), F32)), ("rv_" + k, v((HALF, cols), BF)),
                    ("st_" + k, v((HALF, cols), BF)), ("pt_" + k, v((NO, SR, cols), BF))]
    for k in "gud":
        scratch += [("zs_" + k, v((SR, FF), BF)), ("zr_" + k, v((SR, FF), BF))]
    nsem = 320
    scratch += [("ssem", pltpu.SemaphoreType.DMA((nsem,))), ("rsem", pltpu.SemaphoreType.DMA((nsem,)))]
    names = [n for n, _ in ins] + [n for n, _, _ in outs] + [n for n, _ in scratch]
    def spec(name):
        return pl.BlockSpec(memory_space=pltpu.VMEM if name == "segr" else pl.ANY)

    res = pl.pallas_call(
        functools.partial(layer_kernel, dims, names),
        out_shape=[jax.ShapeDtypeStruct(s, d) for _, s, d in outs],
        in_specs=[spec(n) for n, _ in ins],
        out_specs=[spec(n) for n, _, _ in outs],
        scratch_shapes=[s for _, s in scratch],
        compiler_params=pltpu.CompilerParams(
            collective_id=0, has_side_effects=True, vmem_limit_bytes=67043328),
    )(*[a for _, a in ins])
    res = settle(res)
    return tuple(res[:9]) + (res[9].reshape(SR), res[10].reshape(SR))


def settle(arrays):
    pieces = []
    for n, a in enumerate(arrays):
        if a.ndim == 4:
            pieces += [(n, (m, 0, pl.ds(k * 256, 256))) for m in range(a.shape[0]) for k in range(a.shape[2] // 256)]
        else:
            pieces.append((n, None))

    kinds = [F32] * len(arrays)
    kinds[0] = arrays[0].dtype
    wide = [n for n, a in enumerate(arrays) if a.dtype != kinds[n]]

    def kernel(*refs):
        k = len(arrays)
        src, dst, buf, sem = refs[:k], refs[k:2 * k], refs[2 * k:3 * k], refs[3 * k:]
        last = list(buf)
        for i, n in enumerate(wide):
            last[n] = sem[2 + i]
        pick = lambda ref, at: ref if at is None else ref.at[at]
        come = [pltpu.make_async_copy(pick(src[n], at), pick(buf[n], at), sem[0].at[i]) for i, (n, at) in enumerate(pieces)]
        go = [pltpu.make_async_copy(pick(last[n], at), pick(dst[n], at), sem[1].at[i]) for i, (n, at) in enumerate(pieces)]
        for cp in come:
            cp.start()
        for a, b, (n, at) in zip(come, go, pieces):
            a.wait()
            if n in wide:
                last[n][at] = buf[n][at].astype(F32)
            b.start()
        for cp in go:
            cp.wait()

    hbm = pl.BlockSpec(memory_space=pl.ANY)
    return pl.pallas_call(
        kernel,
        out_shape=[jax.ShapeDtypeStruct(a.shape, d) for a, d in zip(arrays, kinds)],
        in_specs=[hbm] * len(arrays),
        out_specs=[hbm] * len(arrays),
        scratch_shapes=[pltpu.VMEM(a.shape, a.dtype) for a in arrays] + [pltpu.SemaphoreType.DMA((len(pieces),))] * 2
        + [pltpu.VMEM(arrays[n].shape, F32) for n in wide],
    )(*arrays)


def fits(dims, seqs):
    R, D, H, FF, C, NF, NT, MICRO = dims
    blocks = D % (16 * NF * C) == 0 and D % 256 == 0
    return (C, NT, NF, H, MICRO, seqs, R, FF) == (2, 4, 4, 192, 2, 1, 512, 512) and D <= 768 and blocks


SPECS = (
    P(None, "fsdp", "ctx", None),
    P(None, "fsdp", None),
    P(None, "fsdp", "ctx", None),
) + (P(("fsdp", "ctx"), "tp"),) * 7 + (P(("fsdp", "ctx")),) * 2
OUT_SPECS = (P(None, "fsdp", "ctx", None),) * 2 + (P(("fsdp", "ctx"), "tp"),) * 7 + (P(("fsdp", "ctx")),) * 2


def solution(mesh):
    nf, nc, nt = mesh.shape["fsdp"], mesh.shape["ctx"], mesh.shape["tp"]

    def chosen(*args):
        tokens, weight, ffw = args[0], args[3], args[7]
        micro, seqs, rows, width = tokens.shape
        dims = (rows, width, weight.shape[1], ffw.shape[1], nc, nf, nt, micro)
        return fused_shards(dims, *args) if fits(dims, seqs) else shards(*args)

    return jax.shard_map(chosen, mesh=mesh, in_specs=SPECS, out_specs=OUT_SPECS, check_vma=False)
```
